32 devices in a mesh: ctx: 4 (over y, x), fsdp: 8 (over z, core).
Axes of the slice: x: 2, y: 2, z: 4, core: 2. Of those that a mesh axis runs over, the one named last changes fastest.
Arguments:
- block_in: bfloat16 [8, 2048, 1024], P('fsdp', 'ctx'), may hold values from -6 to 6
- cotangent: bfloat16 [8, 2048, 1024], P('fsdp', 'ctx'), may hold values from -6 to 6
- doc_ids: int32 [8, 2048], P('fsdp', 'ctx'), may hold values from 0 to 1, never falling along the last dimension, each value on 1 to 1536 neighbouring positions
- block_ids: int32 [8, 2048], P('fsdp', 'ctx'), may hold values from 0 to 7, never falling along the last dimension, each value on 1 to 512 neighbouring positions
- gain_attn: bfloat16 [1024], P('fsdp'), may hold values from 0.099609375 to 1.8984375
- w_query: bfloat16 [1024, 1024], P('fsdp'), may hold values from -0.1875 to 0.1875
- w_key: bfloat16 [1024, 1024], P('fsdp'), may hold values from -0.1875 to 0.1875
- w_value: bfloat16 [1024, 1024], P('fsdp'), may hold values from -0.1875 to 0.1875
- w_out: bfloat16 [1024, 1024], P('fsdp'), may hold values from -2 to 2
- gain_ffn: bfloat16 [1024], P('fsdp'), may hold values from 0.099609375 to 1.8984375
- w_gate: bfloat16 [1024, 4096], P('fsdp'), may hold values from -0.1875 to 0.1875
- w_up: bfloat16 [1024, 4096], P('fsdp'), may hold values from -0.1875 to 0.1875
- w_down: bfloat16 [4096, 1024], P('fsdp'), may hold values from -0.09375 to 0.09375
Outputs:
- block_out: bfloat16 [8, 2048, 1024], P('fsdp', 'ctx')
- input_grad: float32 [8, 2048, 1024], P('fsdp', 'ctx')
- grad_gain_attn: float32 [1024], P('fsdp')
- grad_query: float32 [1024, 1024], P('fsdp')
- grad_key: float32 [1024, 1024], P('fsdp')
- grad_value: float32 [1024, 1024], P('fsdp')
- grad_out: float32 [1024, 1024], P('fsdp')
- grad_gain_ffn: float32 [1024], P('fsdp')
- grad_gate: float32 [1024, 4096], P('fsdp')
- grad_up: float32 [1024, 4096], P('fsdp')
- grad_down: float32 [4096, 1024], P('fsdp')
The draws below stay inside these ranges and needn't reach their ends.
Inputs may be any that keep to these rules, and one draw needn't show every extreme that they name: doc_ids never fall along a sequence; each sequence holds two documents, each of 512 to 1536 tokens. block_ids never fall along a sequence; every block has 1 to 512 tokens, and in every sequence one block has exactly 512 tokens.
All inputs are finite; a program needn't handle non-finite values.
Results may differ from the reference program's by a relative error of at most 0.022.
Values may be sent and summed in bfloat16 or wider, within the bound.
No kernel may reach another device: no remote copies, remote signals or barrier semaphores. Data moves between devices by JAX's collectives and lax.ppermute only.
A program may use at most 192 MiB of HBM per device.

```python
import math
import jax
import jax.numpy as jnp
import numpy as np
from jax import lax

D = 1024
HEADS = 16
HEAD_DIM = 64
FF = 4096
BLOCK = 256
LEN = 2048
SEQS = 8


def steps_of(stream_key, extent, shards, low, high):
    level, own = 1.0, jax.random.fold_in(stream_key, 6)
    for dim, shards_of in shards:
        draws = jnp.exp(jax.random.uniform(jax.random.fold_in(own, dim), (shards_of,), jnp.float32, low / len(shards), high / len(shards)))
        level = level * jnp.repeat(draws, extent[dim] // shards_of).reshape([-1 if axis == dim else 1 for axis in range(len(extent))])
    return level


def length_profile(count, total, limit, slope):
    weights = [(1 << 20) // math.isqrt(grade ** slope) + 1 for grade in range(2, count + 1)]
    spare, given = total - limit - (count - 1), [1] * (count - 1)
    while spare > 0:
        candidates = [i for i in range(count - 1) if given[i] < limit]
        whole, left = sum([weights[i] for i in candidates]), spare
        for i in candidates:
            more = min(limit - given[i], max(1, left * weights[i] // whole), spare)
            given[i] = given[i] + more
            spare = spare - more
    return np.array([limit] + given)


def uneven_parts(rng, number_of, total, most, lean):
    if number_of == 2:
        one = jax.random.randint(rng, (), max(1, total - most), min(most, total - 1) + 1)
        return jnp.stack([one, total - one])
    lengths = jnp.asarray(length_profile(number_of, total, most, lean), jnp.int32)
    couples = (number_of - 1) // 2
    donor, receiver = lengths[1:1 + 2 * couples:2], lengths[2:2 + 2 * couples:2]
    slack = jnp.minimum(donor - 1, most - receiver)
    passed = jax.random.randint(jax.random.fold_in(rng, 1), (couples,), 0, 1 << 20) % (slack + 1)
    lengths = lengths.at[1:1 + 2 * couples:2].set(donor - passed).at[2:2 + 2 * couples:2].set(receiver + passed)
    return lengths[jax.random.permutation(jax.random.fold_in(rng, 2), number_of)]


def centred(stream_key, dims, width, limit, shards=(), held_as=jnp.bfloat16):
    factor_of = steps_of(stream_key, dims, shards, -0.22, 0.18) if shards else 1.0
    values = jax.random.normal(stream_key, dims, jnp.float32) * width * factor_of
    return jnp.minimum(jnp.maximum(values, -limit), limit).astype(held_as)


def setup_inputs(seed: int = 0) -> dict:
    splits = jax.random.split(jax.random.key(seed), 14)
    return {
        "block_in": centred(splits[0], (SEQS, LEN, D), 1.0, 6.0, ((0, 8), (1, 4))),
        "cotangent": centred(splits[1], (SEQS, LEN, D), 1.0, 6.0, ((0, 8), (1, 4))),
        "doc_ids": jax.vmap(lambda own: jnp.searchsorted(jnp.cumsum(uneven_parts(own, 2, LEN, LEN * 3 // 4, 0)), jnp.arange(LEN), side="right"))(jax.random.split(splits[2], SEQS)).reshape((SEQS, LEN)).astype(jnp.int32),
        "block_ids": jax.vmap(lambda own: jnp.searchsorted(jnp.cumsum(uneven_parts(own, LEN // BLOCK, LEN, 2 * BLOCK, 0)), jnp.arange(LEN), side="right"))(jax.random.split(splits[3], SEQS)).reshape((SEQS, LEN)).astype(jnp.int32),
        "gain_attn": jnp.clip(1.0 + 0.18 * jax.random.normal(splits[4], (D,), jnp.float32), 0.099609375, 1.8984375).astype(jnp.bfloat16),
        "w_query": centred(splits[5], (D, D), D ** -0.5, 0.1875, ((0, 8),)),
        "w_key": centred(splits[6], (D, D), D ** -0.5, 0.1875, ((0, 8),)),
        "w_value": centred(splits[7], (D, D), D ** -0.5, 0.1875, ((0, 8),)),
        "w_out": centred(splits[8], (D, D), (D * 16 // LEN) ** -0.5, 2.0, ((0, 8),)),
        "gain_ffn": jnp.clip(1.0 + 0.18 * jax.random.normal(splits[9], (D,), jnp.float32), 0.099609375, 1.8984375).astype(jnp.bfloat16),
        "w_gate": centred(splits[10], (D, FF), D ** -0.5, 0.1875, ((0, 8),)),
        "w_up": centred(splits[11], (D, FF), D ** -0.5, 0.1875, ((0, 8),)),
        "w_down": centred(splits[12], (FF, D), FF ** -0.5, 0.09375, ((0, 8),)),
    }


@jax.custom_vjp
def low(v):
    return lax.optimization_barrier(v.astype(jnp.bfloat16)).astype(jnp.float32)

@jax.custom_vjp
def low_back(v):
    return v

def low_keep(v):
    return (low(v), None)

def low_pass(kept, grad):
    return (grad,)

def back_keep(v):
    return (v, None)

def back_low(kept, grad):
    return (low(grad),)
low.defvjp(low_keep, low_pass)
low_back.defvjp(back_keep, back_low)
NORM_EPS = 1e-05
MASKED = -1e+30

def matmul(left, right):
    return jnp.dot(left, right, precision=lax.Precision.HIGHEST, preferred_element_type=jnp.float32)

def block_forward(x, gain_attn, w_query, w_key, w_value, w_out, gain_ffn, w_gate, w_up, w_down, docs, blocks):
    scale = HEAD_DIM ** (-0.5)
    inv1 = lax.rsqrt(lax.optimization_barrier(jnp.mean(x * x, axis=-1, keepdims=True)) + NORM_EPS)
    a_one = low(x * inv1 * gain_attn)
    query = low(low_back(matmul(a_one, w_query)))
    keys = low(low_back(matmul(a_one, w_key)))
    values = low(low_back(matmul(a_one, w_value)))
    key_heads = keys.reshape(LEN, HEADS, HEAD_DIM)
    value_heads = values.reshape(LEN, HEADS, HEAD_DIM)
    rows_block = min(512, LEN)
    count = LEN // rows_block

    def attend(items):
        q_rows, q_doc, q_blk = items
        q_heads = q_rows.reshape(rows_block, HEADS, HEAD_DIM)
        scores = jnp.einsum('qhd,khd->hqk', q_heads, key_heads, precision=lax.Precision.HIGHEST) * scale
        scores = low_back(scores)
        allowed = (q_doc[:, None] == docs[None, :]) & (blocks[None, :] <= q_blk[:, None])
        scores = jnp.where(allowed[None], scores, MASKED)
        probs = low(jax.nn.softmax(scores, axis=-1))
        mixed = jnp.einsum('hqk,khd->qhd', probs, value_heads, precision=lax.Precision.HIGHEST)
        return mixed.reshape(rows_block, D)
    attended = lax.map(jax.checkpoint(attend), (query.reshape(count, rows_block, D), docs.reshape(count, rows_block), blocks.reshape(count, rows_block)))
    attended = low(low_back(attended.reshape(LEN, D)))
    hidden = x + low_back(matmul(attended, w_out))
    inv2 = lax.rsqrt(lax.optimization_barrier(jnp.mean(hidden * hidden, axis=-1, keepdims=True)) + NORM_EPS)
    a_two = low(hidden * inv2 * gain_ffn)
    gate = low_back(matmul(a_two, w_gate))
    upper = low_back(matmul(a_two, w_up))
    inner = low(jax.nn.silu(gate) * upper)
    return hidden + low_back(matmul(inner, w_down))

def reference(block_in, cotangent, doc_ids, block_ids, gain_attn, w_query, w_key, w_value, w_out, gain_ffn, w_gate, w_up, w_down):
    params = tuple((p.astype(jnp.float32) for p in (gain_attn, w_query, w_key, w_value, w_out, gain_ffn, w_gate, w_up, w_down)))

    def one_sequence(totals, items):
        x_seq, c_seq, d_seq, b_seq = items

        def forward(x_val, *weights):
            return block_forward(x_val, *weights, d_seq, b_seq)
        out_seq, pull = jax.vjp(forward, x_seq.astype(jnp.float32), *params)
        grads = pull(c_seq.astype(jnp.float32))
        totals = tuple((t + g for t, g in zip(totals, grads[1:])))
        return (totals, (out_seq.astype(jnp.bfloat16), grads[0]))
    start = tuple((jnp.zeros_like(p) for p in params))
    totals, (outs, dxs) = lax.scan(one_sequence, start, (block_in, cotangent, doc_ids, block_ids))
    return (outs, dxs, totals[0], totals[1], totals[2], totals[3], totals[4], totals[5], totals[6], totals[7], totals[8])
```

```python
import functools

import jax
import jax.numpy as jnp
from jax import lax
from jax.experimental import pallas as pl
from jax.experimental.pallas import tpu as pltpu
from jax.sharding import Mesh
from jax.sharding import PartitionSpec as P

HEAD_DIM = 64
NORM_EPS = 1e-05
MASKED = -1e30
START_MAX = -1e29
SCALE = HEAD_DIM ** (-0.5)
BQ = 256
BK = 256
F32 = jnp.float32
BF16 = jnp.bfloat16
NT = (((1,), (1,)), ((), ()))
TN = (((0,), (0,)), ((), ()))


def mm(a, b):
    return jnp.dot(a, b, preferred_element_type=F32)


def mm_nt(a, b):
    return lax.dot_general(a, b, NT, preferred_element_type=F32)


def mm_tn(a, b):
    return lax.dot_general(a, b, TN, preferred_element_type=F32)


def head_stack(rows, heads):
    lane = lax.broadcasted_iota(jnp.int32, rows.shape, 1) // HEAD_DIM
    return jnp.concatenate(
        [jnp.where(lane == h, rows, jnp.zeros_like(rows)) for h in range(heads)], axis=0
    )


def tile_place(tile, per_piece, chip):
    return ((tile // per_piece) ^ chip) * per_piece + tile % per_piece


def allowed_tile(doc_col, blk_col, doc_row, blk_row, k_at, q_at, heads):
    kd, kb = doc_col[pl.ds(k_at, BK), :], blk_col[pl.ds(k_at, BK), :]
    qd, qb = doc_row[:, pl.ds(q_at, BQ)], blk_row[:, pl.ds(q_at, BQ)]
    ok = (kd == qd) & (kb <= qb)
    return jnp.concatenate([ok] * heads, axis=1)


def attend_kernel(heads, piece, info, qkv, doc_col, blk_col, doc_row, blk_row, out, lse, v_t):
    width = heads * HEAD_DIM
    step = pl.program_id(0)
    chip = info[0]
    tiles = qkv.shape[0] // BQ

    @pl.when(step == 0)
    def _():
        v_t[...] = qkv[:, 2 * width : 3 * width].T

    at = tile_place(step, piece // BQ, chip)
    q_at = pl.multiple_of(at * BQ, BQ)
    q_rows = qkv[pl.ds(pl.multiple_of(step * BQ, BQ), BQ), 0:width] * jnp.asarray(SCALE, BF16)
    q_heads = head_stack(q_rows, heads)

    def one(j, carry):
        run_max, run_sum, accs = carry
        k_at = pl.multiple_of(j * BK, BK)
        pos = pl.multiple_of(tile_place(j, piece // BK, chip) * BK, BK)
        keys = qkv[pl.ds(pos, BK), width : 2 * width]
        scores = mm_nt(keys, q_heads)
        ok = allowed_tile(doc_col, blk_col, doc_row, blk_row, k_at, q_at, heads)
        scores = jnp.where(ok, scores, MASKED)
        new_max = jnp.maximum(run_max, jnp.max(scores, axis=0, keepdims=True))
        weights = jnp.exp(scores - new_max)
        factor = jnp.exp(run_max - new_max)
        new_sum = run_sum * factor + jnp.sum(weights, axis=0, keepdims=True)
        weights = weights.astype(BF16)
        new_accs = []
        for h in range(heads):
            v_head = v_t[h * HEAD_DIM : (h + 1) * HEAD_DIM, pl.ds(pos, BK)]
            part = slice(h * BQ, (h + 1) * BQ)
            new_accs.append(accs[h] * factor[:, part] + mm(v_head, weights[:, part]))
        return new_max, new_sum, tuple(new_accs)

    start = (
        jnp.full((1, heads * BQ), START_MAX, F32),
        jnp.zeros((1, heads * BQ), F32),
        tuple(jnp.zeros((HEAD_DIM, BQ), F32) for _ in range(heads)),
    )
    run_max, run_sum, accs = lax.fori_loop(info[1 + at], info[1 + tiles + at], one, start)
    outs = [accs[h] / run_sum[:, h * BQ : (h + 1) * BQ] for h in range(heads)]
    out[...] = jnp.concatenate(outs, axis=0).T.astype(BF16)
    logs = run_max + jnp.log(run_sum)
    for h in range(heads):
        lse[h : h + 1, :] = logs[:, h * BQ : (h + 1) * BQ]


def attend_back_kernel(
    heads, piece, info, qkv, mixed, d_mixed, lse, doc_col, blk_col, doc_row, blk_row, out, k_t, dk, dv
):
    width = heads * HEAD_DIM
    step = pl.program_id(0)
    chip = info[0]
    tiles = qkv.shape[0] // BQ

    @pl.when(step == 0)
    def _():
        k_t[...] = qkv[:, width : 2 * width].T
        dk[...] = jnp.zeros_like(dk)
        dv[...] = jnp.zeros_like(dv)

    at = tile_place(step, piece // BQ, chip)
    q_at = pl.multiple_of(at * BQ, BQ)
    rows = pl.ds(pl.multiple_of(step * BQ, BQ), BQ)
    q_heads = head_stack(qkv[rows, 0:width] * jnp.asarray(SCALE, BF16), heads)
    do_rows = d_mixed[...]
    do_heads = head_stack(do_rows, heads)
    prod = (do_rows.astype(F32) * mixed[...].astype(F32)).T
    delta = jnp.concatenate(
        [
            jnp.sum(prod[h * HEAD_DIM : (h + 1) * HEAD_DIM], axis=0, keepdims=True)
            for h in range(heads)
        ],
        axis=1,
    )
    logs = jnp.concatenate([lse[h : h + 1, :] for h in range(heads)], axis=1)

    def one(j, dqs):
        k_at = pl.multiple_of(j * BK, BK)
        pos = pl.multiple_of(tile_place(j, piece // BK, chip) * BK, BK)
        keys = qkv[pl.ds(pos, BK), width : 2 * width]
        values = qkv[pl.ds(pos, BK), 2 * width : 3 * width]
        scores = mm_nt(keys, q_heads)
        ok = allowed_tile(doc_col, blk_col, doc_row, blk_row, k_at, q_at, heads)
        probs = jnp.where(ok, jnp.exp(scores - logs), 0.0)
        d_probs = mm_nt(values, do_heads)
        d_scores = (probs * (d_probs - delta)).astype(BF16)
        dv[pl.ds(pos, BK), :] += mm(probs.astype(BF16), do_heads)
        dk[pl.ds(pos, BK), :] += mm(d_scores, q_heads)
        new = []
        for h in range(heads):
            k_head = k_t[h * HEAD_DIM : (h + 1) * HEAD_DIM, pl.ds(pos, BK)]
            new.append(dqs[h] + mm(k_head, d_scores[:, h * BQ : (h + 1) * BQ]))
        return tuple(new)

    dqs = lax.fori_loop(
        info[1 + at],
        info[1 + tiles + at],
        one,
        tuple(jnp.zeros((HEAD_DIM, BQ), F32) for _ in range(heads)),
    )
    out[rows, 0:width] = (jnp.concatenate(dqs, axis=0) * SCALE).T.astype(BF16)

    @pl.when(step == tiles - 1)
    def _():
        out[:, width : 2 * width] = dk[...].astype(BF16)
        out[:, 2 * width : 3 * width] = dv[...].astype(BF16)


def whole_spec(shape):
    return pl.BlockSpec(shape, lambda *_: (0,) * len(shape))


def attend(qkv, ids, piece):
    info, doc_col, blk_col, doc_row, blk_row = ids
    rows, width3 = qkv.shape
    width = width3 // 3
    heads = width // HEAD_DIM
    grid_spec = pltpu.PrefetchScalarGridSpec(
        num_scalar_prefetch=1,
        grid=(rows // BQ,),
        in_specs=[
            whole_spec((rows, width3)),
            whole_spec((rows, 1)),
            whole_spec((rows, 1)),
            whole_spec((1, rows)),
            whole_spec((1, rows)),
        ],
        out_specs=[
            pl.BlockSpec((BQ, width), lambda i, *_: (i, 0)),
            pl.BlockSpec((heads, BQ), lambda i, *_: (0, i)),
        ],
        scratch_shapes=[pltpu.VMEM((width, rows), BF16)],
    )
    return pl.pallas_call(
        functools.partial(attend_kernel, heads, piece),
        out_shape=[
            jax.ShapeDtypeStruct((rows, width), BF16),
            jax.ShapeDtypeStruct((heads, rows), F32),
        ],
        grid_spec=grid_spec,
        cost_estimate=pl.CostEstimate(
            flops=8 * rows * rows * width, bytes_accessed=16 * rows * width, transcendentals=rows * rows
        ),
        name="attend",
    )(info, qkv, doc_col, blk_col, doc_row, blk_row)


def attend_back(qkv, mixed, d_mixed, lse, ids, piece):
    info, doc_col, blk_col, doc_row, blk_row = ids
    rows, width3 = qkv.shape
    width = width3 // 3
    heads = width // HEAD_DIM
    grid_spec = pltpu.PrefetchScalarGridSpec(
        num_scalar_prefetch=1,
        grid=(rows // BQ,),
        in_specs=[
            whole_spec((rows, width3)),
            pl.BlockSpec((BQ, width), lambda i, *_: (i, 0)),
            pl.BlockSpec((BQ, width), lambda i, *_: (i, 0)),
            pl.BlockSpec((heads, BQ), lambda i, *_: (0, i)),
            whole_spec((rows, 1)),
            whole_spec((rows, 1)),
            whole_spec((1, rows)),
            whole_spec((1, rows)),
        ],
        out_specs=whole_spec((rows, width3)),
        scratch_shapes=[
            pltpu.VMEM((width, rows), BF16),
            pltpu.VMEM((rows, width), F32),
            pltpu.VMEM((rows, width), F32),
        ],
    )
    return pl.pallas_call(
        functools.partial(attend_back_kernel, heads, piece),
        out_shape=jax.ShapeDtypeStruct((rows, width3), BF16),
        grid_spec=grid_spec,
        cost_estimate=pl.CostEstimate(
            flops=20 * rows * rows * width, bytes_accessed=16 * rows * width, transcendentals=rows * rows
        ),
        name="attend_back",
    )(info, qkv, mixed, d_mixed, lse, doc_col, blk_col, doc_row, blk_row)


def send(value, step):
    count = lax.axis_size("ctx")
    return lax.ppermute(value, "ctx", [(i, i ^ step) for i in range(count)])


def swap(value):
    return lax.ppermute(value, "core", [(0, 1), (1, 0)])


def plane_gather(own):
    count = lax.axis_size("ctx")
    mine = [own] + [send(own, r) for r in range(1, count)]
    return mine, [swap(block) for block in mine]


def plane_sum(mine, other):
    count = lax.axis_size("ctx")
    total = None
    for r in list(range(1, count)) + [0]:
        part = mine[r].astype(F32) + swap(other[r]).astype(F32)
        if r:
            part = send(part.astype(BF16), r).astype(F32)
        total = part if total is None else total + part
    return total


def ordered(first, second, core):
    return jnp.where(core == 0, jnp.stack([first, second]), jnp.stack([second, first]))


def mask_ids(docs, blocks, chip):
    rows = docs.shape[0]
    first_doc = docs[0::BQ][:, None]
    last_doc, last_block = docs[BQ - 1 :: BQ][:, None], blocks[BQ - 1 :: BQ][:, None]
    low = jnp.sum((docs[None] < first_doc).astype(jnp.int32), axis=1) // BK
    ends = jnp.minimum(
        jnp.sum((docs[None] <= last_doc).astype(jnp.int32), axis=1),
        jnp.sum((blocks[None] <= last_block).astype(jnp.int32), axis=1),
    )
    high = (ends + BK - 1) // BK
    info = jnp.concatenate([chip[None].astype(jnp.int32), low, high])
    return (info, docs.reshape(rows, 1), blocks.reshape(rows, 1), docs.reshape(1, rows), blocks.reshape(1, rows))


def body(
    block_in, cotangent, doc_ids, block_ids, gain_attn, w_query, w_key, w_value, w_out, gain_ffn, w_gate, w_up, w_down
):
    n_ctx, n_z = lax.axis_size("ctx"), lax.axis_size("z")
    chip, core = lax.axis_index("ctx"), lax.axis_index("core")
    piece, dim = block_in.shape[1], block_in.shape[2]
    shard = w_query.shape[0]
    width = dim // (2 * n_ctx)
    down_rows = w_down.shape[0]
    cut = down_rows // n_ctx
    hidden_cols = n_z * cut

    all_ids = lax.all_gather(jnp.stack([doc_ids[0], block_ids[0]]), ("ctx", "core"))
    all_ids = all_ids.reshape(n_ctx, 2, 2, piece)

    def ids_of(which):
        seq = lax.dynamic_index_in_dim(all_ids, which, axis=1, keepdims=False)
        return mask_ids(seq[:, 0].reshape(-1), seq[:, 1].reshape(-1), chip)

    def head_cols(which):
        at = (chip * 2 + which) * width
        return jnp.concatenate(
            [lax.dynamic_slice_in_dim(w, at, width, axis=1) for w in (w_query, w_key, w_value)], axis=1
        )

    def hidden_slices(which):
        return jnp.concatenate(
            [
                lax.dynamic_slice_in_dim(w, (2 * z + which) * down_rows + chip * cut, cut, axis=1)
                for w in (w_gate, w_up)
                for z in range(n_z)
            ],
            axis=1,
        )

    def scaled(w, gain):
        return (w.astype(F32) * gain.astype(F32)[:, None]).astype(BF16)

    def over_z(mine, theirs):
        both = ordered(mine, swap(theirs), core).reshape(2 * shard, -1)
        return lax.all_gather(both, "z", axis=0, tiled=True)

    w_qkv = over_z(scaled(head_cols(core), gain_attn), scaled(head_cols(1 - core), gain_attn))
    w_out_full = lax.all_gather(w_out, ("z", "core"), axis=0, tiled=True)
    w_gu = over_z(scaled(hidden_slices(core), gain_ffn), scaled(hidden_slices(1 - core), gain_ffn))
    w_dn = lax.all_gather(
        lax.dynamic_slice_in_dim(w_down, chip * cut, cut, axis=0), "z", axis=0, tiled=True
    )

    x_rows = block_in[0].astype(F32)
    inv1 = lax.rsqrt(jnp.mean(x_rows * x_rows, axis=-1, keepdims=True) + NORM_EPS)
    n_one = x_rows * inv1
    one_mine, one_other = plane_gather(n_one.astype(BF16))
    ids_mine, ids_other = ids_of(core), ids_of(1 - core)

    def project(blocks):
        return jnp.concatenate([mm(b, w_qkv).astype(BF16) for b in blocks], axis=0)

    qkv_mine, qkv_other = project(one_mine), project(one_other)
    mix_mine, lse_mine = attend(qkv_mine, ids_mine, piece)
    mix_other, lse_other = attend(qkv_other, ids_other, piece)
    mixes = jnp.stack([mix_mine, swap(mix_other)]).reshape(2, n_ctx, piece, width)
    parts = [mixes[:, 0]] + [send(mixes[:, r], r) for r in range(1, n_ctx)]
    attended = jnp.concatenate([p[q] for p in parts for q in range(2)], axis=1)

    def relative(rows):
        me = chip * 2 + core
        return jnp.concatenate(
            [lax.dynamic_slice_in_dim(rows, (j ^ me) * width, width, axis=0) for j in range(2 * n_ctx)],
            axis=0,
        )

    w_out_rel = relative(w_out_full)
    hidden = x_rows + mm(attended, w_out_rel)
    inv2 = lax.rsqrt(jnp.mean(hidden * hidden, axis=-1, keepdims=True) + NORM_EPS)
    n_two = hidden * inv2

    cot_mine, cot_other = plane_gather(cotangent[0])
    two_mine, two_other = plane_gather(n_two.astype(BF16))

    def feed(rows, cots):
        gu = mm(rows, w_gu)
        gate, upper = gu[:, :hidden_cols], gu[:, hidden_cols:]
        sigma = jax.nn.sigmoid(gate)
        silu_gate = gate * sigma
        inner = (silu_gate * upper).astype(BF16)
        d_inner = mm_nt(cots, w_dn)
        d_gate = d_inner * upper * sigma * (1.0 + gate * (1.0 - sigma))
        d_gu = jnp.concatenate([d_gate, d_inner * silu_gate], axis=1).astype(BF16)
        return inner, d_gu, mm_nt(d_gu, w_gu).astype(BF16)

    fed_mine = [feed(a, c) for a, c in zip(two_mine, cot_mine)]
    fed_other = [feed(a, c) for a, c in zip(two_other, cot_other)]
    d_norm2 = plane_sum([f[2] for f in fed_mine], [f[2] for f in fed_other])
    out_rows = plane_sum(
        [mm(f[0], w_dn).astype(BF16) for f in fed_mine], [mm(f[0], w_dn).astype(BF16) for f in fed_other]
    )
    block_out = (hidden + out_rows).astype(BF16)
    two_all = jnp.concatenate(two_mine + two_other, axis=0)
    cot_all = jnp.concatenate(cot_mine + cot_other, axis=0)
    inner_all = jnp.concatenate([f[0] for f in fed_mine + fed_other], axis=0)
    d_gu_all = jnp.concatenate([f[1] for f in fed_mine + fed_other], axis=0)
    grad_dn = mm_tn(inner_all, cot_all).astype(BF16)
    grad_gu = mm_tn(two_all, d_gu_all).astype(BF16)
    grad_dn = lax.psum_scatter(grad_dn, "z", scatter_dimension=0, tiled=True)
    grad_gu = lax.psum_scatter(grad_gu, "z", scatter_dimension=0, tiled=True)

    d_hidden = cotangent[0].astype(F32) + inv2 * (
        d_norm2 - n_two * jnp.mean(d_norm2 * n_two, axis=-1, keepdims=True)
    )
    e_rows = d_hidden.astype(BF16)
    d_att = mm_nt(e_rows, w_out_rel).astype(BF16)
    grad_wo = lax.psum_scatter(
        relative(mm_tn(attended, e_rows).astype(BF16)), ("z", "core"), scatter_dimension=0, tiled=True
    )
    grad_wo = lax.psum(grad_wo, "ctx").astype(F32)

    d_parts = [d_att[:, : 2 * width]] + [
        send(d_att[:, 2 * width * r : 2 * width * (r + 1)], r) for r in range(1, n_ctx)
    ]
    d_mix_mine = jnp.concatenate([p[:, :width] for p in d_parts], axis=0)
    d_mix_other = swap(jnp.concatenate([p[:, width:] for p in d_parts], axis=0))
    d_qkv_mine = attend_back(qkv_mine, mix_mine, d_mix_mine, lse_mine, ids_mine, piece)
    d_qkv_other = attend_back(qkv_other, mix_other, d_mix_other, lse_other, ids_other, piece)

    def by_piece(rows):
        return [rows[r * piece : (r + 1) * piece] for r in range(n_ctx)]

    d_norm1 = plane_sum(
        [mm_nt(b, w_qkv).astype(BF16) for b in by_piece(d_qkv_mine)],
        [mm_nt(b, w_qkv).astype(BF16) for b in by_piece(d_qkv_other)],
    )
    input_grad = d_hidden + inv1 * (d_norm1 - n_one * jnp.mean(d_norm1 * n_one, axis=-1, keepdims=True))
    one_all = jnp.concatenate(one_mine + one_other, axis=0)
    grad_qkv = mm_tn(one_all, jnp.concatenate([d_qkv_mine, d_qkv_other], axis=0)).astype(BF16)
    grad_qkv = lax.psum_scatter(grad_qkv, "z", scatter_dimension=0, tiled=True)

    def to_owner(part):
        mine = lax.dynamic_slice_in_dim(part, core * shard, shard, axis=0)
        theirs = lax.dynamic_slice_in_dim(part, (1 - core) * shard, shard, axis=0)
        both = ordered(mine, swap(theirs), core)
        return lax.all_gather(both, "ctx", axis=0).transpose(2, 0, 1, 3)

    qkv_shard = to_owner(grad_qkv).reshape(shard, 2 * n_ctx, 3, width).astype(F32)
    raw_q, raw_k, raw_v = (qkv_shard[:, :, i].reshape(shard, dim) for i in range(3))
    gu_shard = to_owner(grad_gu).reshape(shard, n_ctx, 2, 2, n_z, cut).astype(F32)
    raw_g, raw_u = (
        gu_shard[:, :, :, i].transpose(0, 3, 2, 1, 4).reshape(shard, -1) for i in range(2)
    )
    grad_down = lax.all_gather(grad_dn, "ctx", axis=0, tiled=True).astype(F32)

    def row_sum(pairs):
        return sum(jnp.sum(w.astype(F32) * g, axis=1) for w, g in pairs)

    g1, g2 = gain_attn.astype(F32)[:, None], gain_ffn.astype(F32)[:, None]
    return (
        block_out[None],
        input_grad[None],
        row_sum([(w_query, raw_q), (w_key, raw_k), (w_value, raw_v)]),
        raw_q * g1,
        raw_k * g1,
        raw_v * g1,
        grad_wo,
        row_sum([(w_gate, raw_g), (w_up, raw_u)]),
        raw_g * g2,
        raw_u * g2,
        grad_down,
    )


def solution(mesh):
    n_ctx, n_fsdp = mesh.devices.shape
    inner = Mesh(mesh.devices.reshape(n_ctx, n_fsdp // 2, 2), ("ctx", "z", "core"))
    fsdp = ("z", "core")
    act, ids, vec, mat = P(fsdp, "ctx", None), P(fsdp, "ctx"), P(fsdp), P(fsdp, None)
    return jax.shard_map(
        body,
        mesh=inner,
        in_specs=(act, act, ids, ids, vec, mat, mat, mat, mat, vec, mat, mat, mat),
        out_specs=(act, act, vec, mat, mat, mat, mat, vec, mat, mat, mat),
        check_vma=False,
    )
```

```python
import functools

import jax
import jax.numpy as jnp
from jax import lax
from jax.experimental import pallas as pl
from jax.experimental.pallas import tpu as pltpu
from jax.sharding import Mesh
from jax.sharding import PartitionSpec as P

HEAD_DIM = 64
NORM_EPS = 1e-05
MASKED = -1e30
START_MAX = -1e29
SCALE = HEAD_DIM ** (-0.5)
DOC = 1 << 16
F32 = jnp.float32
BF16 = jnp.bfloat16
NT = (((1,), (1,)), ((), ()))
TN = (((0,), (0,)), ((), ()))


def mm(a, b):
    return jnp.dot(a, b, preferred_element_type=F32)


def mm_nt(a, b):
    return lax.dot_general(a, b, NT, preferred_element_type=F32)


def mm_tn(a, b):
    return lax.dot_general(a, b, TN, preferred_element_type=F32)


def cost(us):
    return pl.CostEstimate(flops=int(us * 1e9), bytes_accessed=1000, transcendentals=0)


def whole_spec(shape, **kw):
    return pl.BlockSpec(shape, lambda *_: (0,) * len(shape), **kw)


def pick_spec(shape, index):
    return pl.BlockSpec((1,) + shape, lambda *_: (index,) + (0,) * len(shape))


def any_spec():
    return pl.BlockSpec(memory_space=pl.ANY)


def call(kernel, name, out_shape, in_specs, out_specs, grid=(1,), scratch=(), estimate=None, prefetch=1):
    return pl.pallas_call(
        kernel,
        out_shape=out_shape,
        grid_spec=pltpu.PrefetchScalarGridSpec(
            num_scalar_prefetch=prefetch,
            grid=grid,
            in_specs=in_specs,
            out_specs=out_specs,
            scratch_shapes=list(scratch),
        ),
        cost_estimate=estimate,
        name=name,
    )


def shape_of(*dims, dtype=BF16):
    return jax.ShapeDtypeStruct(dims, dtype)


def head_stack(rows, heads):
    lane = lax.broadcasted_iota(jnp.int32, rows.shape, 1) // HEAD_DIM
    return jnp.concatenate(
        [jnp.where(lane == h, rows, jnp.zeros_like(rows)) for h in range(heads)], axis=0
    )


def query_tile(step, n, info):
    r, dp = step % n, step // n
    return r, dp, r * 2 + (dp ^ info[1])


def key_tile(a, n, info):
    r = (a // 2) ^ info[0]
    return ((a % 2) ^ info[1]) * n + r, r * 2 + a % 2


def query_bounds(code_row, q_ids, half, heads):
    high = code_row[:, pl.ds(pl.multiple_of(q_ids * half, half), half)]
    low = (high // DOC) * DOC
    return jnp.concatenate([low] * heads, axis=1), jnp.concatenate([high] * heads, axis=1)


def key_pair(first, last, turn, n, info, half, code_col, bounds):
    low, high = bounds
    for i in range(2):
        a = first + 2 * turn + i
        place, k_ids = key_tile(jnp.minimum(a, last - 1), n, info)
        keys = code_col[pl.ds(pl.multiple_of(k_ids * half, half), half), 0:1]
        if i:
            keys = jnp.where(a < last, keys, -1)
        yield pl.multiple_of(place * half, half), (keys >= low) & (keys <= high)


def attend_kernel(n, heads, half, info, *refs):
    blocks, (w, code_row), (qkv, *outs, lse), (v_t, code_col) = (
        refs[: 2 * n],
        refs[2 * n : 2 * n + 2],
        refs[2 * n + 2 : 3 * n + 4],
        refs[3 * n + 4 :],
    )
    width = heads * HEAD_DIM
    step = pl.program_id(0)

    @pl.when(step == 0)
    def _():
        for k in range(2 * n):
            qkv[k * half : (k + 1) * half, :] = mm(blocks[k][0], w[...]).astype(BF16)
        v_t[...] = qkv[:, 2 * width : 3 * width].T
        code_col[...] = jnp.broadcast_to(code_row[...], (8, code_row.shape[1])).T

    r, dp, q_ids = query_tile(step, n, info)
    q_rows = qkv[pl.ds(pl.multiple_of(step * half, half), half), 0:width] * jnp.asarray(SCALE, BF16)
    q_heads = head_stack(q_rows, heads)

    first, last = info[2 + q_ids], info[2 + 2 * n + q_ids]
    bounds = query_bounds(code_row, q_ids, half, heads)

    def one(turn, carry):
        run_max, run_sum, accs = carry
        new_max, tiles = run_max, []
        for pos, keys_ok in key_pair(first, last, turn, n, info, half, code_col, bounds):
            scores = mm_nt(qkv[pl.ds(pos, half), width : 2 * width], q_heads)
            scores = jnp.where(keys_ok, scores, MASKED)
            new_max = jnp.maximum(new_max, jnp.max(scores, axis=0, keepdims=True))
            tiles.append((pos, scores))
        factor = jnp.exp(run_max - new_max)
        new_sum = run_sum * factor
        new_accs = [accs[h] * factor[:, h * half : (h + 1) * half] for h in range(heads)]
        for pos, scores in tiles:
            weights = jnp.exp(scores - new_max)
            new_sum += jnp.sum(weights, axis=0, keepdims=True)
            weights = weights.astype(BF16)
            for h in range(heads):
                v_head = v_t[h * HEAD_DIM : (h + 1) * HEAD_DIM, pl.ds(pos, half)]
                new_accs[h] += mm(v_head, weights[:, h * half : (h + 1) * half])
        return new_max, new_sum, tuple(new_accs)

    start = (
        jnp.full((1, heads * half), START_MAX, F32),
        jnp.zeros((1, heads * half), F32),
        tuple(jnp.zeros((HEAD_DIM, half), F32) for _ in range(heads)),
    )
    run_max, run_sum, accs = lax.fori_loop(0, (last - first + 1) // 2, one, start)
    parts = [accs[h] / run_sum[:, h * half : (h + 1) * half] for h in range(heads)]
    mixed = jnp.concatenate(parts, axis=0).T.astype(BF16)
    for k in range(n):

        @pl.when(r == k)
        def _():
            outs[k][dp] = mixed

    logs = run_max + jnp.log(run_sum)
    at = pl.ds(pl.multiple_of(step * half, half), half)
    for h in range(heads):
        lse[h : h + 1, at] = logs[:, h * half : (h + 1) * half]


def attend(blocks, which, w_qkv, ids, n):
    info, code_row = ids
    half, dim = blocks[0].shape[1:]
    width = dim // (2 * n)
    heads = width // HEAD_DIM
    rows = 2 * n * half
    return call(
        functools.partial(attend_kernel, n, heads, half),
        "attend",
        [shape_of(rows, 3 * width)]
        + [shape_of(2, half, width)] * n
        + [shape_of(heads, rows, dtype=F32)],
        [pick_spec((half, dim), which)] * (2 * n) + [whole_spec((dim, 3 * width)), whole_spec((1, rows))],
        [whole_spec((rows, 3 * width))] + [whole_spec((2, half, width))] * n + [whole_spec((heads, rows))],
        grid=(2 * n,),
        scratch=[pltpu.VMEM((width, rows), BF16), pltpu.VMEM((rows, 8), jnp.int32)],
        estimate=cost(21),
    )(info, *blocks, w_qkv, code_row)


def attend_back_kernel(n, heads, half, info, *refs):
    qkv, w, lse, code_row = refs[:4]
    mixes, d_mixes, (d_other,) = refs[4 : 4 + n], refs[4 + n : 4 + 2 * n], refs[4 + 2 * n : 5 + 2 * n]
    out, part_mine, part_other, k_t, dk, dv, code_col, do_now, mix_now = refs[5 + 2 * n :]
    width = heads * HEAD_DIM
    step = pl.program_id(0)

    @pl.when(step == 0)
    def _():
        k_t[...] = qkv[:, width : 2 * width].T
        code_col[...] = jnp.broadcast_to(code_row[...], (8, code_row.shape[1])).T
        dk[...] = jnp.zeros_like(dk)
        dv[...] = jnp.zeros_like(dv)

    r, dp, q_ids = query_tile(step, n, info)
    rows = pl.ds(pl.multiple_of(step * half, half), half)
    q_heads = head_stack(qkv[rows, 0:width] * jnp.asarray(SCALE, BF16), heads)
    for k in range(n):

        @pl.when(r == k)
        def _():
            mix_now[...] = mixes[k][dp]

        @pl.when((r == k) & (dp == 0))
        def _():
            do_now[...] = d_mixes[k][0]

    @pl.when(dp == 1)
    def _():
        do_now[...] = d_other[r]

    do_rows = do_now[...]
    do_heads = head_stack(do_rows, heads)
    prod = (do_rows.astype(F32) * mix_now[...].astype(F32)).T
    delta = jnp.concatenate(
        [
            jnp.sum(prod[h * HEAD_DIM : (h + 1) * HEAD_DIM], axis=0, keepdims=True)
            for h in range(heads)
        ],
        axis=1,
    )
    logs = jnp.concatenate([lse[h : h + 1, rows] for h in range(heads)], axis=1)

    first, last = info[2 + q_ids], info[2 + 2 * n + q_ids]
    bounds = query_bounds(code_row, q_ids, half, heads)

    def one(turn, dqs):
        new, done = list(dqs), []
        for pos, keys_ok in key_pair(first, last, turn, n, info, half, code_col, bounds):
            keys = qkv[pl.ds(pos, half), width : 2 * width]
            values = qkv[pl.ds(pos, half), 2 * width : 3 * width]
            scores = mm_nt(keys, q_heads)
            probs = jnp.where(keys_ok, jnp.exp(scores - logs), 0.0)
            d_probs = mm_nt(values, do_heads)
            d_scores = (probs * (d_probs - delta)).astype(BF16)
            done.append((pos, mm(probs.astype(BF16), do_heads), mm(d_scores, q_heads)))
            for h in range(heads):
                k_head = k_t[h * HEAD_DIM : (h + 1) * HEAD_DIM, pl.ds(pos, half)]
                new[h] += mm(k_head, d_scores[:, h * half : (h + 1) * half])
        for pos, d_values, d_keys in done:
            dv[pl.ds(pos, half), :] += d_values
            dk[pl.ds(pos, half), :] += d_keys
        return tuple(new)

    dqs = lax.fori_loop(
        0,
        (last - first + 1) // 2,
        one,
        tuple(jnp.zeros((HEAD_DIM, half), F32) for _ in range(heads)),
    )
    out[rows, 0:width] = (jnp.concatenate(dqs, axis=0) * SCALE).T.astype(BF16)

    @pl.when(step == 2 * n - 1)
    def _():
        out[:, width : 2 * width] = dk[...].astype(BF16)
        out[:, 2 * width : 3 * width] = dv[...].astype(BF16)
        for k in range(n):
            part_mine[k] = mm_nt(out[k * half : (k + 1) * half, :], w[...]).astype(BF16)
            part_other[k] = mm_nt(out[(n + k) * half : (n + k + 1) * half, :], w[...]).astype(BF16)


def attend_back(qkv, w_qkv, lse, mixes, d_mixes, d_other, ids, n):
    info, code_row = ids
    rows, width3 = qkv.shape
    width, dim = width3 // 3, w_qkv.shape[0]
    heads = width // HEAD_DIM
    half = rows // (2 * n)
    tile = (2, half, width)
    return call(
        functools.partial(attend_back_kernel, n, heads, half),
        "attend_back",
        [shape_of(rows, width3), shape_of(n, half, dim), shape_of(n, half, dim)],
        [whole_spec((rows, width3)), whole_spec((dim, width3)), whole_spec((heads, rows)), whole_spec((1, rows))]
        + [whole_spec(tile)] * (2 * n)
        + [whole_spec((n, half, width))],
        [whole_spec((rows, width3)), whole_spec((n, half, dim)), whole_spec((n, half, dim))],
        grid=(2 * n,),
        scratch=[
            pltpu.VMEM((width, rows), BF16),
            pltpu.VMEM((rows, width), F32),
            pltpu.VMEM((rows, width), F32),
            pltpu.VMEM((rows, 8), jnp.int32),
            pltpu.VMEM((half, width), BF16),
            pltpu.VMEM((half, width), BF16),
        ],
        estimate=cost(26),
    )(info, qkv, w_qkv, lse, code_row, *mixes, *d_mixes, d_other)


def normed(rows):
    inv = lax.rsqrt(jnp.mean(rows * rows, axis=-1, keepdims=True) + NORM_EPS)
    return rows * inv, inv


def back_normed(rows, d_norm):
    norm, inv = normed(rows)
    return inv * (d_norm - norm * jnp.mean(d_norm * norm, axis=-1, keepdims=True))


def head_rows(info, j, width):
    return pl.ds(pl.multiple_of((j ^ (info[0] * 2 + info[1])) * width, width), width)


def mix_kernel(n, width, info, *refs):
    parts, (others, x, w), (att, hidden, norm) = refs[:n], refs[n : n + 3], refs[n + 3 :]
    total = x[0].astype(F32)
    for r in range(n):
        for q in range(2):
            j = r * 2 + q
            part = others[r] if q else parts[r][0]
            att[:, j * width : (j + 1) * width] = part
            total += mm(part, w[head_rows(info, j, width), :])
    hidden[...] = total
    norm[...] = normed(total)[0].astype(BF16)


def mix(info, parts, others, x, which, w_out, n):
    half, width = parts[0].shape[1:]
    dim = w_out.shape[0]
    return call(
        functools.partial(mix_kernel, n, width),
        "mix",
        [shape_of(half, dim), shape_of(half, dim, dtype=F32), shape_of(half, dim)],
        [whole_spec((2, half, width))] * n
        + [whole_spec((n, half, width)), pick_spec((half, dim), which), whole_spec((dim, dim))],
        [whole_spec((half, dim))] * 3,
        estimate=cost(5),
    )(info, *parts, others, x, w_out)


def feed_kernel(n, half, cols, which, info, *refs):
    two, cots = refs[: 2 * n], refs[2 * n : 4 * n]
    inner_out, d_gu_out, d_mine, d_other, o_mine, o_other, a_buf, c_buf, w_gu, w_dn, sems = refs[-11:]
    w_ffs = refs[4 * n : -11]
    step = pl.program_id(0)
    slot = step % 2

    def copies(r, at):
        got = []
        for dp in range(2):
            rows = pl.ds(dp * half, half)
            got.append(pltpu.make_async_copy(two[dp * n + r], a_buf.at[at, rows], sems.at[at, dp]))
            got.append(pltpu.make_async_copy(cots[dp * n + r].at[which], c_buf.at[at, rows], sems.at[at, 2 + dp]))
        return got

    @pl.when(step == 0)
    def _():
        for c in copies(0, 0):
            c.start()
        if len(w_ffs) == 1:
            n_z = w_ffs[0].shape[0]
            gu_rows, dn_rows = w_gu.shape[0] // n_z, cols // n_z
            for z in range(n_z):
                w_gu[z * gu_rows : (z + 1) * gu_rows, :] = w_ffs[0][z, :gu_rows, :]
                w_dn[z * dn_rows : (z + 1) * dn_rows, :] = w_ffs[0][z, gu_rows:, :]
        else:
            w_gu[...], w_dn[...] = w_ffs[0][...], w_ffs[1][...]

    for r in range(1, n):

        @pl.when(step + 1 == r)
        def _():
            for c in copies(r, r % 2):
                c.start()

    for c in copies(0, slot):
        c.wait()
    rows, cot = a_buf[slot], c_buf[slot]
    gu = mm(rows, w_gu[...])
    d_inner = mm_nt(cot, w_dn[...])
    gate, upper = gu[:, :cols], gu[:, cols:]
    sigma = jax.nn.sigmoid(gate)
    silu_gate = gate * sigma
    inner = (silu_gate * upper).astype(BF16)
    d_gate = (d_inner * upper * sigma * (1.0 + gate * (1.0 - sigma))).astype(BF16)
    d_upper = (d_inner * silu_gate).astype(BF16)
    inner_out[...] = inner
    d_gu_out[:, :cols] = d_gate
    d_gu_out[:, cols:] = d_upper
    d_rows = (mm_nt(d_gate, w_gu[:, :cols]) + mm_nt(d_upper, w_gu[:, cols:])).astype(BF16)
    d_mine[0] = d_rows[:half]
    d_other[0] = d_rows[half:]
    o_rows = mm(inner, w_dn[...]).astype(BF16)
    o_mine[0] = o_rows[:half]
    o_other[0] = o_rows[half:]


def feed(two, cots, which, w_ffs, cols, info, n):
    half, dim = two[0].shape
    rows = 2 * n * half
    block = pl.BlockSpec((1, half, dim), lambda i, *_: (i, 0, 0))
    return call(
        functools.partial(feed_kernel, n, half, cols, which),
        "feed",
        [shape_of(rows, cols), shape_of(rows, 2 * cols)] + [shape_of(n, half, dim)] * 4,
        [any_spec()] * (4 * n) + [whole_spec(w.shape) for w in w_ffs],
        [
            pl.BlockSpec((2 * half, cols), lambda i, *_: (i, 0)),
            pl.BlockSpec((2 * half, 2 * cols), lambda i, *_: (i, 0)),
        ]
        + [block] * 4,
        grid=(n,),
        scratch=[
            pltpu.VMEM((2, 2 * half, dim), BF16),
            pltpu.VMEM((2, 2 * half, dim), BF16),
            pltpu.VMEM((dim, 2 * cols), BF16),
            pltpu.VMEM((cols, dim), BF16),
            pltpu.SemaphoreType.DMA((2, 4)),
        ],
        estimate=cost(20),
    )(info, *two, *cots, *w_ffs)


def feed_grads_kernel(n, n_z, half, info, *refs):
    two, cots = (refs[: 2 * n], refs[2 * n : 4 * n]), refs[4 * n : 6 * n]
    inners, d_gus = refs[6 * n : 6 * n + 2], refs[6 * n + 2 : 6 * n + 4]
    a_buf, c_buf, z_buf, g_buf, acc_gu, acc_dn, sems = refs[-7:]
    outs = refs[6 * n + 4 : -7]
    step = pl.program_id(0)
    slot = step % 2
    gu_rows, dn_rows = acc_gu.shape[0] // n_z, acc_dn.shape[0] // n_z

    def copies(t, at):
        s, r = t // n, t % n
        got = []
        for dp in range(2):
            rows = pl.ds(dp * half, half)
            got.append(pltpu.make_async_copy(two[s][dp * n + r], a_buf.at[at, rows], sems.at[at, dp]))
            got.append(pltpu.make_async_copy(cots[dp * n + r].at[s], c_buf.at[at, rows], sems.at[at, 2 + dp]))
        rows = pl.ds(2 * r * half, 2 * half)
        got.append(pltpu.make_async_copy(inners[s].at[rows], z_buf.at[at], sems.at[at, 4]))
        got.append(pltpu.make_async_copy(d_gus[s].at[rows], g_buf.at[at], sems.at[at, 5]))
        return got

    @pl.when(step == 0)
    def _():
        for c in copies(0, 0):
            c.start()
        acc_gu[...] = jnp.zeros_like(acc_gu)
        acc_dn[...] = jnp.zeros_like(acc_dn)

    for t in range(1, 2 * n):

        @pl.when(step + 1 == t)
        def _():
            for c in copies(t, t % 2):
                c.start()

    for c in copies(0, slot):
        c.wait()
    acc_gu[...] += mm_tn(a_buf[slot], g_buf[slot])
    acc_dn[...] += mm_tn(z_buf[slot], c_buf[slot])

    @pl.when(step == 2 * n - 1)
    def _():
        if len(outs) == 1:
            for z in range(n_z):
                outs[0][z, :gu_rows, :] = acc_gu[z * gu_rows : (z + 1) * gu_rows, :].astype(BF16)
                outs[0][z, gu_rows:, :] = acc_dn[z * dn_rows : (z + 1) * dn_rows, :].astype(BF16)
        else:
            outs[0][...], outs[1][...] = acc_gu[...].astype(BF16), acc_dn[...].astype(BF16)


def feed_grads(two, cots, inners, d_gus, info, n, n_z):
    half, dim = two[0][0].shape
    cols = inners[0].shape[1]
    shapes = [(n_z, (dim + cols) // n_z, dim)] if 2 * cols == dim else [(dim, 2 * cols), (cols, dim)]
    return call(
        functools.partial(feed_grads_kernel, n, n_z, half),
        "feed_grads",
        [shape_of(*shape) for shape in shapes],
        [any_spec()] * (6 * n + 4),
        [whole_spec(shape) for shape in shapes],
        grid=(2 * n,),
        scratch=[
            pltpu.VMEM((2, 2 * half, dim), BF16),
            pltpu.VMEM((2, 2 * half, dim), BF16),
            pltpu.VMEM((2, 2 * half, cols), BF16),
            pltpu.VMEM((2, 2 * half, 2 * cols), BF16),
            pltpu.VMEM((dim, 2 * cols), F32),
            pltpu.VMEM((cols, dim), F32),
            pltpu.SemaphoreType.DMA((2, 6)),
        ],
        estimate=cost(20),
    )(info, *two[0], *two[1], *cots, *inners, *d_gus)


def turn_kernel(n, width, info, *refs):
    parts, (cot, hidden, w), (d_hidden, e_out), outs = (
        refs[:n],
        refs[n : n + 3],
        refs[n + 3 : n + 5],
        refs[n + 5 :],
    )
    d_norm = parts[0][...].astype(F32)
    for r in range(1, n):
        d_norm += parts[r][...].astype(F32)
    total = cot[0].astype(F32) + back_normed(hidden[...], d_norm)
    d_hidden[...] = total
    e_rows = total.astype(BF16)
    e_out[...] = e_rows
    for r in range(n):
        for q in range(2):
            outs[r][q] = mm_nt(e_rows, w[head_rows(info, r * 2 + q, width), :]).astype(BF16)


def turn(info, parts, cot, which, hidden, w_out, width, n):
    half, dim = hidden.shape
    return call(
        functools.partial(turn_kernel, n, width),
        "turn",
        [shape_of(half, dim, dtype=F32), shape_of(half, dim)] + [shape_of(2, half, width)] * n,
        [whole_spec((half, dim))] * n
        + [pick_spec((half, dim), which), whole_spec((half, dim)), whole_spec((dim, dim))],
        [whole_spec((half, dim))] * 2 + [whole_spec((2, half, width))] * n,
        estimate=cost(6),
    )(info, *parts, cot, hidden, w_out)


def out_grads_kernel(n, width, info, att0, att1, e0, e1, out):
    for j in range(2 * n):
        cols = slice(j * width, (j + 1) * width)
        total = mm_tn(att0[:, cols], e0[...]) + mm_tn(att1[:, cols], e1[...])
        out[head_rows(info, j, width), :] = total.astype(BF16)


def out_grads(info, atts, es, width, n):
    half, dim = es[0].shape
    return call(
        functools.partial(out_grads_kernel, n, width),
        "out_grads",
        shape_of(dim, dim),
        [whole_spec((half, dim))] * 4,
        whole_spec((dim, dim)),
        estimate=cost(5),
    )(info, *atts, *es)


def qkv_grads_kernel(n, half, info, *refs):
    blocks, (d0, d1, out) = refs[: 2 * n], refs[2 * n :]
    total = None
    for s, d_qkv in enumerate((d0, d1)):
        for k in range(2 * n):
            part = mm_tn(d_qkv[k * half : (k + 1) * half, :], blocks[k][s])
            total = part if total is None else total + part
    out[...] = total.T.astype(BF16)


def qkv_grads(info, blocks, d_qkvs, n):
    half, dim = blocks[0].shape[1:]
    rows, width3 = d_qkvs[0].shape
    return call(
        functools.partial(qkv_grads_kernel, n, half),
        "qkv_grads",
        shape_of(dim, width3),
        [whole_spec((2, half, dim))] * (2 * n) + [whole_spec((rows, width3))] * 2,
        whole_spec((dim, width3)),
        estimate=cost(9),
    )(info, *blocks, *d_qkvs)


def pack_qkv_kernel(width, info, gain, wq, wk, wv, mine, theirs):
    scale = gain[...]
    mine[...] = jnp.zeros_like(mine)
    theirs[...] = jnp.zeros_like(theirs)
    for out, flip in ((mine, 0), (theirs, 1)):
        at = (info[0] * 2 + (info[1] ^ flip)) * width
        for i, w in enumerate((wq, wk, wv)):
            rows = w[:, pl.ds(pl.multiple_of(at, width), width)].astype(F32)
            out[:, i * width : (i + 1) * width] = (rows * scale).astype(BF16)


def pack_hidden_kernel(n_z, cut, down_rows, info, gain, wg, wu, mine, theirs):
    scale = gain[...]
    for out, flip in ((mine, 0), (theirs, 1)):
        for i, w in enumerate((wg, wu)):
            for z in range(n_z):
                at = (2 * z + (info[1] ^ flip)) * down_rows + info[0] * cut
                rows = w[:, pl.ds(pl.multiple_of(at, cut), cut)].astype(F32)
                to = (i * n_z + z) * cut
                out[:, to : to + cut] = (rows * scale).astype(BF16)


def pack(kernel, name, info, gain, weights, cols):
    shard = gain.shape[0]
    return call(
        kernel,
        name,
        [shape_of(shard, cols)] * 2,
        [whole_spec(a.shape) for a in (gain, *weights)],
        [whole_spec((shard, cols))] * 2,
        estimate=cost(9),
    )(info, gain, *weights)


def finish_kernel(n, shard, cut, down_rows, info, *refs):
    parts, (gain, wg, wu), (gg, gu, gd, gain_out) = refs[:n], refs[n : n + 3], refs[n + 3 :]
    chip, core = info[0], info[1]
    scale = gain[...]
    half = wg.shape[1] // (2 * n)
    total = jnp.zeros((shard, 1), F32)
    for r in range(n):
        gd[pl.ds(pl.multiple_of((chip ^ r) * cut, cut), cut), :] = parts[r][2 * shard : 2 * shard + cut, :].astype(F32)
        for q in range(2):
            rows = slice(q * shard, (q + 1) * shard)
            for z in range(half // cut):
                at = (2 * z + (core ^ q)) * down_rows + (chip ^ r) * cut
                at = pl.ds(pl.multiple_of(at, cut), cut)
                raw = parts[r][rows, z * cut : (z + 1) * cut].astype(F32)
                total += jnp.sum(raw * wg[:, at].astype(F32), axis=1, keepdims=True)
                gg[:, at] = raw * scale
                raw = parts[r][rows, half + z * cut : half + (z + 1) * cut].astype(F32)
                total += jnp.sum(raw * wu[:, at].astype(F32), axis=1, keepdims=True)
                gu[:, at] = raw * scale
    gain_out[...] = jnp.broadcast_to(total, (shard, 128)).T[0:1, :]


def finish_qkv_kernel(n, width, info, *refs):
    parts, (gain, *ws), (*grads, go, gain_out) = refs[:n], refs[n : n + 4], refs[n + 4 :]
    out = parts[0][:, 6 * width :].astype(F32)
    for r in range(1, n):
        out += parts[r][:, 6 * width :].astype(F32)
    go[...] = out
    scale = gain[...]
    total = jnp.zeros(scale.shape, F32)
    for r in range(n):
        for q in range(2):
            at = head_rows(info, r * 2 + q, width)
            for i in range(3):
                raw = parts[r][:, (3 * q + i) * width : (3 * q + i + 1) * width].astype(F32)
                total += jnp.sum(raw * ws[i][:, at].astype(F32), axis=1, keepdims=True)
                grads[i][:, at] = raw * scale
    gain_out[...] = jnp.broadcast_to(total, (scale.shape[0], 128)).T[0:1, :]


def send(value, step):
    count = lax.axis_size("ctx")
    return lax.ppermute(value, "ctx", [(i, i ^ step) for i in range(count)])


def swap(value):
    return lax.ppermute(value, "core", [(0, 1), (1, 0)])


def after(value, *others):
    return lax.optimization_barrier((value,) + others)[0]


def gather_near(own):
    n = lax.axis_size("ctx")
    return [send(own, r) for r in range(1, 3 if n == 4 else n)]


def gather_far(near):
    n = lax.axis_size("ctx")
    if n != 4:
        return near
    onward = jnp.where(lax.axis_index("core") == 0, near[1], near[0])
    pairs = [(c * 2 + p, (c ^ (1 + p)) * 2 + p) for c in range(n) for p in range(2)]
    return near + [lax.ppermute(onward, ("ctx", "core"), pairs)]


def gather_cores(own, others):
    mine = [own] + others
    return mine + [swap(block) for block in mine]


def together(*values):
    return lax.optimization_barrier(values)


def plane_join(mine, other):
    got = swap(other)
    return [(mine[r].astype(F32) + got[r].astype(F32)).astype(BF16) for r in range(mine.shape[0])]


def plane_send(joined):
    return [joined[0]] + [send(joined[r], r) for r in range(1, len(joined))]


def ordered(first, second, core):
    return jnp.where(core == 0, jnp.stack([first, second]), jnp.stack([second, first]))


def send_heads(parts):
    return [parts[0]] + [send(parts[r], r) for r in range(1, len(parts))]


def other_heads(got):
    return swap(jnp.stack([g[1] for g in got]))


def mask_info(codes, half, chip, core):
    tiles = codes.reshape(-1, half)
    first, last = tiles[:, :1], tiles[:, half - 1 :]
    every = codes.reshape(1, -1)

    def count(test):
        return jnp.sum(test.astype(jnp.int32), axis=1)

    low = count(every // DOC < first // DOC) // half
    ends = jnp.minimum(count(every // DOC <= last // DOC), count(every % DOC <= last % DOC))
    high = (ends + half - 1) // half
    info = jnp.concatenate([jnp.stack([chip, core]).astype(jnp.int32), low, high])
    return info, every


def body(
    block_in, cotangent, doc_ids, block_ids, gain_attn, w_query, w_key, w_value, w_out, gain_ffn, w_gate, w_up, w_down
):
    n, n_z = lax.axis_size("ctx"), lax.axis_size("z")
    chip, core = lax.axis_index("ctx"), lax.axis_index("core")
    piece, dim = block_in.shape[1], block_in.shape[2]
    half = piece // 2
    shard = w_query.shape[0]
    width = dim // (2 * n)
    down_rows = w_down.shape[0]
    cut = down_rows // n
    me = jnp.stack([chip, core]).astype(jnp.int32)

    def own_half(rows, which):
        return lax.dynamic_slice_in_dim(rows, which * half, half, axis=0)

    def both_rows(rows):
        return ordered(own_half(rows, core), swap(own_half(rows, 1 - core)), core)

    x_rows = both_rows(block_in[0])
    n_one, inv1 = normed(x_rows.astype(F32))
    one_own = n_one.astype(BF16)
    one_near = gather_near(one_own)

    def head_cols(which):
        at = (chip * 2 + which) * width
        return jnp.concatenate(
            [lax.dynamic_slice_in_dim(w, at, width, axis=1) for w in (w_query, w_key, w_value)], axis=1
        )

    def hidden_slices(which):
        return jnp.concatenate(
            [
                lax.dynamic_slice_in_dim(w, (2 * z + which) * down_rows + chip * cut, cut, axis=1)
                for w in (w_gate, w_up)
                for z in range(n_z)
            ],
            axis=1,
        )

    def scaled(w, gain):
        return (w.astype(F32) * gain.astype(F32)[:, None]).astype(BF16)

    def over_z(mine, theirs):
        both = ordered(mine, swap(theirs), core).reshape(2 * shard, -1)
        return lax.all_gather(both, "z", axis=0, tiled=True)

    g1, g2 = gain_attn.astype(F32)[:, None], gain_ffn.astype(F32)[:, None]
    if cut % 128 == 0:
        packed = after(me, one_own)
        w_qkv = over_z(
            *pack(functools.partial(pack_qkv_kernel, width), "pack_qkv", packed, g1, (w_query, w_key, w_value), 4 * width)
        )
        hidden_pair = pack(
            functools.partial(pack_hidden_kernel, n_z, cut, down_rows),
            "pack_hidden",
            packed,
            g2,
            (w_gate, w_up),
            2 * n_z * cut,
        )
    else:
        w_qkv = over_z(scaled(head_cols(core), gain_attn), scaled(head_cols(1 - core), gain_attn))
        hidden_pair = scaled(hidden_slices(core), gain_ffn), scaled(hidden_slices(1 - core), gain_ffn)
    w_out_full = lax.all_gather(after(w_out, w_qkv), ("z", "core"), axis=0, tiled=True)
    cols = n_z * cut
    down_cut = lax.dynamic_slice_in_dim(w_down, chip * cut, cut, axis=0)
    if 2 * cols == dim:
        gu_cut = ordered(hidden_pair[0], swap(hidden_pair[1]), core).reshape(2 * shard, dim)
        w_ff = jnp.concatenate([gu_cut, down_cut], axis=0)
        w_ffs = [lax.all_gather(after(w_ff, w_out_full), "z", axis=0)]
    else:
        w_ffs = [over_z(*hidden_pair), lax.all_gather(down_cut, "z", axis=0, tiled=True)]

    one_near, w_qkv, code = together(one_near, w_qkv, doc_ids[0] * DOC + block_ids[0])
    one = gather_cores(one_own, gather_far(one_near))
    codes = jnp.stack([code] + [send(code, r) for r in range(1, n)])
    codes = ordered(codes, swap(codes), core)
    ids = [mask_info(codes[s], half, chip, core) for s in range(2)]
    infos, code_rows = [i[0] for i in ids], [i[1] for i in ids]
    cot_rows = both_rows(after(cotangent[0], one_own))
    one, infos, cot_own = together(one, infos, cot_rows)

    cot_near = gather_near(cot_own)
    qkv0, *mixed0, lse0 = attend(one, 0, w_qkv, (infos[0], code_rows[0]), n)
    mixed0, cot_near, info1 = together(mixed0, cot_near, infos[1])
    got0 = send_heads(mixed0)
    cot_all = gather_far(cot_near)
    qkv1, *mixed1, lse1 = attend(one, 1, w_qkv, (info1, code_rows[1]), n)
    other0 = other_heads(got0)
    mixed1, got0, other0, cot_all, go = together(mixed1, got0, other0, cot_all, me)
    got1 = send_heads(mixed1)
    cots = gather_cores(cot_own, cot_all)
    att0, hidden0, norm0 = mix(go, got0, other0, x_rows, 0, w_out_full, n)
    other1 = other_heads(got1)
    norm0, got1, other1, go = together(norm0, got1, other1, me)
    near0 = gather_near(norm0)
    att1, hidden1, norm1 = mix(go, got1, other1, x_rows, 1, w_out_full, n)
    near0, norm1, cots = together(near0, norm1, cots)
    two0 = gather_cores(norm0, gather_far(near0))
    two0, norm1, go = together(two0, norm1, me)

    near1 = gather_near(norm1)
    inner0, d_gu0, d_mine0, d_other0, o_mine0, o_other0 = feed(two0, cots, 0, w_ffs, cols, go, n)
    near1, d_mine0, d_other0 = together(near1, d_mine0, d_other0)
    far1 = gather_far(near1)
    joined0 = plane_join(d_mine0, d_other0)
    two1 = gather_cores(norm1, far1)
    joined0, two1, go = together(joined0, two1, me)
    parts0 = plane_send(joined0)
    inner1, d_gu1, d_mine1, d_other1, o_mine1, o_other1 = feed(two1, cots, 1, w_ffs, cols, go, n)
    parts0, d_mine1, d_other1, go = together(parts0, d_mine1, d_other1, me)
    joined1 = plane_join(d_mine1, d_other1)
    d_hidden0, e0, *d_mix0 = turn(go, parts0, cot_rows, 0, hidden0, w_out_full, width, n)
    joined1, d_mix0, o_other0, o_other1, go = together(joined1, d_mix0, o_other0, o_other1, me)
    parts1 = plane_send(joined1)
    d_got0 = send_heads(d_mix0)
    out_others = [swap(o_other0), swap(o_other1)]
    grads_ff = feed_grads((two0, two1), cots, (inner0, inner1), (d_gu0, d_gu1), go, n, n_z)
    d_other_heads0 = other_heads(d_got0)
    parts1, d_got0, d_other_heads0, out_others, raw_ff, go = together(
        parts1, d_got0, d_other_heads0, out_others, grads_ff, me
    )
    grads_ff = [lax.psum_scatter(g, "z", scatter_dimension=0, tiled=True) for g in raw_ff]
    d_hidden1, e1, *d_mix1 = turn(go, parts1, cot_rows, 1, hidden1, w_out_full, width, n)
    d_mix1, o_mine0, o_mine1, go = together(d_mix1, o_mine0, o_mine1, me)
    d_got1 = send_heads(d_mix1)
    d_other_heads1 = other_heads(d_got1)
    grads_wo = out_grads(go, (att0, att1), (e0, e1), width, n)
    wo_shard = lax.psum_scatter(grads_wo, ("z", "core"), scatter_dimension=0, tiled=True)
    outs = [
        jnp.stack([(m[r].astype(F32) + t[r].astype(F32)).astype(BF16) for m, t in zip((o_mine0, o_mine1), out_others)])
        for r in range(n)
    ]
    outs, grads_wo, info0 = together(outs, grads_wo, infos[0])

    out_near = [send(outs[r], r) for r in range(1, 3)]
    d_qkv0, a_mine0, a_other0 = attend_back(
        qkv0, w_qkv, lse0, mixed0, d_got0, d_other_heads0, (info0, code_rows[0]), n
    )
    out_near, a_mine0, a_other0, d_got1, d_other_heads1 = together(out_near, a_mine0, a_other0, d_got1, d_other_heads1)
    joined0 = plane_join(a_mine0, a_other0)
    joined0, info1 = together(joined0, infos[1])
    parts0 = plane_send(joined0)
    d_qkv1, a_mine1, a_other1 = attend_back(
        qkv1, w_qkv, lse1, mixed1, d_got1, d_other_heads1, (info1, code_rows[1]), n
    )
    parts0, a_mine1, a_other1, grads_ff = together(parts0, a_mine1, a_other1, grads_ff)
    joined1 = plane_join(a_mine1, a_other1)
    joined1, go, outs_far = together(joined1, me, outs[3:])
    parts1 = plane_send(joined1)
    grad_qkv = qkv_grads(go, one, (d_qkv0, d_qkv1), n)
    grad_qkv = lax.psum_scatter(grad_qkv, "z", scatter_dimension=0, tiled=True)
    out_parts = [outs[0]] + out_near + [send(o, r) for r, o in enumerate(outs_far, 3)]
    out_rows = jnp.stack([hidden0, hidden1])
    for part in out_parts:
        out_rows = out_rows + part.astype(F32)
    out_rows = out_rows.astype(BF16)
    in_rows = [
        d_hidden + back_normed(x_rows[s].astype(F32), sum(p.astype(F32) for p in parts))
        for s, (d_hidden, parts) in enumerate(((d_hidden0, parts0), (d_hidden1, parts1)))
    ]

    def own_rows(pair):
        mine = lax.dynamic_index_in_dim(pair, core, 0, keepdims=False)
        theirs = swap(lax.dynamic_index_in_dim(pair, 1 - core, 0, keepdims=False))
        return ordered(mine, theirs, core).reshape(1, piece, dim)

    block_out = own_rows(out_rows)
    input_grad = own_rows(jnp.stack(in_rows))

    def to_owner(part):
        mine = lax.dynamic_slice_in_dim(part, core * shard, shard, axis=0)
        theirs = lax.dynamic_slice_in_dim(part, (1 - core) * shard, shard, axis=0)
        return mine, swap(theirs)

    if len(grads_ff) == 1:
        gu_part, dn_part = grads_ff[0][0, : 2 * shard], grads_ff[0][0, 2 * shard :]
    else:
        gu_part, dn_part = grads_ff
    if cut % 128 == 0:
        sent = jnp.concatenate([*to_owner(gu_part), dn_part], axis=0)
        packs = [sent] + [send(sent, r) for r in range(1, n)]
        ff = w_gate.shape[1]
        raw = call(
            functools.partial(finish_kernel, n, shard, cut, down_rows),
            "finish",
            [shape_of(shard, ff, dtype=F32)] * 2
            + [shape_of(down_rows, dim, dtype=F32), shape_of(1, shard, dtype=F32)],
            [whole_spec(sent.shape)] * n + [whole_spec((shard, 1)), whole_spec((shard, ff)), whole_spec((shard, ff))],
            [whole_spec((shard, ff))] * 2 + [whole_spec((down_rows, dim)), whole_spec((1, shard))],
            estimate=cost(7),
        )(me, *packs, g2, w_gate, w_up)
        grad_gate, grad_up, grad_down, grad_gain_ffn = raw
        both = jnp.concatenate([*to_owner(grad_qkv), wo_shard], axis=1)
        boths = [both] + [send(both, r) for r in range(1, n)]
        raw = call(
            functools.partial(finish_qkv_kernel, n, width),
            "finish_qkv",
            [shape_of(shard, dim, dtype=F32)] * 4 + [shape_of(1, shard, dtype=F32)],
            [whole_spec(both.shape)] * n + [whole_spec((shard, 1))] + [whole_spec((shard, dim))] * 3,
            [whole_spec((shard, dim))] * 4 + [whole_spec((1, shard))],
            estimate=cost(4),
        )(me, *boths, g1, w_query, w_key, w_value)
        grad_q, grad_k, grad_v, grad_wo, grad_gain_attn = raw
        grad_gain_attn, grad_gain_ffn = grad_gain_attn.reshape(shard), grad_gain_ffn.reshape(shard)
    else:

        def over_ctx(part):
            both = ordered(*to_owner(part), core)
            return lax.all_gather(both, "ctx", axis=0).transpose(2, 0, 1, 3)

        qkv_shard = over_ctx(grad_qkv).reshape(shard, 2 * n, 3, width).astype(F32)
        raw_q, raw_k, raw_v = (qkv_shard[:, :, i].reshape(shard, dim) for i in range(3))
        gu_shard = over_ctx(gu_part).reshape(shard, n, 2, 2, n_z, cut).astype(F32)
        raw_g, raw_u = (
            gu_shard[:, :, :, i].transpose(0, 3, 2, 1, 4).reshape(shard, -1) for i in range(2)
        )
        grad_down = lax.all_gather(dn_part, "ctx", axis=0, tiled=True).astype(F32)
        grad_wo = lax.psum(wo_shard, "ctx").astype(F32)

        def row_sum(pairs):
            return sum(jnp.sum(w.astype(F32) * g, axis=1) for w, g in pairs)

        grad_gain_attn = row_sum([(w_query, raw_q), (w_key, raw_k), (w_value, raw_v)])
        grad_gain_ffn = row_sum([(w_gate, raw_g), (w_up, raw_u)])
        grad_q, grad_k, grad_v, grad_gate, grad_up = raw_q * g1, raw_k * g1, raw_v * g1, raw_g * g2, raw_u * g2
    return (
        block_out,
        input_grad,
        grad_gain_attn,
        grad_q,
        grad_k,
        grad_v,
        grad_wo,
        grad_gain_ffn,
        grad_gate,
        grad_up,
        grad_down,
    )


def solution(mesh):
    n_ctx, n_fsdp = mesh.devices.shape
    inner = Mesh(mesh.devices.reshape(n_ctx, n_fsdp // 2, 2), ("ctx", "z", "core"))
    fsdp = ("z", "core")
    act, ids, vec, mat = P(fsdp, "ctx", None), P(fsdp, "ctx"), P(fsdp), P(fsdp, None)
    return jax.shard_map(
        body,
        mesh=inner,
        in_specs=(act, act, ids, ids, vec, mat, mat, mat, mat, vec, mat, mat, mat),
        out_specs=(act, act, vec, mat, mat, mat, mat, vec, mat, mat, mat),
        check_vma=False,
    )
```

```python
import functools

import jax
import jax.numpy as jnp
from jax import lax
from jax.experimental import pallas as pl
from jax.experimental.pallas import tpu as pltpu
from jax.sharding import Mesh
from jax.sharding import PartitionSpec as P

HEAD_DIM = 64
NORM_EPS = 1e-05
MASKED = -1e30
START_MAX = -1e29
SCALE = HEAD_DIM ** (-0.5)
DOC = 1 << 16
F32 = jnp.float32
BF16 = jnp.bfloat16
NT = (((1,), (1,)), ((), ()))
TN = (((0,), (0,)), ((), ()))


def mm(a, b):
    return jnp.dot(a, b, preferred_element_type=F32)


def mm_nt(a, b):
    return lax.dot_general(a, b, NT, preferred_element_type=F32)


def mm_tn(a, b):
    return lax.dot_general(a, b, TN, preferred_element_type=F32)


def cost(us):
    return pl.CostEstimate(flops=int(us * 1e9), bytes_accessed=1000, transcendentals=0)


def whole_spec(shape, **kw):
    return pl.BlockSpec(shape, lambda *_: (0,) * len(shape), **kw)


def pick_spec(shape, index):
    return pl.BlockSpec((1,) + shape, lambda *_: (index,) + (0,) * len(shape))


def any_spec():
    return pl.BlockSpec(memory_space=pl.ANY)


def call(kernel, name, out_shape, in_specs, out_specs, grid=(1,), scratch=(), estimate=None, prefetch=1):
    return pl.pallas_call(
        kernel,
        out_shape=out_shape,
        grid_spec=pltpu.PrefetchScalarGridSpec(
            num_scalar_prefetch=prefetch,
            grid=grid,
            in_specs=in_specs,
            out_specs=out_specs,
            scratch_shapes=list(scratch),
        ),
        cost_estimate=estimate,
        name=name,
    )


def shape_of(*dims, dtype=BF16):
    return jax.ShapeDtypeStruct(dims, dtype)


def head_stack(rows, heads):
    lane = lax.broadcasted_iota(jnp.int32, rows.shape, 1) // HEAD_DIM
    return jnp.concatenate(
        [jnp.where(lane == h, rows, jnp.zeros_like(rows)) for h in range(heads)], axis=0
    )


def query_tile(step, n, info):
    r, dp = step % n, step // n
    return r, dp, r * 2 + (dp ^ info[1])


def key_tile(a, n, info):
    r = (a // 2) ^ info[0]
    return ((a % 2) ^ info[1]) * n + r, r * 2 + a % 2


def query_bounds(code_row, q_ids, half, heads):
    high = code_row[:, pl.ds(pl.multiple_of(q_ids * half, half), half)]
    low = (high // DOC) * DOC
    return jnp.concatenate([low] * heads, axis=1), jnp.concatenate([high] * heads, axis=1)


def key_pair(first, last, turn, n, info, half, code_col, bounds):
    low, high = bounds
    for i in range(2):
        a = first + 2 * turn + i
        place, k_ids = key_tile(jnp.minimum(a, last - 1), n, info)
        keys = code_col[pl.ds(pl.multiple_of(k_ids * half, half), half), 0:1]
        if i:
            keys = jnp.where(a < last, keys, -1)
        yield pl.multiple_of(place * half, half), (keys >= low) & (keys <= high)


def attend_kernel(n, heads, half, info, *refs):
    blocks, (w, code_row), (qkv, *outs, lse), (v_t, code_col) = (
        refs[: 2 * n],
        refs[2 * n : 2 * n + 2],
        refs[2 * n + 2 : 3 * n + 4],
        refs[3 * n + 4 :],
    )
    width = heads * HEAD_DIM
    step = pl.program_id(0)

    @pl.when(step == 0)
    def _():
        for k in range(2 * n):
            qkv[k * half : (k + 1) * half, :] = mm(blocks[k][0], w[...]).astype(BF16)
        v_t[...] = qkv[:, 2 * width : 3 * width].T
        code_col[...] = jnp.broadcast_to(code_row[...], (8, code_row.shape[1])).T

    r, dp, q_ids = query_tile(step, n, info)
    q_rows = qkv[pl.ds(pl.multiple_of(step * half, half), half), 0:width] * jnp.asarray(SCALE, BF16)
    q_heads = head_stack(q_rows, heads)

    first, last = info[2 + q_ids], info[2 + 2 * n + q_ids]
    bounds = query_bounds(code_row, q_ids, half, heads)

    def one(turn, carry):
        run_max, run_sum, accs = carry
        new_max, tiles = run_max, []
        for pos, keys_ok in key_pair(first, last, turn, n, info, half, code_col, bounds):
            scores = mm_nt(qkv[pl.ds(pos, half), width : 2 * width], q_heads)
            scores = jnp.where(keys_ok, scores, MASKED)
            new_max = jnp.maximum(new_max, jnp.max(scores, axis=0, keepdims=True))
            tiles.append((pos, scores))
        factor = jnp.exp(run_max - new_max)
        new_sum = run_sum * factor
        new_accs = [accs[h] * factor[:, h * half : (h + 1) * half] for h in range(heads)]
        for pos, scores in tiles:
            weights = jnp.exp(scores - new_max)
            new_sum += jnp.sum(weights, axis=0, keepdims=True)
            weights = weights.astype(BF16)
            for h in range(heads):
                v_head = v_t[h * HEAD_DIM : (h + 1) * HEAD_DIM, pl.ds(pos, half)]
                new_accs[h] += mm(v_head, weights[:, h * half : (h + 1) * half])
        return new_max, new_sum, tuple(new_accs)

    start = (
        jnp.full((1, heads * half), START_MAX, F32),
        jnp.zeros((1, heads * half), F32),
        tuple(jnp.zeros((HEAD_DIM, half), F32) for _ in range(heads)),
    )
    run_max, run_sum, accs = lax.fori_loop(0, (last - first + 1) // 2, one, start)
    parts = [accs[h] / run_sum[:, h * half : (h + 1) * half] for h in range(heads)]
    mixed = jnp.concatenate(parts, axis=0).T.astype(BF16)
    for k in range(n):

        @pl.when(r == k)
        def _():
            outs[k][dp] = mixed

    logs = run_max + jnp.log(run_sum)
    at = pl.ds(pl.multiple_of(step * half, half), half)
    for h in range(heads):
        lse[h : h + 1, at] = logs[:, h * half : (h + 1) * half]


def attend(blocks, which, w_qkv, ids, n):
    info, code_row = ids
    half, dim = blocks[0].shape[1:]
    width = dim // (2 * n)
    heads = width // HEAD_DIM
    rows = 2 * n * half
    return call(
        functools.partial(attend_kernel, n, heads, half),
        "attend",
        [shape_of(rows, 3 * width)]
        + [shape_of(2, half, width)] * n
        + [shape_of(heads, rows, dtype=F32)],
        [pick_spec((half, dim), which)] * (2 * n) + [whole_spec((dim, 3 * width)), whole_spec((1, rows))],
        [whole_spec((rows, 3 * width))] + [whole_spec((2, half, width))] * n + [whole_spec((heads, rows))],
        grid=(2 * n,),
        scratch=[pltpu.VMEM((width, rows), BF16), pltpu.VMEM((rows, 8), jnp.int32)],
        estimate=cost(21),
    )(info, *blocks, w_qkv, code_row)


def attend_back_kernel(n, heads, half, info, *refs):
    qkv, w, lse, code_row = refs[:4]
    mixes, d_mixes, (d_other,) = refs[4 : 4 + n], refs[4 + n : 4 + 2 * n], refs[4 + 2 * n : 5 + 2 * n]
    out, part_mine, part_other, k_t, dk, dv, code_col, do_now, mix_now = refs[5 + 2 * n :]
    width = heads * HEAD_DIM
    step = pl.program_id(0)

    @pl.when(step == 0)
    def _():
        k_t[...] = qkv[:, width : 2 * width].T
        code_col[...] = jnp.broadcast_to(code_row[...], (8, code_row.shape[1])).T
        dk[...] = jnp.zeros_like(dk)
        dv[...] = jnp.zeros_like(dv)

    r, dp, q_ids = query_tile(step, n, info)
    rows = pl.ds(pl.multiple_of(step * half, half), half)
    q_heads = head_stack(qkv[rows, 0:width] * jnp.asarray(SCALE, BF16), heads)
    for k in range(n):

        @pl.when(r == k)
        def _():
            mix_now[...] = mixes[k][dp]

        @pl.when((r == k) & (dp == 0))
        def _():
            do_now[...] = d_mixes[k][0]

    @pl.when(dp == 1)
    def _():
        do_now[...] = d_other[r]

    do_rows = do_now[...]
    do_heads = head_stack(do_rows, heads)
    prod = (do_rows.astype(F32) * mix_now[...].astype(F32)).T
    delta = jnp.concatenate(
        [
            jnp.sum(prod[h * HEAD_DIM : (h + 1) * HEAD_DIM], axis=0, keepdims=True)
            for h in range(heads)
        ],
        axis=1,
    )
    logs = jnp.concatenate([lse[h : h + 1, rows] for h in range(heads)], axis=1)

    first, last = info[2 + q_ids], info[2 + 2 * n + q_ids]
    bounds = query_bounds(code_row, q_ids, half, heads)

    def one(turn, dqs):
        new, done = list(dqs), []
        for pos, keys_ok in key_pair(first, last, turn, n, info, half, code_col, bounds):
            keys = qkv[pl.ds(pos, half), width : 2 * width]
            values = qkv[pl.ds(pos, half), 2 * width : 3 * width]
            scores = mm_nt(keys, q_heads)
            probs = jnp.where(keys_ok, jnp.exp(scores - logs), 0.0)
            d_probs = mm_nt(values, do_heads)
            d_scores = (probs * (d_probs - delta)).astype(BF16)
            done.append((pos, mm(probs.astype(BF16), do_heads), mm(d_scores, q_heads)))
            for h in range(heads):
                k_head = k_t[h * HEAD_DIM : (h + 1) * HEAD_DIM, pl.ds(pos, half)]
                new[h] += mm(k_head, d_scores[:, h * half : (h + 1) * half])
        for pos, d_values, d_keys in done:
            dv[pl.ds(pos, half), :] += d_values
            dk[pl.ds(pos, half), :] += d_keys
        return tuple(new)

    dqs = lax.fori_loop(
        0,
        (last - first + 1) // 2,
        one,
        tuple(jnp.zeros((HEAD_DIM, half), F32) for _ in range(heads)),
    )
    out[rows, 0:width] = (jnp.concatenate(dqs, axis=0) * SCALE).T.astype(BF16)

    @pl.when(step == 2 * n - 1)
    def _():
        out[:, width : 2 * width] = dk[...].astype(BF16)
        out[:, 2 * width : 3 * width] = dv[...].astype(BF16)
        for k in range(n):
            part_mine[k] = mm_nt(out[k * half : (k + 1) * half, :], w[...]).astype(BF16)
            part_other[k] = mm_nt(out[(n + k) * half : (n + k + 1) * half, :], w[...]).astype(BF16)


def attend_back(qkv, w_qkv, lse, mixes, d_mixes, d_other, ids, n):
    info, code_row = ids
    rows, width3 = qkv.shape
    width, dim = width3 // 3, w_qkv.shape[0]
    heads = width // HEAD_DIM
    half = rows // (2 * n)
    tile = (2, half, width)
    return call(
        functools.partial(attend_back_kernel, n, heads, half),
        "attend_back",
        [shape_of(rows, width3), shape_of(n, half, dim), shape_of(n, half, dim)],
        [whole_spec((rows, width3)), whole_spec((dim, width3)), whole_spec((heads, rows)), whole_spec((1, rows))]
        + [whole_spec(tile)] * (2 * n)
        + [whole_spec((n, half, width))],
        [whole_spec((rows, width3)), whole_spec((n, half, dim)), whole_spec((n, half, dim))],
        grid=(2 * n,),
        scratch=[
            pltpu.VMEM((width, rows), BF16),
            pltpu.VMEM((rows, width), F32),
            pltpu.VMEM((rows, width), F32),
            pltpu.VMEM((rows, 8), jnp.int32),
            pltpu.VMEM((half, width), BF16),
            pltpu.VMEM((half, width), BF16),
        ],
        estimate=cost(26),
    )(info, qkv, w_qkv, lse, code_row, *mixes, *d_mixes, d_other)


def normed(rows):
    inv = lax.rsqrt(jnp.mean(rows * rows, axis=-1, keepdims=True) + NORM_EPS)
    return rows * inv, inv


def back_normed(rows, d_norm):
    norm, inv = normed(rows)
    return inv * (d_norm - norm * jnp.mean(d_norm * norm, axis=-1, keepdims=True))


def head_rows(info, j, width):
    return pl.ds(pl.multiple_of((j ^ (info[0] * 2 + info[1])) * width, width), width)


def chip_rows(info, r, width):
    return pl.ds(pl.multiple_of((r ^ info[0]) * 2 * width, 2 * width), 2 * width)


def mix_kernel(n, width, info, *refs):
    parts, (others, x, w), (att, hidden, norm) = refs[:n], refs[n : n + 3], refs[n + 3 :]
    total = x[0].astype(F32)
    for r in range(n):
        mine, other = parts[r][0], others[r]
        pair = jnp.concatenate([jnp.where(info[1] == 0, mine, other), jnp.where(info[1] == 0, other, mine)], axis=1)
        att[:, 2 * r * width : 2 * (r + 1) * width] = pair
        total += mm(pair, w[chip_rows(info, r, width), :])
    hidden[...] = total
    norm[...] = normed(total)[0].astype(BF16)


def mix(info, parts, others, x, which, w_out, n):
    half, width = parts[0].shape[1:]
    dim = w_out.shape[0]
    return call(
        functools.partial(mix_kernel, n, width),
        "mix",
        [shape_of(half, dim), shape_of(half, dim, dtype=F32), shape_of(half, dim)],
        [whole_spec((2, half, width))] * n
        + [whole_spec((n, half, width)), pick_spec((half, dim), which), whole_spec((dim, dim))],
        [whole_spec((half, dim))] * 3,
        estimate=cost(5),
    )(info, *parts, others, x, w_out)


def feed_kernel(n, half, cols, which, info, *refs):
    two, cots = refs[: 2 * n], refs[2 * n : 4 * n]
    inner_out, d_gu_out, d_mine, d_other, o_mine, o_other, a_buf, c_buf, w_gu, w_dn, sems = refs[-11:]
    w_ffs = refs[4 * n : -11]
    step = pl.program_id(0)
    slot = step % 2

    def copies(r, at):
        got = []
        for dp in range(2):
            rows = pl.ds(dp * half, half)
            got.append(pltpu.make_async_copy(two[dp * n + r], a_buf.at[at, rows], sems.at[at, dp]))
            got.append(pltpu.make_async_copy(cots[dp * n + r].at[which], c_buf.at[at, rows], sems.at[at, 2 + dp]))
        return got

    @pl.when(step == 0)
    def _():
        for c in copies(0, 0):
            c.start()
        if len(w_ffs) == 1:
            n_z = w_ffs[0].shape[0]
            gu_rows, dn_rows = w_gu.shape[0] // n_z, cols // n_z
            for z in range(n_z):
                w_gu[z * gu_rows : (z + 1) * gu_rows, :] = w_ffs[0][z, :gu_rows, :]
                w_dn[z * dn_rows : (z + 1) * dn_rows, :] = w_ffs[0][z, gu_rows:, :]
        else:
            w_gu[...], w_dn[...] = w_ffs[0][...], w_ffs[1][...]

    for r in range(1, n):

        @pl.when(step + 1 == r)
        def _():
            for c in copies(r, r % 2):
                c.start()

    for c in copies(0, slot):
        c.wait()
    rows, cot = a_buf[slot], c_buf[slot]
    gu = mm(rows, w_gu[...])
    d_inner = mm_nt(cot, w_dn[...])
    gate, upper = gu[:, :cols], gu[:, cols:]
    sigma = jax.nn.sigmoid(gate)
    silu_gate = gate * sigma
    inner = (silu_gate * upper).astype(BF16)
    d_gate = (d_inner * upper * sigma * (1.0 + gate * (1.0 - sigma))).astype(BF16)
    d_upper = (d_inner * silu_gate).astype(BF16)
    inner_out[...] = inner
    d_gu_out[:, :cols] = d_gate
    d_gu_out[:, cols:] = d_upper
    d_rows = (mm_nt(d_gate, w_gu[:, :cols]) + mm_nt(d_upper, w_gu[:, cols:])).astype(BF16)
    d_mine[0] = d_rows[:half]
    d_other[0] = d_rows[half:]
    o_rows = mm(inner, w_dn[...]).astype(BF16)
    o_mine[0] = o_rows[:half]
    o_other[0] = o_rows[half:]


def feed(two, cots, which, w_ffs, cols, info, n):
    half, dim = two[0].shape
    rows = 2 * n * half
    block = pl.BlockSpec((1, half, dim), lambda i, *_: (i, 0, 0))
    return call(
        functools.partial(feed_kernel, n, half, cols, which),
        "feed",
        [shape_of(rows, cols), shape_of(rows, 2 * cols)] + [shape_of(n, half, dim)] * 4,
        [any_spec()] * (4 * n) + [whole_spec(w.shape) for w in w_ffs],
        [
            pl.BlockSpec((2 * half, cols), lambda i, *_: (i, 0)),
            pl.BlockSpec((2 * half, 2 * cols), lambda i, *_: (i, 0)),
        ]
        + [block] * 4,
        grid=(n,),
        scratch=[
            pltpu.VMEM((2, 2 * half, dim), BF16),
            pltpu.VMEM((2, 2 * half, dim), BF16),
            pltpu.VMEM((dim, 2 * cols), BF16),
            pltpu.VMEM((cols, dim), BF16),
            pltpu.SemaphoreType.DMA((2, 4)),
        ],
        estimate=cost(20),
    )(info, *two, *cots, *w_ffs)


def feed_grads_kernel(n, n_z, half, info, *refs):
    two, cots = (refs[: 2 * n], refs[2 * n : 4 * n]), refs[4 * n : 6 * n]
    inners, d_gus = refs[6 * n : 6 * n + 2], refs[6 * n + 2 : 6 * n + 4]
    a_buf, c_buf, z_buf, g_buf, acc_gu, acc_dn, sems = refs[-7:]
    outs = refs[6 * n + 4 : -7]
    step = pl.program_id(0)
    slot = step % 2
    gu_rows, dn_rows = acc_gu.shape[0] // n_z, acc_dn.shape[0] // n_z

    def copies(t, at):
        s, r = t // n, t % n
        got = []
        for dp in range(2):
            rows = pl.ds(dp * half, half)
            got.append(pltpu.make_async_copy(two[s][dp * n + r], a_buf.at[at, rows], sems.at[at, dp]))
            got.append(pltpu.make_async_copy(cots[dp * n + r].at[s], c_buf.at[at, rows], sems.at[at, 2 + dp]))
        rows = pl.ds(2 * r * half, 2 * half)
        got.append(pltpu.make_async_copy(inners[s].at[rows], z_buf.at[at], sems.at[at, 4]))
        got.append(pltpu.make_async_copy(d_gus[s].at[rows], g_buf.at[at], sems.at[at, 5]))
        return got

    @pl.when(step == 0)
    def _():
        for c in copies(0, 0):
            c.start()
        acc_gu[...] = jnp.zeros_like(acc_gu)
        acc_dn[...] = jnp.zeros_like(acc_dn)

    for t in range(1, 2 * n):

        @pl.when(step + 1 == t)
        def _():
            for c in copies(t, t % 2):
                c.start()

    for c in copies(0, slot):
        c.wait()
    acc_gu[...] += mm_tn(a_buf[slot], g_buf[slot])
    acc_dn[...] += mm_tn(z_buf[slot], c_buf[slot])

    @pl.when(step == 2 * n - 1)
    def _():
        if len(outs) == 1:
            for z in range(n_z):
                outs[0][z, :gu_rows, :] = acc_gu[z * gu_rows : (z + 1) * gu_rows, :].astype(BF16)
                outs[0][z, gu_rows:, :] = acc_dn[z * dn_rows : (z + 1) * dn_rows, :].astype(BF16)
        else:
            outs[0][...], outs[1][...] = acc_gu[...].astype(BF16), acc_dn[...].astype(BF16)


def feed_grads(two, cots, inners, d_gus, info, n, n_z):
    half, dim = two[0][0].shape
    cols = inners[0].shape[1]
    shapes = [(n_z, (dim + cols) // n_z, dim)] if 2 * cols == dim else [(dim, 2 * cols), (cols, dim)]
    return call(
        functools.partial(feed_grads_kernel, n, n_z, half),
        "feed_grads",
        [shape_of(*shape) for shape in shapes],
        [any_spec()] * (6 * n + 4),
        [whole_spec(shape) for shape in shapes],
        grid=(2 * n,),
        scratch=[
            pltpu.VMEM((2, 2 * half, dim), BF16),
            pltpu.VMEM((2, 2 * half, dim), BF16),
            pltpu.VMEM((2, 2 * half, cols), BF16),
            pltpu.VMEM((2, 2 * half, 2 * cols), BF16),
            pltpu.VMEM((dim, 2 * cols), F32),
            pltpu.VMEM((cols, dim), F32),
            pltpu.SemaphoreType.DMA((2, 6)),
        ],
        estimate=cost(20),
    )(info, *two[0], *two[1], *cots, *inners, *d_gus)


def turn_kernel(n, width, info, *refs):
    parts, (cot, hidden, w), (d_hidden, e_out), outs = (
        refs[:n],
        refs[n : n + 3],
        refs[n + 3 : n + 5],
        refs[n + 5 :],
    )
    d_norm = parts[0][...].astype(F32)
    for r in range(1, n):
        d_norm += parts[r][...].astype(F32)
    total = cot[0].astype(F32) + back_normed(hidden[...], d_norm)
    d_hidden[...] = total
    e_rows = total.astype(BF16)
    e_out[...] = e_rows
    for r in range(n):
        pair = mm_nt(e_rows, w[chip_rows(info, r, width), :]).astype(BF16)
        outs[r][info[1]] = pair[:, :width]
        outs[r][1 - info[1]] = pair[:, width:]


def turn(info, parts, cot, which, hidden, w_out, width, n):
    half, dim = hidden.shape
    return call(
        functools.partial(turn_kernel, n, width),
        "turn",
        [shape_of(half, dim, dtype=F32), shape_of(half, dim)] + [shape_of(2, half, width)] * n,
        [whole_spec((half, dim))] * n
        + [pick_spec((half, dim), which), whole_spec((half, dim)), whole_spec((dim, dim))],
        [whole_spec((half, dim))] * 2 + [whole_spec((2, half, width))] * n,
        estimate=cost(6),
    )(info, *parts, cot, hidden, w_out)


def out_grads_kernel(n, width, info, att0, att1, e0, e1, out):
    for r in range(n):
        cols = slice(2 * r * width, 2 * (r + 1) * width)
        total = mm_tn(att0[:, cols], e0[...]) + mm_tn(att1[:, cols], e1[...])
        out[chip_rows(info, r, width), :] = total.astype(BF16)


def out_grads(info, atts, es, width, n):
    half, dim = es[0].shape
    return call(
        functools.partial(out_grads_kernel, n, width),
        "out_grads",
        shape_of(dim, dim),
        [whole_spec((half, dim))] * 4,
        whole_spec((dim, dim)),
        estimate=cost(5),
    )(info, *atts, *es)


def qkv_grads_kernel(n, half, info, *refs):
    blocks, (d0, d1, out) = refs[: 2 * n], refs[2 * n :]
    total = None
    for s, d_qkv in enumerate((d0, d1)):
        for k in range(2 * n):
            part = mm_tn(d_qkv[k * half : (k + 1) * half, :], blocks[k][s])
            total = part if total is None else total + part
    out[...] = total.T.astype(BF16)


def qkv_grads(info, blocks, d_qkvs, n):
    half, dim = blocks[0].shape[1:]
    rows, width3 = d_qkvs[0].shape
    return call(
        functools.partial(qkv_grads_kernel, n, half),
        "qkv_grads",
        shape_of(dim, width3),
        [whole_spec((2, half, dim))] * (2 * n) + [whole_spec((rows, width3))] * 2,
        whole_spec((dim, width3)),
        estimate=cost(0.2),
    )(info, *blocks, *d_qkvs)


def pack_qkv_kernel(width, info, gain, wq, wk, wv, mine, theirs):
    scale = gain[...]
    mine[...] = jnp.zeros_like(mine)
    theirs[...] = jnp.zeros_like(theirs)
    for out, flip in ((mine, 0), (theirs, 1)):
        at = (info[0] * 2 + (info[1] ^ flip)) * width
        for i, w in enumerate((wq, wk, wv)):
            rows = w[:, pl.ds(pl.multiple_of(at, width), width)].astype(F32)
            out[:, i * width : (i + 1) * width] = (rows * scale).astype(BF16)


def pack_hidden_kernel(n_z, cut, down_rows, info, gain, wg, wu, mine, theirs):
    scale = gain[...]
    for out, flip in ((mine, 0), (theirs, 1)):
        for i, w in enumerate((wg, wu)):
            for z in range(n_z):
                at = (2 * z + (info[1] ^ flip)) * down_rows + info[0] * cut
                rows = w[:, pl.ds(pl.multiple_of(at, cut), cut)].astype(F32)
                to = (i * n_z + z) * cut
                out[:, to : to + cut] = (rows * scale).astype(BF16)


def pack(kernel, name, info, gain, weights, cols):
    shard = gain.shape[0]
    return call(
        kernel,
        name,
        [shape_of(shard, cols)] * 2,
        [whole_spec(a.shape) for a in (gain, *weights)],
        [whole_spec((shard, cols))] * 2,
        estimate=cost(9),
    )(info, gain, *weights)


def finish_kernel(n, shard, cut, down_rows, info, *refs):
    parts, (gain, wg, wu), (gg, gu, gd, gain_out) = refs[:n], refs[n : n + 3], refs[n + 3 :]
    chip, core = info[0], info[1]
    scale = gain[...]
    half = wg.shape[1] // (2 * n)
    total = jnp.zeros((shard, 1), F32)
    for r in range(n):
        gd[pl.ds(pl.multiple_of((chip ^ r) * cut, cut), cut), :] = parts[r][2 * shard : 2 * shard + cut, :].astype(F32)
        for q in range(2):
            rows = slice(q * shard, (q + 1) * shard)
            for z in range(half // cut):
                at = (2 * z + (core ^ q)) * down_rows + (chip ^ r) * cut
                at = pl.ds(pl.multiple_of(at, cut), cut)
                raw = parts[r][rows, z * cut : (z + 1) * cut].astype(F32)
                total += jnp.sum(raw * wg[:, at].astype(F32), axis=1, keepdims=True)
                gg[:, at] = raw * scale
                raw = parts[r][rows, half + z * cut : half + (z + 1) * cut].astype(F32)
                total += jnp.sum(raw * wu[:, at].astype(F32), axis=1, keepdims=True)
                gu[:, at] = raw * scale
    gain_out[...] = jnp.broadcast_to(total, (shard, 128)).T[0:1, :]


def finish_qkv_kernel(n, width, info, *refs):
    parts, (gain, *ws), (*grads, go, gain_out) = refs[:n], refs[n : n + 4], refs[n + 4 :]
    out = parts[0][:, 6 * width :].astype(F32)
    for r in range(1, n):
        out += parts[r][:, 6 * width :].astype(F32)
    go[...] = out
    scale = gain[...]
    total = jnp.zeros(scale.shape, F32)
    for r in range(n):
        for q in range(2):
            at = head_rows(info, r * 2 + q, width)
            for i in range(3):
                raw = parts[r][:, (3 * q + i) * width : (3 * q + i + 1) * width].astype(F32)
                total += jnp.sum(raw * ws[i][:, at].astype(F32), axis=1, keepdims=True)
                grads[i][:, at] = raw * scale
    gain_out[...] = jnp.broadcast_to(total, (scale.shape[0], 128)).T[0:1, :]


def send(value, step):
    count = lax.axis_size("ctx")
    return lax.ppermute(value, "ctx", [(i, i ^ step) for i in range(count)])


def swap(value):
    return lax.ppermute(value, "core", [(0, 1), (1, 0)])


def after(value, *others):
    return lax.optimization_barrier((value,) + others)[0]


def gather_near(own):
    n = lax.axis_size("ctx")
    return [send(own, r) for r in range(1, 3 if n == 4 else n)]


def onward_of(near):
    return jnp.where(lax.axis_index("core") == 0, near[1], near[0])


def gather_far(near):
    n = lax.axis_size("ctx")
    if n != 4:
        return near
    onward = onward_of(near)
    pairs = [(c * 2 + p, (c ^ (1 + p)) * 2 + p) for c in range(n) for p in range(2)]
    return near + [lax.ppermute(onward, ("ctx", "core"), pairs)]


def gather_cores(own, others):
    mine = [own] + others
    return mine + [swap(block) for block in mine]


def together(*values):
    return lax.optimization_barrier(values)


def plane_join(mine, other):
    return sum_cores(mine, swap(other))


def sum_cores(mine, got):
    return [(mine[r].astype(F32) + got[r].astype(F32)).astype(BF16) for r in range(mine.shape[0])]


def sum_far(joined):
    n = lax.axis_size("ctx")
    pairs = [(c * 2 + p, (c ^ (1 + p)) * 2 + p) for c in range(n) for p in range(2)]
    return lax.ppermute(joined[3], ("ctx", "core"), pairs)


def sum_onward(joined, far):
    core = lax.axis_index("core")
    by1, by2 = (
        (joined[r].astype(F32) + jnp.where(core == 2 - r, far.astype(F32), 0.0)).astype(BF16) for r in (1, 2)
    )
    return [by1, by2]


def plane_send(joined):
    return [joined[0]] + [send(joined[r], r) for r in range(1, len(joined))]


def ordered(first, second, core):
    return jnp.where(core == 0, jnp.stack([first, second]), jnp.stack([second, first]))


def send_heads(parts):
    return [parts[0]] + [send(parts[r], r) for r in range(1, len(parts))]


def other_heads(got):
    return swap(jnp.stack([g[1] for g in got]))


def mask_info(codes, half, chip, core):
    tiles = codes.reshape(-1, half)
    first, last = tiles[:, :1], tiles[:, half - 1 :]
    every = codes.reshape(1, -1)

    def count(test):
        return jnp.sum(test.astype(jnp.int32), axis=1)

    low = count(every // DOC < first // DOC) // half
    ends = jnp.minimum(count(every // DOC <= last // DOC), count(every % DOC <= last % DOC))
    high = (ends + half - 1) // half
    info = jnp.concatenate([jnp.stack([chip, core]).astype(jnp.int32), low, high])
    return info, every


def body(
    block_in, cotangent, doc_ids, block_ids, gain_attn, w_query, w_key, w_value, w_out, gain_ffn, w_gate, w_up, w_down
):
    n, n_z = lax.axis_size("ctx"), lax.axis_size("z")
    chip, core = lax.axis_index("ctx"), lax.axis_index("core")
    piece, dim = block_in.shape[1], block_in.shape[2]
    half = piece // 2
    shard = w_query.shape[0]
    width = dim // (2 * n)
    down_rows = w_down.shape[0]
    cut = down_rows // n
    me = jnp.stack([chip, core]).astype(jnp.int32)

    def own_half(rows, which):
        return lax.dynamic_slice_in_dim(rows, which * half, half, axis=0)

    def both_rows(rows):
        return ordered(own_half(rows, core), swap(own_half(rows, 1 - core)), core)

    x_rows = both_rows(block_in[0])
    n_one, inv1 = normed(x_rows.astype(F32))
    one_own = n_one.astype(BF16)
    one_near = gather_near(one_own)
    first = after(me, one_own)

    def head_cols(which):
        at = (chip * 2 + which) * width
        return jnp.concatenate(
            [lax.dynamic_slice_in_dim(w, at, width, axis=1) for w in (w_query, w_key, w_value)], axis=1
        )

    def hidden_slices(which):
        return jnp.concatenate(
            [
                lax.dynamic_slice_in_dim(w, (2 * z + which) * down_rows + chip * cut, cut, axis=1)
                for w in (w_gate, w_up)
                for z in range(n_z)
            ],
            axis=1,
        )

    def scaled(w, gain):
        return (w.astype(F32) * gain.astype(F32)[:, None]).astype(BF16)

    def core_rows(mine, theirs):
        return ordered(mine, swap(theirs), core).reshape(2 * shard, -1)

    def over_z(mine, theirs):
        return lax.all_gather(core_rows(mine, theirs), "z", axis=0, tiled=True)

    g1, g2 = gain_attn.astype(F32)[:, None], gain_ffn.astype(F32)[:, None]
    if cut % 128 == 0:
        packed = after(me, one_own)
        w_qkv = core_rows(
            *pack(functools.partial(pack_qkv_kernel, width), "pack_qkv", packed, g1, (w_query, w_key, w_value), 4 * width)
        )
        packed = after(packed, w_qkv)
        w_qkv = lax.all_gather(w_qkv, "z", axis=0, tiled=True)
        hidden_pair = pack(
            functools.partial(pack_hidden_kernel, n_z, cut, down_rows),
            "pack_hidden",
            packed,
            g2,
            (w_gate, w_up),
            2 * n_z * cut,
        )
    else:
        w_qkv = over_z(scaled(head_cols(core), gain_attn), scaled(head_cols(1 - core), gain_attn))
        hidden_pair = scaled(hidden_slices(core), gain_ffn), scaled(hidden_slices(1 - core), gain_ffn)
    w_out_full = lax.all_gather(after(w_out, w_qkv), ("z", "core"), axis=0, tiled=True)
    cols = n_z * cut
    down_cut = lax.dynamic_slice_in_dim(w_down, chip * cut, cut, axis=0)
    if 2 * cols == dim:
        gu_cut = ordered(hidden_pair[0], swap(hidden_pair[1]), core).reshape(2 * shard, dim)
        w_ff = jnp.concatenate([gu_cut, down_cut], axis=0)
        w_ffs = [lax.all_gather(after(w_ff, w_out_full), "z", axis=0)]
    else:
        w_ffs = [over_z(*hidden_pair), lax.all_gather(down_cut, "z", axis=0, tiled=True)]

    code = doc_ids[0] * DOC + block_ids[0]
    code, cot_rows = after((code, cotangent[0]), hidden_pair)
    codes = jnp.stack([code] + [send(code, r) for r in range(1, n)])
    codes = ordered(codes, swap(codes), core)
    ids = [mask_info(codes[s], half, chip, core) for s in range(2)]
    infos, code_rows = [i[0] for i in ids], [i[1] for i in ids]
    cot_rows = both_rows(cot_rows)
    one_near, infos, cot_rows = together(one_near, infos, cot_rows)
    one = gather_cores(one_own, gather_far(one_near))
    one, cot_own = together(one, cot_rows)

    def to_owner(part):
        mine = lax.dynamic_slice_in_dim(part, core * shard, shard, axis=0)
        theirs = lax.dynamic_slice_in_dim(part, (1 - core) * shard, shard, axis=0)
        return mine, swap(theirs)

    cot_near = gather_near(cot_own)
    qkv0, *mixed0, lse0 = attend(one, 0, w_qkv, (infos[0], code_rows[0]), n)
    mixed0, cot_near, info1 = together(mixed0, cot_near, infos[1])
    got0 = send_heads(mixed0)
    cot_all = gather_far(cot_near)
    qkv1, *mixed1, lse1 = attend(one, 1, w_qkv, (info1, code_rows[1]), n)
    mixed1, got0, cot_all, go = together(mixed1, got0, cot_all, me)
    got1 = send_heads(mixed1)
    other0 = other_heads(got0)
    cots = gather_cores(cot_own, cot_all)
    att0, hidden0, norm0 = mix(go, got0, other0, x_rows, 0, w_out_full, n)
    norm0, got1, go = together(norm0, got1, me)
    near0 = gather_near(norm0)
    other1 = other_heads(got1)
    att1, hidden1, norm1 = mix(go, got1, other1, x_rows, 1, w_out_full, n)
    near0, norm1, cots = together(near0, norm1, cots)
    far0 = gather_far(near0)
    two0 = gather_cores(norm0, far0)
    two0, norm1, go = together(two0, norm1, me)

    two_got = [send(norm1, r) for r in range(1, n)]
    inner0, d_gu0, d_mine0, d_other0, o_mine0, o_other0 = feed(two0, cots, 0, w_ffs, cols, go, n)
    two_got, d_mine0, d_other0, o_other0 = together(two_got, d_mine0, d_other0, o_other0)
    two1 = gather_cores(norm1, two_got)
    joined0 = plane_join(d_mine0, d_other0)
    o_got0 = swap(o_other0)
    joined0, two1, go = together(joined0, two1, me)
    parts0 = plane_send(joined0)
    inner1, d_gu1, d_mine1, d_other1, o_mine1, o_other1 = feed(two1, cots, 1, w_ffs, cols, go, n)
    parts0, d_mine1, d_other1, o_got0, go = together(parts0, d_mine1, d_other1, o_got0, me)
    d_got, o_got1 = swap(d_other1), swap(o_other1)
    d_hidden0, e0, *d_mix0 = turn(go, parts0, cot_rows, 0, hidden0, w_out_full, width, n)
    d_got, d_mix0, d_mine1, o_mine0, o_mine1, o_got1 = together(d_got, d_mix0, d_mine1, o_mine0, o_mine1, o_got1)
    joined1 = sum_cores(d_mine1, d_got)

    def out_sum(r, *more):
        pairs = ((o_mine0, o_got0), (o_mine1, o_got1))
        sums = [mine[r].astype(F32) + got[r].astype(F32) for mine, got in pairs]
        for far in more:
            sums = [a + b for a, b in zip(sums, far)]
        return jnp.stack([a.astype(BF16) for a in sums])

    out_far = out_sum(n - 1)
    joined1, d_mix0, out_far, go = together(joined1, d_mix0, out_far, me)
    d_got0 = send_heads(d_mix0)
    if n == 4:
        pairs = [(c * 2 + p, (c ^ (1 + p)) * 2 + p) for c in range(n) for p in range(2)]
        out_far = lax.ppermute(out_far, ("ctx", "core"), pairs)
    parts1 = plane_send(joined1)
    raw_ff = feed_grads((two0, two1), cots, (inner0, inner1), (d_gu0, d_gu1), go, n, n_z)
    grads_ff = [lax.psum_scatter(g, "z", scatter_dimension=0, tiled=True) for g in raw_ff]
    parts1, d_got0, raw_ff, out_far = together(parts1, d_got0, raw_ff, out_far)
    d_other_heads0 = other_heads(d_got0)
    if n == 4:
        outs = [out_sum(0)]
        for r in range(1, 3):
            far = jnp.where(core == 2 - r, out_far.astype(F32), 0.0)
            outs.append(out_sum(r, [far[0], far[1]]))
    else:
        outs = [out_sum(r) for r in range(n - 1)] + [out_far]
    outs, d_other_heads0, info0 = together(outs, d_other_heads0, infos[0])

    out_parts = plane_send(outs)
    d_qkv0, a_mine0, a_other0 = attend_back(
        qkv0, w_qkv, lse0, mixed0, d_got0, d_other_heads0, (info0, code_rows[0]), n
    )
    out_parts, a_mine0, a_other0, go = together(out_parts, a_mine0, a_other0, me)
    a_got0 = swap(a_other0)
    d_hidden1, e1, *d_mix1 = turn(go, parts1, cot_rows, 1, hidden1, w_out_full, width, n)
    d_mix1, a_mine0, a_got0 = together(d_mix1, a_mine0, a_got0)
    d_got1 = send_heads(d_mix1)
    joined0 = sum_cores(a_mine0, a_got0)
    joined0, go = together(joined0, after(me, d_mix1))
    parts0 = plane_send(joined0)
    grads_wo = out_grads(go, (att0, att1), (e0, e1), width, n)
    grads_wo, d_got1 = together(grads_wo, d_got1)
    wo_shard = lax.psum_scatter(grads_wo, ("z", "core"), scatter_dimension=0, tiled=True)
    d_other_heads1 = other_heads(d_got1)
    info1, grads_ff, d_other_heads1 = together(infos[1], grads_ff, d_other_heads1)
    lanes = cut % 128 == 0
    if lanes:
        gu_part, dn_part = grads_ff[0][0, : 2 * shard], grads_ff[0][0, 2 * shard :]
        ff_own = jnp.concatenate([*to_owner(gu_part), dn_part], axis=0)
        ff_own, info1 = together(ff_own, info1)
        ff_packs = gather_near(ff_own)
    else:
        ff_own, ff_packs = None, []
    d_qkv1, a_mine1, a_other1 = attend_back(
        qkv1, w_qkv, lse1, mixed1, d_got1, d_other_heads1, (info1, code_rows[1]), n
    )
    raw_qkv = qkv_grads(me, one, (d_qkv0, d_qkv1), n)
    parts0, a_mine1, a_other1, ff_packs, wo_shard, _ = together(
        parts0, a_mine1, a_other1, ff_packs, wo_shard, raw_qkv
    )
    grad_qkv = lax.psum_scatter(raw_qkv, "z", scatter_dimension=0, tiled=True)
    a_got1 = swap(a_other1)
    if lanes:
        ff_packs = [ff_own] + gather_far(ff_packs)
        a_mine1, a_got1, ff_packs = together(a_mine1, a_got1, ff_packs)
    joined1 = sum_cores(a_mine1, a_got1)
    parts1 = plane_send(joined1)
    out_rows = jnp.stack([hidden0, hidden1])
    for part in out_parts:
        out_rows = out_rows + part.astype(F32)
    out_rows = out_rows.astype(BF16)
    in_rows = [
        d_hidden + back_normed(x_rows[s].astype(F32), sum(p.astype(F32) for p in parts))
        for s, (d_hidden, parts) in enumerate(((d_hidden0, parts0), (d_hidden1, parts1)))
    ]

    def own_rows(pair):
        mine = lax.dynamic_index_in_dim(pair, core, 0, keepdims=False)
        theirs = swap(lax.dynamic_index_in_dim(pair, 1 - core, 0, keepdims=False))
        return ordered(mine, theirs, core).reshape(1, piece, dim)

    block_out = own_rows(out_rows)
    input_grad = own_rows(jnp.stack(in_rows))

    if lanes:
        ff = w_gate.shape[1]
        raw = call(
            functools.partial(finish_kernel, n, shard, cut, down_rows),
            "finish",
            [shape_of(shard, ff, dtype=F32)] * 2
            + [shape_of(down_rows, dim, dtype=F32), shape_of(1, shard, dtype=F32)],
            [whole_spec(ff_own.shape)] * n + [whole_spec((shard, 1)), whole_spec((shard, ff)), whole_spec((shard, ff))],
            [whole_spec((shard, ff))] * 2 + [whole_spec((down_rows, dim)), whole_spec((1, shard))],
            estimate=cost(7),
        )(me, *ff_packs, g2, w_gate, w_up)
        grad_gate, grad_up, grad_down, grad_gain_ffn = raw
        both = jnp.concatenate([*to_owner(grad_qkv), wo_shard], axis=1)
        boths = [both] + [send(both, r) for r in range(1, n)]
        raw = call(
            functools.partial(finish_qkv_kernel, n, width),
            "finish_qkv",
            [shape_of(shard, dim, dtype=F32)] * 4 + [shape_of(1, shard, dtype=F32)],
            [whole_spec(both.shape)] * n + [whole_spec((shard, 1))] + [whole_spec((shard, dim))] * 3,
            [whole_spec((shard, dim))] * 4 + [whole_spec((1, shard))],
            estimate=cost(4),
        )(after(me, grad_gain_ffn, input_grad, block_out), *boths, g1, w_query, w_key, w_value)
        grad_q, grad_k, grad_v, grad_wo, grad_gain_attn = raw
        grad_gain_attn, grad_gain_ffn = grad_gain_attn.reshape(shard), grad_gain_ffn.reshape(shard)
    else:

        def over_ctx(part):
            both = ordered(*to_owner(part), core)
            return lax.all_gather(both, "ctx", axis=0).transpose(2, 0, 1, 3)

        qkv_shard = over_ctx(grad_qkv).reshape(shard, 2 * n, 3, width).astype(F32)
        raw_q, raw_k, raw_v = (qkv_shard[:, :, i].reshape(shard, dim) for i in range(3))
        gu_part, dn_part = grads_ff
        gu_shard = over_ctx(gu_part).reshape(shard, n, 2, 2, n_z, cut).astype(F32)
        raw_g, raw_u = (
            gu_shard[:, :, :, i].transpose(0, 3, 2, 1, 4).reshape(shard, -1) for i in range(2)
        )
        grad_down = lax.all_gather(dn_part, "ctx", axis=0, tiled=True).astype(F32)
        grad_wo = lax.psum(wo_shard, "ctx").astype(F32)

        def row_sum(pairs):
            return sum(jnp.sum(w.astype(F32) * g, axis=1) for w, g in pairs)

        grad_gain_attn = row_sum([(w_query, raw_q), (w_key, raw_k), (w_value, raw_v)])
        grad_gain_ffn = row_sum([(w_gate, raw_g), (w_up, raw_u)])
        grad_q, grad_k, grad_v, grad_gate, grad_up = raw_q * g1, raw_k * g1, raw_v * g1, raw_g * g2, raw_u * g2
    return (
        block_out,
        input_grad,
        grad_gain_attn,
        grad_q,
        grad_k,
        grad_v,
        grad_wo,
        grad_gain_ffn,
        grad_gate,
        grad_up,
        grad_down,
    )


def solution(mesh):
    n_ctx, n_fsdp = mesh.devices.shape
    inner = Mesh(mesh.devices.reshape(n_ctx, n_fsdp // 2, 2), ("ctx", "z", "core"))
    fsdp = ("z", "core")
    act, ids, vec, mat = P(fsdp, "ctx", None), P(fsdp, "ctx"), P(fsdp), P(fsdp, None)
    return jax.shard_map(
        body,
        mesh=inner,
        in_specs=(act, act, ids, ids, vec, mat, mat, mat, mat, vec, mat, mat, mat),
        out_specs=(act, act, vec, mat, mat, mat, mat, vec, mat, mat, mat),
        check_vma=False,
    )
```

```python
import functools

import jax
import jax.numpy as jnp
from jax import lax
from jax.experimental import pallas as pl
from jax.experimental.pallas import tpu as pltpu
from jax.sharding import Mesh
from jax.sharding import PartitionSpec as P

HEAD_DIM = 64
NORM_EPS = 1e-05
MASKED = -1e30
START_MAX = -1e29
SCALE = HEAD_DIM ** (-0.5)
DOC = 1 << 16
F32 = jnp.float32
BF16 = jnp.bfloat16
NT = (((1,), (1,)), ((), ()))
TN = (((0,), (0,)), ((), ()))


def mm(a, b):
    return jnp.dot(a, b, preferred_element_type=F32)


def mm_nt(a, b):
    return lax.dot_general(a, b, NT, preferred_element_type=F32)


def mm_tn(a, b):
    return lax.dot_general(a, b, TN, preferred_element_type=F32)


def cost(us):
    return pl.CostEstimate(flops=int(us * 1e9), bytes_accessed=1000, transcendentals=0)


def whole_spec(shape, **kw):
    return pl.BlockSpec(shape, lambda *_: (0,) * len(shape), **kw)


def pick_spec(shape, index):
    return pl.BlockSpec((1,) + shape, lambda *_: (index,) + (0,) * len(shape))


def any_spec():
    return pl.BlockSpec(memory_space=pl.ANY)


def call(kernel, name, out_shape, in_specs, out_specs, grid=(1,), scratch=(), estimate=None, prefetch=1):
    return pl.pallas_call(
        kernel,
        out_shape=out_shape,
        grid_spec=pltpu.PrefetchScalarGridSpec(
            num_scalar_prefetch=prefetch,
            grid=grid,
            in_specs=in_specs,
            out_specs=out_specs,
            scratch_shapes=list(scratch),
        ),
        cost_estimate=estimate,
        name=name,
    )


def shape_of(*dims, dtype=BF16):
    return jax.ShapeDtypeStruct(dims, dtype)


def head_stack(rows, heads):
    lane = lax.broadcasted_iota(jnp.int32, rows.shape, 1) // HEAD_DIM
    return jnp.concatenate(
        [jnp.where(lane == h, rows, jnp.zeros_like(rows)) for h in range(heads)], axis=0
    )


def query_tile(step, n, info):
    r, dp = step % n, step // n
    return r, dp, r * 2 + (dp ^ info[1])


def key_tile(a, n, info):
    r = (a // 2) ^ info[0]
    return ((a % 2) ^ info[1]) * n + r, r * 2 + a % 2


def query_bounds(code_row, q_ids, half, heads):
    high = code_row[:, pl.ds(pl.multiple_of(q_ids * half, half), half)]
    low = (high // DOC) * DOC
    return jnp.concatenate([low] * heads, axis=1), jnp.concatenate([high] * heads, axis=1)


def key_pair(first, last, turn, n, info, half, code_col, bounds):
    low, high = bounds
    for i in range(2):
        a = first + 2 * turn + i
        place, k_ids = key_tile(jnp.minimum(a, last - 1), n, info)
        keys = code_col[pl.ds(pl.multiple_of(k_ids * half, half), half), 0:1]
        if i:
            keys = jnp.where(a < last, keys, -1)
        yield pl.multiple_of(place * half, half), (keys >= low) & (keys <= high)


def attend_kernel(n, heads, half, info, *refs):
    blocks, (w, code_row), (qkv, *outs, lse), (v_t, code_col) = (
        refs[: 2 * n],
        refs[2 * n : 2 * n + 2],
        refs[2 * n + 2 : 3 * n + 4],
        refs[3 * n + 4 :],
    )
    width = heads * HEAD_DIM
    step = pl.program_id(0)

    @pl.when(step == 0)
    def _():
        for k in range(2 * n):
            qkv[k * half : (k + 1) * half, :] = mm(blocks[k][0], w[...]).astype(BF16)
        v_t[...] = qkv[:, 2 * width : 3 * width].T
        code_col[...] = jnp.broadcast_to(code_row[...], (8, code_row.shape[1])).T

    r, dp, q_ids = query_tile(step, n, info)
    q_rows = qkv[pl.ds(pl.multiple_of(step * half, half), half), 0:width] * jnp.asarray(SCALE, BF16)
    q_heads = head_stack(q_rows, heads)

    first, last = info[2 + q_ids], info[2 + 2 * n + q_ids]
    bounds = query_bounds(code_row, q_ids, half, heads)

    def one(turn, carry):
        run_max, run_sum, accs = carry
        new_max, tiles = run_max, []
        for pos, keys_ok in key_pair(first, last, turn, n, info, half, code_col, bounds):
            scores = mm_nt(qkv[pl.ds(pos, half), width : 2 * width], q_heads)
            scores = jnp.where(keys_ok, scores, MASKED)
            new_max = jnp.maximum(new_max, jnp.max(scores, axis=0, keepdims=True))
            tiles.append((pos, scores))
        factor = jnp.exp(run_max - new_max)
        new_sum = run_sum * factor
        new_accs = [accs[h] * factor[:, h * half : (h + 1) * half] for h in range(heads)]
        for pos, scores in tiles:
            weights = jnp.exp(scores - new_max)
            new_sum += jnp.sum(weights, axis=0, keepdims=True)
            weights = weights.astype(BF16)
            for h in range(heads):
                v_head = v_t[h * HEAD_DIM : (h + 1) * HEAD_DIM, pl.ds(pos, half)]
                new_accs[h] += mm(v_head, weights[:, h * half : (h + 1) * half])
        return new_max, new_sum, tuple(new_accs)

    start = (
        jnp.full((1, heads * half), START_MAX, F32),
        jnp.zeros((1, heads * half), F32),
        tuple(jnp.zeros((HEAD_DIM, half), F32) for _ in range(heads)),
    )
    run_max, run_sum, accs = lax.fori_loop(0, (last - first + 1) // 2, one, start)
    parts = [accs[h] / run_sum[:, h * half : (h + 1) * half] for h in range(heads)]
    mixed = jnp.concatenate(parts, axis=0).T.astype(BF16)
    for k in range(n):

        @pl.when(r == k)
        def _():
            outs[k][dp] = mixed

    logs = run_max + jnp.log(run_sum)
    at = pl.ds(pl.multiple_of(step * half, half), half)
    for h in range(heads):
        lse[h : h + 1, at] = logs[:, h * half : (h + 1) * half]


def attend(blocks, which, w_qkv, ids, n):
    info, code_row = ids
    half, dim = blocks[0].shape[1:]
    width = dim // (2 * n)
    heads = width // HEAD_DIM
    rows = 2 * n * half
    return call(
        functools.partial(attend_kernel, n, heads, half),
        "attend",
        [shape_of(rows, 3 * width)]
        + [shape_of(2, half, width)] * n
        + [shape_of(heads, rows, dtype=F32)],
        [pick_spec((half, dim), which)] * (2 * n) + [whole_spec((dim, 3 * width)), whole_spec((1, rows))],
        [whole_spec((rows, 3 * width))] + [whole_spec((2, half, width))] * n + [whole_spec((heads, rows))],
        grid=(2 * n,),
        scratch=[pltpu.VMEM((width, rows), BF16), pltpu.VMEM((rows, 8), jnp.int32)],
        estimate=cost(21),
    )(info, *blocks, w_qkv, code_row)


def attend_back_kernel(n, heads, half, info, *refs):
    qkv, w, lse, code_row = refs[:4]
    mixes, d_mixes, (d_other,) = refs[4 : 4 + n], refs[4 + n : 4 + 2 * n], refs[4 + 2 * n : 5 + 2 * n]
    out, part_mine, part_other, k_t, dk, dv, code_col, do_now, mix_now = refs[5 + 2 * n :]
    width = heads * HEAD_DIM
    step = pl.program_id(0)

    @pl.when(step == 0)
    def _():
        k_t[...] = qkv[:, width : 2 * width].T
        code_col[...] = jnp.broadcast_to(code_row[...], (8, code_row.shape[1])).T
        dk[...] = jnp.zeros_like(dk)
        dv[...] = jnp.zeros_like(dv)

    r, dp, q_ids = query_tile(step, n, info)
    rows = pl.ds(pl.multiple_of(step * half, half), half)
    q_heads = head_stack(qkv[rows, 0:width] * jnp.asarray(SCALE, BF16), heads)
    for k in range(n):

        @pl.when(r == k)
        def _():
            mix_now[...] = mixes[k][dp]

        @pl.when((r == k) & (dp == 0))
        def _():
            do_now[...] = d_mixes[k][0]

    @pl.when(dp == 1)
    def _():
        do_now[...] = d_other[r]

    do_rows = do_now[...]
    do_heads = head_stack(do_rows, heads)
    prod = (do_rows.astype(F32) * mix_now[...].astype(F32)).T
    delta = jnp.concatenate(
        [
            jnp.sum(prod[h * HEAD_DIM : (h + 1) * HEAD_DIM], axis=0, keepdims=True)
            for h in range(heads)
        ],
        axis=1,
    )
    logs = jnp.concatenate([lse[h : h + 1, rows] for h in range(heads)], axis=1)

    first, last = info[2 + q_ids], info[2 + 2 * n + q_ids]
    bounds = query_bounds(code_row, q_ids, half, heads)

    def one(turn, dqs):
        new, done = list(dqs), []
        for pos, keys_ok in key_pair(first, last, turn, n, info, half, code_col, bounds):
            keys = qkv[pl.ds(pos, half), width : 2 * width]
            values = qkv[pl.ds(pos, half), 2 * width : 3 * width]
            scores = mm_nt(keys, q_heads)
            probs = jnp.where(keys_ok, jnp.exp(scores - logs), 0.0)
            d_probs = mm_nt(values, do_heads)
            d_scores = (probs * (d_probs - delta)).astype(BF16)
            done.append((pos, mm(probs.astype(BF16), do_heads), mm(d_scores, q_heads)))
            for h in range(heads):
                k_head = k_t[h * HEAD_DIM : (h + 1) * HEAD_DIM, pl.ds(pos, half)]
                new[h] += mm(k_head, d_scores[:, h * half : (h + 1) * half])
        for pos, d_values, d_keys in done:
            dv[pl.ds(pos, half), :] += d_values
            dk[pl.ds(pos, half), :] += d_keys
        return tuple(new)

    dqs = lax.fori_loop(
        0,
        (last - first + 1) // 2,
        one,
        tuple(jnp.zeros((HEAD_DIM, half), F32) for _ in range(heads)),
    )
    out[rows, 0:width] = (jnp.concatenate(dqs, axis=0) * SCALE).T.astype(BF16)

    @pl.when(step == 2 * n - 1)
    def _():
        out[:, width : 2 * width] = dk[...].astype(BF16)
        out[:, 2 * width : 3 * width] = dv[...].astype(BF16)
        for k in range(n):
            part_mine[k] = mm_nt(out[k * half : (k + 1) * half, :], w[...]).astype(BF16)
            part_other[k] = mm_nt(out[(n + k) * half : (n + k + 1) * half, :], w[...]).astype(BF16)


def attend_back(qkv, w_qkv, lse, mixes, d_mixes, d_other, ids, n):
    info, code_row = ids
    rows, width3 = qkv.shape
    width, dim = width3 // 3, w_qkv.shape[0]
    heads = width // HEAD_DIM
    half = rows // (2 * n)
    tile = (2, half, width)
    return call(
        functools.partial(attend_back_kernel, n, heads, half),
        "attend_back",
        [shape_of(rows, width3), shape_of(n, half, dim), shape_of(n, half, dim)],
        [whole_spec((rows, width3)), whole_spec((dim, width3)), whole_spec((heads, rows)), whole_spec((1, rows))]
        + [whole_spec(tile)] * (2 * n)
        + [whole_spec((n, half, width))],
        [whole_spec((rows, width3)), whole_spec((n, half, dim)), whole_spec((n, half, dim))],
        grid=(2 * n,),
        scratch=[
            pltpu.VMEM((width, rows), BF16),
            pltpu.VMEM((rows, width), F32),
            pltpu.VMEM((rows, width), F32),
            pltpu.VMEM((rows, 8), jnp.int32),
            pltpu.VMEM((half, width), BF16),
            pltpu.VMEM((half, width), BF16),
        ],
        estimate=cost(26),
    )(info, qkv, w_qkv, lse, code_row, *mixes, *d_mixes, d_other)


def normed(rows):
    inv = lax.rsqrt(jnp.mean(rows * rows, axis=-1, keepdims=True) + NORM_EPS)
    return rows * inv, inv


def back_normed(rows, d_norm):
    norm, inv = normed(rows)
    return inv * (d_norm - norm * jnp.mean(d_norm * norm, axis=-1, keepdims=True))


def head_rows(info, j, width):
    return pl.ds(pl.multiple_of((j ^ (info[0] * 2 + info[1])) * width, width), width)


def chip_rows(info, r, width):
    return pl.ds(pl.multiple_of((r ^ info[0]) * 2 * width, 2 * width), 2 * width)


def mix_kernel(n, width, info, *refs):
    parts, (others, x, w), (att, hidden, norm) = refs[:n], refs[n : n + 3], refs[n + 3 :]
    total = x[0].astype(F32)
    for r in range(n):
        mine, other = parts[r][0], others[r]
        pair = jnp.concatenate([jnp.where(info[1] == 0, mine, other), jnp.where(info[1] == 0, other, mine)], axis=1)
        att[:, 2 * r * width : 2 * (r + 1) * width] = pair
        total += mm(pair, w[chip_rows(info, r, width), :])
    hidden[...] = total
    norm[...] = normed(total)[0].astype(BF16)


def mix(info, parts, others, x, which, w_out, n):
    half, width = parts[0].shape[1:]
    dim = w_out.shape[0]
    return call(
        functools.partial(mix_kernel, n, width),
        "mix",
        [shape_of(half, dim), shape_of(half, dim, dtype=F32), shape_of(half, dim)],
        [whole_spec((2, half, width))] * n
        + [whole_spec((n, half, width)), pick_spec((half, dim), which), whole_spec((dim, dim))],
        [whole_spec((half, dim))] * 3,
        estimate=cost(5),
    )(info, *parts, others, x, w_out)


def feed_kernel(n, half, cols, which, info, *refs):
    two, cots = refs[: 2 * n], refs[2 * n : 4 * n]
    inner_out, d_gu_out, d_mine, d_other, o_mine, o_other, a_buf, c_buf, w_gu, w_dn, sems = refs[-11:]
    w_ffs = refs[4 * n : -11]
    step = pl.program_id(0)
    slot = step % 2

    def copies(r, at):
        got = []
        for dp in range(2):
            rows = pl.ds(dp * half, half)
            got.append(pltpu.make_async_copy(two[dp * n + r], a_buf.at[at, rows], sems.at[at, dp]))
            got.append(pltpu.make_async_copy(cots[dp * n + r].at[which], c_buf.at[at, rows], sems.at[at, 2 + dp]))
        return got

    @pl.when(step == 0)
    def _():
        for c in copies(0, 0):
            c.start()
        if len(w_ffs) == 1:
            n_z = w_ffs[0].shape[0]
            gu_rows, dn_rows = w_gu.shape[0] // n_z, cols // n_z
            for z in range(n_z):
                w_gu[z * gu_rows : (z + 1) * gu_rows, :] = w_ffs[0][z, :gu_rows, :]
                w_dn[z * dn_rows : (z + 1) * dn_rows, :] = w_ffs[0][z, gu_rows:, :]
        else:
            w_gu[...], w_dn[...] = w_ffs[0][...], w_ffs[1][...]

    for r in range(1, n):

        @pl.when(step + 1 == r)
        def _():
            for c in copies(r, r % 2):
                c.start()

    for c in copies(0, slot):
        c.wait()
    rows, cot = a_buf[slot], c_buf[slot]
    gu = mm(rows, w_gu[...])
    d_inner = mm_nt(cot, w_dn[...])
    gate, upper = gu[:, :cols], gu[:, cols:]
    sigma = jax.nn.sigmoid(gate)
    silu_gate = gate * sigma
    inner = (silu_gate * upper).astype(BF16)
    d_gate = (d_inner * upper * sigma * (1.0 + gate * (1.0 - sigma))).astype(BF16)
    d_upper = (d_inner * silu_gate).astype(BF16)
    inner_out[...] = inner
    d_gu_out[:, :cols] = d_gate
    d_gu_out[:, cols:] = d_upper
    d_rows = (mm_nt(d_gate, w_gu[:, :cols]) + mm_nt(d_upper, w_gu[:, cols:])).astype(BF16)
    d_mine[0] = d_rows[:half]
    d_other[0] = d_rows[half:]
    o_rows = mm(inner, w_dn[...]).astype(BF16)
    o_mine[0] = o_rows[:half]
    o_other[0] = o_rows[half:]


def feed(two, cots, which, w_ffs, cols, info, n):
    half, dim = two[0].shape
    rows = 2 * n * half
    block = pl.BlockSpec((1, half, dim), lambda i, *_: (i, 0, 0))
    return call(
        functools.partial(feed_kernel, n, half, cols, which),
        "feed",
        [shape_of(rows, cols), shape_of(rows, 2 * cols)] + [shape_of(n, half, dim)] * 4,
        [any_spec()] * (4 * n) + [whole_spec(w.shape) for w in w_ffs],
        [
            pl.BlockSpec((2 * half, cols), lambda i, *_: (i, 0)),
            pl.BlockSpec((2 * half, 2 * cols), lambda i, *_: (i, 0)),
        ]
        + [block] * 4,
        grid=(n,),
        scratch=[
            pltpu.VMEM((2, 2 * half, dim), BF16),
            pltpu.VMEM((2, 2 * half, dim), BF16),
            pltpu.VMEM((dim, 2 * cols), BF16),
            pltpu.VMEM((cols, dim), BF16),
            pltpu.SemaphoreType.DMA((2, 4)),
        ],
        estimate=cost(20),
    )(info, *two, *cots, *w_ffs)


def feed_grads_kernel(n, n_z, half, info, *refs):
    two, cots = (refs[: 2 * n], refs[2 * n : 4 * n]), refs[4 * n : 6 * n]
    inners, d_gus = refs[6 * n : 6 * n + 2], refs[6 * n + 2 : 6 * n + 4]
    a_buf, c_buf, z_buf, g_buf, acc_gu, acc_dn, sems = refs[-7:]
    outs = refs[6 * n + 4 : -7]
    step = pl.program_id(0)
    slot = step % 2
    gu_rows, dn_rows = acc_gu.shape[0] // n_z, acc_dn.shape[0] // n_z

    def copies(t, at):
        s, r = t // n, t % n
        got = []
        for dp in range(2):
            rows = pl.ds(dp * half, half)
            got.append(pltpu.make_async_copy(two[s][dp * n + r], a_buf.at[at, rows], sems.at[at, dp]))
            got.append(pltpu.make_async_copy(cots[dp * n + r].at[s], c_buf.at[at, rows], sems.at[at, 2 + dp]))
        rows = pl.ds(2 * r * half, 2 * half)
        got.append(pltpu.make_async_copy(inners[s].at[rows], z_buf.at[at], sems.at[at, 4]))
        got.append(pltpu.make_async_copy(d_gus[s].at[rows], g_buf.at[at], sems.at[at, 5]))
        return got

    @pl.when(step == 0)
    def _():
        for c in copies(0, 0):
            c.start()
        acc_gu[...] = jnp.zeros_like(acc_gu)
        acc_dn[...] = jnp.zeros_like(acc_dn)

    for t in range(1, 2 * n):

        @pl.when(step + 1 == t)
        def _():
            for c in copies(t, t % 2):
                c.start()

    for c in copies(0, slot):
        c.wait()
    acc_gu[...] += mm_tn(a_buf[slot], g_buf[slot])
    acc_dn[...] += mm_tn(z_buf[slot], c_buf[slot])

    @pl.when(step == 2 * n - 1)
    def _():
        if len(outs) == 1:
            for z in range(n_z):
                outs[0][z, :gu_rows, :] = acc_gu[z * gu_rows : (z + 1) * gu_rows, :].astype(BF16)
                outs[0][z, gu_rows:, :] = acc_dn[z * dn_rows : (z + 1) * dn_rows, :].astype(BF16)
        else:
            outs[0][...], outs[1][...] = acc_gu[...].astype(BF16), acc_dn[...].astype(BF16)


def feed_grads(two, cots, inners, d_gus, info, n, n_z):
    half, dim = two[0][0].shape
    cols = inners[0].shape[1]
    shapes = [(n_z, (dim + cols) // n_z, dim)] if 2 * cols == dim else [(dim, 2 * cols), (cols, dim)]
    return call(
        functools.partial(feed_grads_kernel, n, n_z, half),
        "feed_grads",
        [shape_of(*shape) for shape in shapes],
        [any_spec()] * (6 * n + 4),
        [whole_spec(shape) for shape in shapes],
        grid=(2 * n,),
        scratch=[
            pltpu.VMEM((2, 2 * half, dim), BF16),
            pltpu.VMEM((2, 2 * half, dim), BF16),
            pltpu.VMEM((2, 2 * half, cols), BF16),
            pltpu.VMEM((2, 2 * half, 2 * cols), BF16),
            pltpu.VMEM((dim, 2 * cols), F32),
            pltpu.VMEM((cols, dim), F32),
            pltpu.SemaphoreType.DMA((2, 6)),
        ],
        estimate=cost(20),
    )(info, *two[0], *two[1], *cots, *inners, *d_gus)


def turn_kernel(n, width, info, *refs):
    parts, (cot, hidden, w), (d_hidden, e_out), outs = (
        refs[:n],
        refs[n : n + 3],
        refs[n + 3 : n + 5],
        refs[n + 5 :],
    )
    d_norm = parts[0][...].astype(F32)
    for r in range(1, n):
        d_norm += parts[r][...].astype(F32)
    total = cot[0].astype(F32) + back_normed(hidden[...], d_norm)
    d_hidden[...] = total
    e_rows = total.astype(BF16)
    e_out[...] = e_rows
    for r in range(n):
        pair = mm_nt(e_rows, w[chip_rows(info, r, width), :]).astype(BF16)
        outs[r][info[1]] = pair[:, :width]
        outs[r][1 - info[1]] = pair[:, width:]


def turn(info, parts, cot, which, hidden, w_out, width, n):
    half, dim = hidden.shape
    return call(
        functools.partial(turn_kernel, n, width),
        "turn",
        [shape_of(half, dim, dtype=F32), shape_of(half, dim)] + [shape_of(2, half, width)] * n,
        [whole_spec((half, dim))] * n
        + [pick_spec((half, dim), which), whole_spec((half, dim)), whole_spec((dim, dim))],
        [whole_spec((half, dim))] * 2 + [whole_spec((2, half, width))] * n,
        estimate=cost(6),
    )(info, *parts, cot, hidden, w_out)


def out_grads_kernel(n, width, info, att0, att1, e0, e1, out):
    for r in range(n):
        cols = slice(2 * r * width, 2 * (r + 1) * width)
        total = mm_tn(att0[:, cols], e0[...]) + mm_tn(att1[:, cols], e1[...])
        out[chip_rows(info, r, width), :] = total.astype(BF16)


def out_grads(info, atts, es, width, n):
    half, dim = es[0].shape
    return call(
        functools.partial(out_grads_kernel, n, width),
        "out_grads",
        shape_of(dim, dim),
        [whole_spec((half, dim))] * 4,
        whole_spec((dim, dim)),
        estimate=cost(5),
    )(info, *atts, *es)


def qkv_grads_kernel(n, half, info, *refs):
    blocks, (d0, d1, out) = refs[: 2 * n], refs[2 * n :]
    total = None
    for s, d_qkv in enumerate((d0, d1)):
        for k in range(2 * n):
            part = mm_tn(d_qkv[k * half : (k + 1) * half, :], blocks[k][s])
            total = part if total is None else total + part
    out[...] = total.T.astype(BF16)


def qkv_grads(info, blocks, d_qkvs, n):
    half, dim = blocks[0].shape[1:]
    rows, width3 = d_qkvs[0].shape
    return call(
        functools.partial(qkv_grads_kernel, n, half),
        "qkv_grads",
        shape_of(dim, width3),
        [whole_spec((2, half, dim))] * (2 * n) + [whole_spec((rows, width3))] * 2,
        whole_spec((dim, width3)),
        estimate=cost(0.2),
    )(info, *blocks, *d_qkvs)


def pack_qkv_kernel(width, info, gain, wq, wk, wv, mine, theirs):
    scale = gain[...]
    mine[...] = jnp.zeros_like(mine)
    theirs[...] = jnp.zeros_like(theirs)
    for out, flip in ((mine, 0), (theirs, 1)):
        at = (info[0] * 2 + (info[1] ^ flip)) * width
        for i, w in enumerate((wq, wk, wv)):
            rows = w[:, pl.ds(pl.multiple_of(at, width), width)].astype(F32)
            out[:, i * width : (i + 1) * width] = (rows * scale).astype(BF16)


def pack_hidden_kernel(n_z, cut, down_rows, info, gain, wg, wu, mine, theirs):
    scale = gain[...]
    for out, flip in ((mine, 0), (theirs, 1)):
        for i, w in enumerate((wg, wu)):
            for z in range(n_z):
                at = (2 * z + (info[1] ^ flip)) * down_rows + info[0] * cut
                rows = w[:, pl.ds(pl.multiple_of(at, cut), cut)].astype(F32)
                to = (i * n_z + z) * cut
                out[:, to : to + cut] = (rows * scale).astype(BF16)


def pack(kernel, name, info, gain, weights, cols):
    shard = gain.shape[0]
    return call(
        kernel,
        name,
        [shape_of(shard, cols)] * 2,
        [whole_spec(a.shape) for a in (gain, *weights)],
        [whole_spec((shard, cols))] * 2,
        estimate=cost(9),
    )(info, gain, *weights)


def finish_kernel(n, shard, cut, down_rows, info, *refs):
    parts, (gain, wg, wu), (gg, gu, gd, gain_out) = refs[:n], refs[n : n + 3], refs[n + 3 :]
    chip, core = info[0], info[1]
    scale = gain[...]
    half = wg.shape[1] // (2 * n)
    total = jnp.zeros((shard, 1), F32)
    for r in range(n):
        gd[pl.ds(pl.multiple_of((chip ^ r) * cut, cut), cut), :] = parts[r][2 * shard : 2 * shard + cut, :].astype(F32)
        for q in range(2):
            rows = slice(q * shard, (q + 1) * shard)
            for z in range(half // cut):
                at = (2 * z + (core ^ q)) * down_rows + (chip ^ r) * cut
                at = pl.ds(pl.multiple_of(at, cut), cut)
                raw = parts[r][rows, z * cut : (z + 1) * cut].astype(F32)
                total += jnp.sum(raw * wg[:, at].astype(F32), axis=1, keepdims=True)
                gg[:, at] = raw * scale
                raw = parts[r][rows, half + z * cut : half + (z + 1) * cut].astype(F32)
                total += jnp.sum(raw * wu[:, at].astype(F32), axis=1, keepdims=True)
                gu[:, at] = raw * scale
    gain_out[...] = jnp.broadcast_to(total, (shard, 128)).T[0:1, :]


def finish_qkv_kernel(n, width, info, *refs):
    parts, (gain, *ws), (*grads, go, gain_out) = refs[:n], refs[n : n + 4], refs[n + 4 :]
    out = parts[0][:, 6 * width :].astype(F32)
    for r in range(1, n):
        out += parts[r][:, 6 * width :].astype(F32)
    go[...] = out
    scale = gain[...]
    total = jnp.zeros(scale.shape, F32)
    for r in range(n):
        for q in range(2):
            at = head_rows(info, r * 2 + q, width)
            for i in range(3):
                raw = parts[r][:, (3 * q + i) * width : (3 * q + i + 1) * width].astype(F32)
                total += jnp.sum(raw * ws[i][:, at].astype(F32), axis=1, keepdims=True)
                grads[i][:, at] = raw * scale
    gain_out[...] = jnp.broadcast_to(total, (scale.shape[0], 128)).T[0:1, :]


def send(value, step):
    count = lax.axis_size("ctx")
    return lax.ppermute(value, "ctx", [(i, i ^ step) for i in range(count)])


def swap(value):
    return lax.ppermute(value, "core", [(0, 1), (1, 0)])


def after(value, *others):
    return lax.optimization_barrier((value,) + others)[0]


def gather_near(own):
    n = lax.axis_size("ctx")
    return [send(own, r) for r in range(1, 3 if n == 4 else n)]


def onward_of(near):
    return jnp.where(lax.axis_index("core") == 0, near[1], near[0])


def gather_far(near):
    n = lax.axis_size("ctx")
    if n != 4:
        return near
    onward = onward_of(near)
    pairs = [(c * 2 + p, (c ^ (1 + p)) * 2 + p) for c in range(n) for p in range(2)]
    return near + [lax.ppermute(onward, ("ctx", "core"), pairs)]


def gather_cores(own, others):
    mine = [own] + others
    return mine + [swap(block) for block in mine]


def together(*values):
    return lax.optimization_barrier(values)


def plane_join(mine, other):
    return sum_cores(mine, swap(other))


def sum_cores(mine, got):
    return [(mine[r].astype(F32) + got[r].astype(F32)).astype(BF16) for r in range(mine.shape[0])]


def sum_far(joined):
    n = lax.axis_size("ctx")
    pairs = [(c * 2 + p, (c ^ (1 + p)) * 2 + p) for c in range(n) for p in range(2)]
    return lax.ppermute(joined[3], ("ctx", "core"), pairs)


def sum_onward(joined, far):
    core = lax.axis_index("core")
    by1, by2 = (
        (joined[r].astype(F32) + jnp.where(core == 2 - r, far.astype(F32), 0.0)).astype(BF16) for r in (1, 2)
    )
    return [by1, by2]


def plane_send(joined):
    return [joined[0]] + [send(joined[r], r) for r in range(1, len(joined))]


def ordered(first, second, core):
    return jnp.where(core == 0, jnp.stack([first, second]), jnp.stack([second, first]))


def send_heads(parts):
    return [parts[0]] + [send(parts[r], r) for r in range(1, len(parts))]


def other_heads(got):
    return swap(jnp.stack([g[1] for g in got]))


def mask_info(codes, half, chip, core):
    tiles = codes.reshape(-1, half)
    first, last = tiles[:, :1], tiles[:, half - 1 :]
    every = codes.reshape(1, -1)

    def count(test):
        return jnp.sum(test.astype(jnp.int32), axis=1)

    low = count(every // DOC < first // DOC) // half
    ends = jnp.minimum(count(every // DOC <= last // DOC), count(every % DOC <= last % DOC))
    high = (ends + half - 1) // half
    info = jnp.concatenate([jnp.stack([chip, core]).astype(jnp.int32), low, high])
    return info, every


def body(
    block_in, cotangent, doc_ids, block_ids, gain_attn, w_query, w_key, w_value, w_out, gain_ffn, w_gate, w_up, w_down
):
    n, n_z = lax.axis_size("ctx"), lax.axis_size("z")
    chip, core = lax.axis_index("ctx"), lax.axis_index("core")
    piece, dim = block_in.shape[1], block_in.shape[2]
    half = piece // 2
    shard = w_query.shape[0]
    width = dim // (2 * n)
    down_rows = w_down.shape[0]
    cut = down_rows // n
    me = jnp.stack([chip, core]).astype(jnp.int32)

    def own_half(rows, which):
        return lax.dynamic_slice_in_dim(rows, which * half, half, axis=0)

    def both_rows(rows):
        return ordered(own_half(rows, core), swap(own_half(rows, 1 - core)), core)

    x_rows = both_rows(block_in[0])
    n_one, inv1 = normed(x_rows.astype(F32))
    one_own = n_one.astype(BF16)
    one_near = gather_near(one_own)
    first = after(me, one_own)

    def head_cols(which):
        at = (chip * 2 + which) * width
        return jnp.concatenate(
            [lax.dynamic_slice_in_dim(w, at, width, axis=1) for w in (w_query, w_key, w_value)], axis=1
        )

    def hidden_slices(which):
        return jnp.concatenate(
            [
                lax.dynamic_slice_in_dim(w, (2 * z + which) * down_rows + chip * cut, cut, axis=1)
                for w in (w_gate, w_up)
                for z in range(n_z)
            ],
            axis=1,
        )

    def scaled(w, gain):
        return (w.astype(F32) * gain.astype(F32)[:, None]).astype(BF16)

    def core_rows(mine, theirs):
        return ordered(mine, swap(theirs), core).reshape(2 * shard, -1)

    def over_z(mine, theirs):
        return lax.all_gather(core_rows(mine, theirs), "z", axis=0, tiled=True)

    g1, g2 = gain_attn.astype(F32)[:, None], gain_ffn.astype(F32)[:, None]
    if cut % 128 == 0:
        packed = after(me, one_own)
        w_qkv = core_rows(
            *pack(functools.partial(pack_qkv_kernel, width), "pack_qkv", packed, g1, (w_query, w_key, w_value), 4 * width)
        )
        packed = after(packed, w_qkv)
        w_qkv = lax.all_gather(w_qkv, "z", axis=0, tiled=True)
        hidden_pair = pack(
            functools.partial(pack_hidden_kernel, n_z, cut, down_rows),
            "pack_hidden",
            packed,
            g2,
            (w_gate, w_up),
            2 * n_z * cut,
        )
    else:
        w_qkv = over_z(scaled(head_cols(core), gain_attn), scaled(head_cols(1 - core), gain_attn))
        hidden_pair = scaled(hidden_slices(core), gain_ffn), scaled(hidden_slices(1 - core), gain_ffn)
    w_out_full = lax.all_gather(after(w_out, w_qkv), ("z", "core"), axis=0, tiled=True)
    cols = n_z * cut
    down_cut = lax.dynamic_slice_in_dim(w_down, chip * cut, cut, axis=0)
    if 2 * cols == dim:
        gu_cut = ordered(hidden_pair[0], swap(hidden_pair[1]), core).reshape(2 * shard, dim)
        w_ff = jnp.concatenate([gu_cut, down_cut], axis=0)
        w_ffs = [lax.all_gather(after(w_ff, w_out_full), "z", axis=0)]
    else:
        w_ffs = [over_z(*hidden_pair), lax.all_gather(down_cut, "z", axis=0, tiled=True)]

    code = doc_ids[0] * DOC + block_ids[0]
    code, cot_rows = after((code, cotangent[0]), hidden_pair)
    codes = jnp.stack([code] + [send(code, r) for r in range(1, n)])
    codes = ordered(codes, swap(codes), core)
    ids = [mask_info(codes[s], half, chip, core) for s in range(2)]
    infos, code_rows = [i[0] for i in ids], [i[1] for i in ids]
    cot_rows = both_rows(cot_rows)
    one_near, infos, cot_rows = together(one_near, infos, cot_rows)
    one = gather_cores(one_own, gather_far(one_near))
    one, cot_own = together(one, cot_rows)

    def to_owner(part):
        mine = lax.dynamic_slice_in_dim(part, core * shard, shard, axis=0)
        theirs = lax.dynamic_slice_in_dim(part, (1 - core) * shard, shard, axis=0)
        return mine, swap(theirs)

    cot_near = gather_near(cot_own)
    qkv0, *mixed0, lse0 = attend(one, 0, w_qkv, (infos[0], code_rows[0]), n)
    mixed0, cot_near, info1 = together(mixed0, cot_near, infos[1])
    got0 = send_heads(mixed0)
    cot_all = gather_far(cot_near)
    qkv1, *mixed1, lse1 = attend(one, 1, w_qkv, (info1, code_rows[1]), n)
    mixed1, got0, cot_all, go = together(mixed1, got0, cot_all, me)
    got1 = send_heads(mixed1)
    other0 = other_heads(got0)
    cots = gather_cores(cot_own, cot_all)
    att0, hidden0, norm0 = mix(go, got0, other0, x_rows, 0, w_out_full, n)
    norm0, got1, go = together(norm0, got1, me)
    near0 = gather_near(norm0)
    other1 = other_heads(got1)
    att1, hidden1, norm1 = mix(go, got1, other1, x_rows, 1, w_out_full, n)
    near0, norm1, cots = together(near0, norm1, cots)
    far0 = gather_far(near0)
    two0 = gather_cores(norm0, far0)
    two0, norm1, go = together(two0, norm1, me)

    two_got = [send(norm1, r) for r in range(1, n)]
    inner0, d_gu0, d_mine0, d_other0, o_mine0, o_other0 = feed(two0, cots, 0, w_ffs, cols, go, n)
    two_got, d_mine0, d_other0, o_other0 = together(two_got, d_mine0, d_other0, o_other0)
    two1 = gather_cores(norm1, two_got)
    joined0 = plane_join(d_mine0, d_other0)
    o_got0 = swap(o_other0)
    joined0, two1, go = together(joined0, two1, me)
    parts0 = plane_send(joined0)
    inner1, d_gu1, d_mine1, d_other1, o_mine1, o_other1 = feed(two1, cots, 1, w_ffs, cols, go, n)
    parts0, d_mine1, d_other1, o_got0, go = together(parts0, d_mine1, d_other1, o_got0, me)
    d_got, o_got1 = swap(d_other1), swap(o_other1)
    d_hidden0, e0, *d_mix0 = turn(go, parts0, cot_rows, 0, hidden0, w_out_full, width, n)
    d_got, d_mix0, d_mine1, o_mine0, o_mine1, o_got1 = together(d_got, d_mix0, d_mine1, o_mine0, o_mine1, o_got1)
    joined1 = sum_cores(d_mine1, d_got)

    def out_sum(r, *more):
        pairs = ((o_mine0, o_got0), (o_mine1, o_got1))
        sums = [mine[r].astype(F32) + got[r].astype(F32) for mine, got in pairs]
        for far in more:
            sums = [a + b for a, b in zip(sums, far)]
        return jnp.stack([a.astype(BF16) for a in sums])

    out_far = out_sum(n - 1)
    joined1, d_mix0, out_far, go = together(joined1, d_mix0, out_far, me)
    d_got0 = send_heads(d_mix0)
    if n == 4:
        pairs = [(c * 2 + p, (c ^ (1 + p)) * 2 + p) for c in range(n) for p in range(2)]
        out_far = lax.ppermute(out_far, ("ctx", "core"), pairs)
    parts1 = plane_send(joined1)
    raw_ff = feed_grads((two0, two1), cots, (inner0, inner1), (d_gu0, d_gu1), go, n, n_z)
    grads_ff = [lax.psum_scatter(g, "z", scatter_dimension=0, tiled=True) for g in raw_ff]
    parts1, d_got0, raw_ff, out_far = together(parts1, d_got0, raw_ff, out_far)
    d_other_heads0 = other_heads(d_got0)
    if n == 4:
        outs = [out_sum(0)]
        for r in range(1, 3):
            far = jnp.where(core == 2 - r, out_far.astype(F32), 0.0)
            outs.append(out_sum(r, [far[0], far[1]]))
    else:
        outs = [out_sum(r) for r in range(n - 1)] + [out_far]
    outs, d_other_heads0, info0 = together(outs, d_other_heads0, infos[0])

    out_parts = plane_send(outs)
    d_qkv0, a_mine0, a_other0 = attend_back(
        qkv0, w_qkv, lse0, mixed0, d_got0, d_other_heads0, (info0, code_rows[0]), n
    )
    out_parts, a_mine0, a_other0, go = together(out_parts, a_mine0, a_other0, me)
    a_got0 = swap(a_other0)
    d_hidden1, e1, *d_mix1 = turn(go, parts1, cot_rows, 1, hidden1, w_out_full, width, n)
    d_mix1, a_mine0, a_got0 = together(d_mix1, a_mine0, a_got0)
    d_got1 = send_heads(d_mix1)
    joined0 = sum_cores(a_mine0, a_got0)
    joined0, go = together(joined0, after(me, d_mix1))
    parts0 = plane_send(joined0)
    grads_wo = out_grads(go, (att0, att1), (e0, e1), width, n)
    grads_wo, d_got1 = together(grads_wo, d_got1)
    wo_shard = lax.psum_scatter(grads_wo, ("z", "core"), scatter_dimension=0, tiled=True)
    d_other_heads1 = other_heads(d_got1)
    info1, grads_ff, d_other_heads1 = together(infos[1], grads_ff, d_other_heads1)
    lanes = cut % 128 == 0
    if lanes:
        gu_part, dn_part = grads_ff[0][0, : 2 * shard], grads_ff[0][0, 2 * shard :]
        ff_own = jnp.concatenate([*to_owner(gu_part), dn_part], axis=0)
        ff_own, info1 = together(ff_own, info1)
        ff_packs = gather_near(ff_own)
    else:
        ff_own, ff_packs = None, []
    d_qkv1, a_mine1, a_other1 = attend_back(
        qkv1, w_qkv, lse1, mixed1, d_got1, d_other_heads1, (info1, code_rows[1]), n
    )
    raw_qkv = qkv_grads(me, one, (d_qkv0, d_qkv1), n)
    parts0, a_mine1, a_other1, ff_packs, wo_shard, _ = together(
        parts0, a_mine1, a_other1, ff_packs, wo_shard, raw_qkv
    )
    grad_qkv = lax.psum_scatter(raw_qkv, "z", scatter_dimension=0, tiled=True)
    a_got1 = swap(a_other1)
    if lanes:
        ff_packs = [ff_own] + gather_far(ff_packs)
    joined1 = sum_cores(a_mine1, a_got1)
    if lanes:
        joined1, ff_packs = together(joined1, ff_packs)
    parts1 = plane_send(joined1)
    out_rows = jnp.stack([hidden0, hidden1])
    for part in out_parts:
        out_rows = out_rows + part.astype(F32)
    out_rows = out_rows.astype(BF16)
    if lanes:
        both = jnp.concatenate([*to_owner(grad_qkv), wo_shard], axis=1)
        parts1 = after(parts1, both)
        boths = [both] + [send(both, r) for r in range(1, n)]
    in_rows = [
        d_hidden + back_normed(x_rows[s].astype(F32), sum(p.astype(F32) for p in parts))
        for s, (d_hidden, parts) in enumerate(((d_hidden0, parts0), (d_hidden1, parts1)))
    ]

    def own_rows(pair):
        mine = lax.dynamic_index_in_dim(pair, core, 0, keepdims=False)
        theirs = swap(lax.dynamic_index_in_dim(pair, 1 - core, 0, keepdims=False))
        return ordered(mine, theirs, core).reshape(1, piece, dim)

    block_out = own_rows(out_rows)
    input_grad = own_rows(jnp.stack(in_rows))

    if lanes:
        ff = w_gate.shape[1]
        raw = call(
            functools.partial(finish_kernel, n, shard, cut, down_rows),
            "finish",
            [shape_of(shard, ff, dtype=F32)] * 2
            + [shape_of(down_rows, dim, dtype=F32), shape_of(1, shard, dtype=F32)],
            [whole_spec(ff_own.shape)] * n + [whole_spec((shard, 1)), whole_spec((shard, ff)), whole_spec((shard, ff))],
            [whole_spec((shard, ff))] * 2 + [whole_spec((down_rows, dim)), whole_spec((1, shard))],
            estimate=cost(7),
        )(me, *ff_packs, g2, w_gate, w_up)
        grad_gate, grad_up, grad_down, grad_gain_ffn = raw
        raw = call(
            functools.partial(finish_qkv_kernel, n, width),
            "finish_qkv",
            [shape_of(shard, dim, dtype=F32)] * 4 + [shape_of(1, shard, dtype=F32)],
            [whole_spec(both.shape)] * n + [whole_spec((shard, 1))] + [whole_spec((shard, dim))] * 3,
            [whole_spec((shard, dim))] * 4 + [whole_spec((1, shard))],
            estimate=cost(4),
        )(after(me, grad_gain_ffn, input_grad, block_out), *boths, g1, w_query, w_key, w_value)
        grad_q, grad_k, grad_v, grad_wo, grad_gain_attn = raw
        grad_gain_attn, grad_gain_ffn = grad_gain_attn.reshape(shard), grad_gain_ffn.reshape(shard)
    else:

        def over_ctx(part):
            both = ordered(*to_owner(part), core)
            return lax.all_gather(both, "ctx", axis=0).transpose(2, 0, 1, 3)

        qkv_shard = over_ctx(grad_qkv).reshape(shard, 2 * n, 3, width).astype(F32)
        raw_q, raw_k, raw_v = (qkv_shard[:, :, i].reshape(shard, dim) for i in range(3))
        gu_part, dn_part = grads_ff
        gu_shard = over_ctx(gu_part).reshape(shard, n, 2, 2, n_z, cut).astype(F32)
        raw_g, raw_u = (
            gu_shard[:, :, :, i].transpose(0, 3, 2, 1, 4).reshape(shard, -1) for i in range(2)
        )
        grad_down = lax.all_gather(dn_part, "ctx", axis=0, tiled=True).astype(F32)
        grad_wo = lax.psum(wo_shard, "ctx").astype(F32)

        def row_sum(pairs):
            return sum(jnp.sum(w.astype(F32) * g, axis=1) for w, g in pairs)

        grad_gain_attn = row_sum([(w_query, raw_q), (w_key, raw_k), (w_value, raw_v)])
        grad_gain_ffn = row_sum([(w_gate, raw_g), (w_up, raw_u)])
        grad_q, grad_k, grad_v, grad_gate, grad_up = raw_q * g1, raw_k * g1, raw_v * g1, raw_g * g2, raw_u * g2
    return (
        block_out,
        input_grad,
        grad_gain_attn,
        grad_q,
        grad_k,
        grad_v,
        grad_wo,
        grad_gain_ffn,
        grad_gate,
        grad_up,
        grad_down,
    )


def solution(mesh):
    n_ctx, n_fsdp = mesh.devices.shape
    inner = Mesh(mesh.devices.reshape(n_ctx, n_fsdp // 2, 2), ("ctx", "z", "core"))
    fsdp = ("z", "core")
    act, ids, vec, mat = P(fsdp, "ctx", None), P(fsdp, "ctx"), P(fsdp), P(fsdp, None)
    return jax.shard_map(
        body,
        mesh=inner,
        in_specs=(act, act, ids, ids, vec, mat, mat, mat, mat, vec, mat, mat, mat),
        out_specs=(act, act, vec, mat, mat, mat, mat, vec, mat, mat, mat),
        check_vma=False,
    )
```

```python
import functools

import jax
import jax.numpy as jnp
from jax import lax
from jax.experimental import pallas as pl
from jax.experimental.pallas import tpu as pltpu
from jax.sharding import Mesh
from jax.sharding import PartitionSpec as P

HEAD_DIM = 64
NORM_EPS = 1e-05
MASKED = -1e30
START_MAX = -1e29
SCALE = HEAD_DIM ** (-0.5)
DOC = 1 << 16
F32 = jnp.float32
BF16 = jnp.bfloat16
NT = (((1,), (1,)), ((), ()))
TN = (((0,), (0,)), ((), ()))


def mm(a, b):
    return jnp.dot(a, b, preferred_element_type=F32)


def mm_nt(a, b):
    return lax.dot_general(a, b, NT, preferred_element_type=F32)


def mm_tn(a, b):
    return lax.dot_general(a, b, TN, preferred_element_type=F32)


def cost(us):
    return pl.CostEstimate(flops=int(us * 1e9), bytes_accessed=1000, transcendentals=0)


def whole_spec(shape, **kw):
    return pl.BlockSpec(shape, lambda *_: (0,) * len(shape), **kw)


def pick_spec(shape, index):
    return pl.BlockSpec((1,) + shape, lambda *_: (index,) + (0,) * len(shape))


def any_spec():
    return pl.BlockSpec(memory_space=pl.ANY)


def call(kernel, name, out_shape, in_specs, out_specs, grid=(1,), scratch=(), estimate=None, prefetch=1):
    return pl.pallas_call(
        kernel,
        out_shape=out_shape,
        grid_spec=pltpu.PrefetchScalarGridSpec(
            num_scalar_prefetch=prefetch,
            grid=grid,
            in_specs=in_specs,
            out_specs=out_specs,
            scratch_shapes=list(scratch),
        ),
        cost_estimate=estimate,
        name=name,
    )


def shape_of(*dims, dtype=BF16):
    return jax.ShapeDtypeStruct(dims, dtype)


def head_stack(rows, heads):
    lane = lax.broadcasted_iota(jnp.int32, rows.shape, 1) // HEAD_DIM
    return jnp.concatenate(
        [jnp.where(lane == h, rows, jnp.zeros_like(rows)) for h in range(heads)], axis=0
    )


def query_tile(step, n, info):
    r, dp = step % n, step // n
    return r, dp, r * 2 + (dp ^ info[1])


def key_tile(a, n, info):
    r = (a // 2) ^ info[0]
    return ((a % 2) ^ info[1]) * n + r, r * 2 + a % 2


def query_bounds(code_row, q_ids, half, heads):
    high = code_row[:, pl.ds(pl.multiple_of(q_ids * half, half), half)]
    low = (high // DOC) * DOC
    return jnp.concatenate([low] * heads, axis=1), jnp.concatenate([high] * heads, axis=1)


def key_pair(first, last, turn, n, info, half, code_col, bounds):
    low, high = bounds
    for i in range(2):
        a = first + 2 * turn + i
        place, k_ids = key_tile(jnp.minimum(a, last - 1), n, info)
        keys = code_col[pl.ds(pl.multiple_of(k_ids * half, half), half), 0:1]
        if i:
            keys = jnp.where(a < last, keys, -1)
        yield pl.multiple_of(place * half, half), (keys >= low) & (keys <= high)


def attend_kernel(n, heads, half, info, *refs):
    blocks, (w, code_row), (qkv, *outs, lse), (v_t, code_col) = (
        refs[: 2 * n],
        refs[2 * n : 2 * n + 2],
        refs[2 * n + 2 : 3 * n + 4],
        refs[3 * n + 4 :],
    )
    width = heads * HEAD_DIM
    step = pl.program_id(0)

    @pl.when(step == 0)
    def _():
        for k in range(2 * n):
            qkv[k * half : (k + 1) * half, :] = mm(blocks[k][0], w[...]).astype(BF16)
        v_t[...] = qkv[:, 2 * width : 3 * width].T
        code_col[...] = jnp.broadcast_to(code_row[...], (8, code_row.shape[1])).T

    r, dp, q_ids = query_tile(step, n, info)
    q_rows = qkv[pl.ds(pl.multiple_of(step * half, half), half), 0:width] * jnp.asarray(SCALE, BF16)
    q_heads = head_stack(q_rows, heads)

    first, last = info[2 + q_ids], info[2 + 2 * n + q_ids]
    bounds = query_bounds(code_row, q_ids, half, heads)

    def one(turn, carry):
        run_max, run_sum, accs = carry
        new_max, tiles = run_max, []
        for pos, keys_ok in key_pair(first, last, turn, n, info, half, code_col, bounds):
            scores = mm_nt(qkv[pl.ds(pos, half), width : 2 * width], q_heads)
            scores = jnp.where(keys_ok, scores, MASKED)
            new_max = jnp.maximum(new_max, jnp.max(scores, axis=0, keepdims=True))
            tiles.append((pos, scores))
        factor = jnp.exp(run_max - new_max)
        new_sum = run_sum * factor
        new_accs = [accs[h] * factor[:, h * half : (h + 1) * half] for h in range(heads)]
        for pos, scores in tiles:
            weights = jnp.exp(scores - new_max)
            new_sum += jnp.sum(weights, axis=0, keepdims=True)
            weights = weights.astype(BF16)
            for h in range(heads):
                v_head = v_t[h * HEAD_DIM : (h + 1) * HEAD_DIM, pl.ds(pos, half)]
                new_accs[h] += mm(v_head, weights[:, h * half : (h + 1) * half])
        return new_max, new_sum, tuple(new_accs)

    start = (
        jnp.full((1, heads * half), START_MAX, F32),
        jnp.zeros((1, heads * half), F32),
        tuple(jnp.zeros((HEAD_DIM, half), F32) for _ in range(heads)),
    )
    run_max, run_sum, accs = lax.fori_loop(0, (last - first + 1) // 2, one, start)
    parts = [accs[h] / run_sum[:, h * half : (h + 1) * half] for h in range(heads)]
    mixed = jnp.concatenate(parts, axis=0).T.astype(BF16)
    for k in range(n):

        @pl.when(r == k)
        def _():
            outs[k][dp] = mixed

    logs = run_max + jnp.log(run_sum)
    at = pl.ds(pl.multiple_of(step * half, half), half)
    for h in range(heads):
        lse[h : h + 1, at] = logs[:, h * half : (h + 1) * half]


def attend(blocks, which, w_qkv, ids, n):
    info, code_row = ids
    half, dim = blocks[0].shape[1:]
    width = dim // (2 * n)
    heads = width // HEAD_DIM
    rows = 2 * n * half
    return call(
        functools.partial(attend_kernel, n, heads, half),
        "attend",
        [shape_of(rows, 3 * width)]
        + [shape_of(2, half, width)] * n
        + [shape_of(heads, rows, dtype=F32)],
        [pick_spec((half, dim), which)] * (2 * n) + [whole_spec((dim, 3 * width)), whole_spec((1, rows))],
        [whole_spec((rows, 3 * width))] + [whole_spec((2, half, width))] * n + [whole_spec((heads, rows))],
        grid=(2 * n,),
        scratch=[pltpu.VMEM((width, rows), BF16), pltpu.VMEM((rows, 8), jnp.int32)],
        estimate=cost(21),
    )(info, *blocks, w_qkv, code_row)


def attend_back_kernel(n, heads, half, info, *refs):
    qkv, w, lse, code_row = refs[:4]
    mixes, d_mixes, (d_other,) = refs[4 : 4 + n], refs[4 + n : 4 + 2 * n], refs[4 + 2 * n : 5 + 2 * n]
    out, part_mine, part_other, k_t, dk, dv, code_col, do_now, mix_now = refs[5 + 2 * n :]
    width = heads * HEAD_DIM
    step = pl.program_id(0)

    @pl.when(step == 0)
    def _():
        k_t[...] = qkv[:, width : 2 * width].T
        code_col[...] = jnp.broadcast_to(code_row[...], (8, code_row.shape[1])).T
        dk[...] = jnp.zeros_like(dk)
        dv[...] = jnp.zeros_like(dv)

    r, dp, q_ids = query_tile(step, n, info)
    rows = pl.ds(pl.multiple_of(step * half, half), half)
    q_heads = head_stack(qkv[rows, 0:width] * jnp.asarray(SCALE, BF16), heads)
    for k in range(n):

        @pl.when(r == k)
        def _():
            mix_now[...] = mixes[k][dp]

        @pl.when((r == k) & (dp == 0))
        def _():
            do_now[...] = d_mixes[k][0]

    @pl.when(dp == 1)
    def _():
        do_now[...] = d_other[r]

    do_rows = do_now[...]
    do_heads = head_stack(do_rows, heads)
    prod = (do_rows.astype(F32) * mix_now[...].astype(F32)).T
    delta = jnp.concatenate(
        [
            jnp.sum(prod[h * HEAD_DIM : (h + 1) * HEAD_DIM], axis=0, keepdims=True)
            for h in range(heads)
        ],
        axis=1,
    )
    logs = jnp.concatenate([lse[h : h + 1, rows] for h in range(heads)], axis=1)

    first, last = info[2 + q_ids], info[2 + 2 * n + q_ids]
    bounds = query_bounds(code_row, q_ids, half, heads)

    def one(turn, dqs):
        new, done = list(dqs), []
        for pos, keys_ok in key_pair(first, last, turn, n, info, half, code_col, bounds):
            keys = qkv[pl.ds(pos, half), width : 2 * width]
            values = qkv[pl.ds(pos, half), 2 * width : 3 * width]
            scores = mm_nt(keys, q_heads)
            probs = jnp.where(keys_ok, jnp.exp(scores - logs), 0.0)
            d_probs = mm_nt(values, do_heads)
            d_scores = (probs * (d_probs - delta)).astype(BF16)
            done.append((pos, mm(probs.astype(BF16), do_heads), mm(d_scores, q_heads)))
            for h in range(heads):
                k_head = k_t[h * HEAD_DIM : (h + 1) * HEAD_DIM, pl.ds(pos, half)]
                new[h] += mm(k_head, d_scores[:, h * half : (h + 1) * half])
        for pos, d_values, d_keys in done:
            dv[pl.ds(pos, half), :] += d_values
            dk[pl.ds(pos, half), :] += d_keys
        return tuple(new)

    dqs = lax.fori_loop(
        0,
        (last - first + 1) // 2,
        one,
        tuple(jnp.zeros((HEAD_DIM, half), F32) for _ in range(heads)),
    )
    out[rows, 0:width] = (jnp.concatenate(dqs, axis=0) * SCALE).T.astype(BF16)

    @pl.when(step == 2 * n - 1)
    def _():
        out[:, width : 2 * width] = dk[...].astype(BF16)
        out[:, 2 * width : 3 * width] = dv[...].astype(BF16)
        for k in range(n):
            part_mine[k] = mm_nt(out[k * half : (k + 1) * half, :], w[...]).astype(BF16)
            part_other[k] = mm_nt(out[(n + k) * half : (n + k + 1) * half, :], w[...]).astype(BF16)


def attend_back(qkv, w_qkv, lse, mixes, d_mixes, d_other, ids, n):
    info, code_row = ids
    rows, width3 = qkv.shape
    width, dim = width3 // 3, w_qkv.shape[0]
    heads = width // HEAD_DIM
    half = rows // (2 * n)
    tile = (2, half, width)
    return call(
        functools.partial(attend_back_kernel, n, heads, half),
        "attend_back",
        [shape_of(rows, width3), shape_of(n, half, dim), shape_of(n, half, dim)],
        [whole_spec((rows, width3)), whole_spec((dim, width3)), whole_spec((heads, rows)), whole_spec((1, rows))]
        + [whole_spec(tile)] * (2 * n)
        + [whole_spec((n, half, width))],
        [whole_spec((rows, width3)), whole_spec((n, half, dim)), whole_spec((n, half, dim))],
        grid=(2 * n,),
        scratch=[
            pltpu.VMEM((width, rows), BF16),
            pltpu.VMEM((rows, width), F32),
            pltpu.VMEM((rows, width), F32),
            pltpu.VMEM((rows, 8), jnp.int32),
            pltpu.VMEM((half, width), BF16),
            pltpu.VMEM((half, width), BF16),
        ],
        estimate=cost(26),
    )(info, qkv, w_qkv, lse, code_row, *mixes, *d_mixes, d_other)


def normed(rows):
    inv = lax.rsqrt(jnp.mean(rows * rows, axis=-1, keepdims=True) + NORM_EPS)
    return rows * inv, inv


def back_normed(rows, d_norm):
    norm, inv = normed(rows)
    return inv * (d_norm - norm * jnp.mean(d_norm * norm, axis=-1, keepdims=True))


def head_rows(info, j, width):
    return pl.ds(pl.multiple_of((j ^ (info[0] * 2 + info[1])) * width, width), width)


def chip_rows(info, r, width):
    return pl.ds(pl.multiple_of((r ^ info[0]) * 2 * width, 2 * width), 2 * width)


def mix_kernel(n, width, info, *refs):
    parts, (others, x, w), (att, hidden, norm) = refs[:n], refs[n : n + 3], refs[n + 3 :]
    total = x[0].astype(F32)
    for r in range(n):
        mine, other = parts[r][0], others[r]
        pair = jnp.concatenate([jnp.where(info[1] == 0, mine, other), jnp.where(info[1] == 0, other, mine)], axis=1)
        att[:, 2 * r * width : 2 * (r + 1) * width] = pair
        total += mm(pair, w[chip_rows(info, r, width), :])
    hidden[...] = total
    norm[...] = normed(total)[0].astype(BF16)


def mix(info, parts, others, x, which, w_out, n):
    half, width = parts[0].shape[1:]
    dim = w_out.shape[0]
    return call(
        functools.partial(mix_kernel, n, width),
        "mix",
        [shape_of(half, dim), shape_of(half, dim, dtype=F32), shape_of(half, dim)],
        [whole_spec((2, half, width))] * n
        + [whole_spec((n, half, width)), pick_spec((half, dim), which), whole_spec((dim, dim))],
        [whole_spec((half, dim))] * 3,
        estimate=cost(5),
    )(info, *parts, others, x, w_out)


def feed_kernel(n, half, cols, which, info, *refs):
    two, cots = refs[: 2 * n], refs[2 * n : 4 * n]
    inner_out, d_gu_out, d_mine, d_other, o_mine, o_other, a_buf, c_buf, w_gu, w_dn, sems = refs[-11:]
    w_ffs = refs[4 * n : -11]
    step = pl.program_id(0)
    slot = step % 2

    def copies(r, at):
        got = []
        for dp in range(2):
            rows = pl.ds(dp * half, half)
            got.append(pltpu.make_async_copy(two[dp * n + r], a_buf.at[at, rows], sems.at[at, dp]))
            got.append(pltpu.make_async_copy(cots[dp * n + r].at[which], c_buf.at[at, rows], sems.at[at, 2 + dp]))
        return got

    @pl.when(step == 0)
    def _():
        for c in copies(0, 0):
            c.start()
        if len(w_ffs) == 1:
            n_z = w_ffs[0].shape[0]
            gu_rows, dn_rows = w_gu.shape[0] // n_z, cols // n_z
            for z in range(n_z):
                w_gu[z * gu_rows : (z + 1) * gu_rows, :] = w_ffs[0][z, :gu_rows, :]
                w_dn[z * dn_rows : (z + 1) * dn_rows, :] = w_ffs[0][z, gu_rows:, :]
        else:
            w_gu[...], w_dn[...] = w_ffs[0][...], w_ffs[1][...]

    for r in range(1, n):

        @pl.when(step + 1 == r)
        def _():
            for c in copies(r, r % 2):
                c.start()

    for c in copies(0, slot):
        c.wait()
    rows, cot = a_buf[slot], c_buf[slot]
    gu = mm(rows, w_gu[...])
    d_inner = mm_nt(cot, w_dn[...])
    gate, upper = gu[:, :cols], gu[:, cols:]
    sigma = jax.nn.sigmoid(gate)
    silu_gate = gate * sigma
    inner = (silu_gate * upper).astype(BF16)
    d_gate = (d_inner * upper * sigma * (1.0 + gate * (1.0 - sigma))).astype(BF16)
    d_upper = (d_inner * silu_gate).astype(BF16)
    inner_out[...] = inner
    d_gu_out[:, :cols] = d_gate
    d_gu_out[:, cols:] = d_upper
    d_rows = (mm_nt(d_gate, w_gu[:, :cols]) + mm_nt(d_upper, w_gu[:, cols:])).astype(BF16)
    d_mine[0] = d_rows[:half]
    d_other[0] = d_rows[half:]
    o_rows = mm(inner, w_dn[...]).astype(BF16)
    o_mine[0] = o_rows[:half]
    o_other[0] = o_rows[half:]


def feed(two, cots, which, w_ffs, cols, info, n):
    half, dim = two[0].shape
    rows = 2 * n * half
    block = pl.BlockSpec((1, half, dim), lambda i, *_: (i, 0, 0))
    return call(
        functools.partial(feed_kernel, n, half, cols, which),
        "feed",
        [shape_of(rows, cols), shape_of(rows, 2 * cols)] + [shape_of(n, half, dim)] * 4,
        [any_spec()] * (4 * n) + [whole_spec(w.shape) for w in w_ffs],
        [
            pl.BlockSpec((2 * half, cols), lambda i, *_: (i, 0)),
            pl.BlockSpec((2 * half, 2 * cols), lambda i, *_: (i, 0)),
        ]
        + [block] * 4,
        grid=(n,),
        scratch=[
            pltpu.VMEM((2, 2 * half, dim), BF16),
            pltpu.VMEM((2, 2 * half, dim), BF16),
            pltpu.VMEM((dim, 2 * cols), BF16),
            pltpu.VMEM((cols, dim), BF16),
            pltpu.SemaphoreType.DMA((2, 4)),
        ],
        estimate=cost(20),
    )(info, *two, *cots, *w_ffs)


def feed_grads_kernel(n, n_z, half, info, *refs):
    two, cots = (refs[: 2 * n], refs[2 * n : 4 * n]), refs[4 * n : 6 * n]
    inners, d_gus = refs[6 * n : 6 * n + 2], refs[6 * n + 2 : 6 * n + 4]
    a_buf, c_buf, z_buf, g_buf, acc_gu, acc_dn, sems = refs[-7:]
    outs = refs[6 * n + 4 : -7]
    step = pl.program_id(0)
    slot = step % 2
    gu_rows, dn_rows = acc_gu.shape[0] // n_z, acc_dn.shape[0] // n_z

    def copies(t, at):
        s, r = t // n, t % n
        got = []
        for dp in range(2):
            rows = pl.ds(dp * half, half)
            got.append(pltpu.make_async_copy(two[s][dp * n + r], a_buf.at[at, rows], sems.at[at, dp]))
            got.append(pltpu.make_async_copy(cots[dp * n + r].at[s], c_buf.at[at, rows], sems.at[at, 2 + dp]))
        rows = pl.ds(2 * r * half, 2 * half)
        got.append(pltpu.make_async_copy(inners[s].at[rows], z_buf.at[at], sems.at[at, 4]))
        got.append(pltpu.make_async_copy(d_gus[s].at[rows], g_buf.at[at], sems.at[at, 5]))
        return got

    @pl.when(step == 0)
    def _():
        for c in copies(0, 0):
            c.start()
        acc_gu[...] = jnp.zeros_like(acc_gu)
        acc_dn[...] = jnp.zeros_like(acc_dn)

    for t in range(1, 2 * n):

        @pl.when(step + 1 == t)
        def _():
            for c in copies(t, t % 2):
                c.start()

    for c in copies(0, slot):
        c.wait()
    acc_gu[...] += mm_tn(a_buf[slot], g_buf[slot])
    acc_dn[...] += mm_tn(z_buf[slot], c_buf[slot])

    @pl.when(step == 2 * n - 1)
    def _():
        if len(outs) == 1:
            for z in range(n_z):
                outs[0][z, :gu_rows, :] = acc_gu[z * gu_rows : (z + 1) * gu_rows, :].astype(BF16)
                outs[0][z, gu_rows:, :] = acc_dn[z * dn_rows : (z + 1) * dn_rows, :].astype(BF16)
        else:
            outs[0][...], outs[1][...] = acc_gu[...].astype(BF16), acc_dn[...].astype(BF16)


def feed_grads(two, cots, inners, d_gus, info, n, n_z):
    half, dim = two[0][0].shape
    cols = inners[0].shape[1]
    shapes = [(n_z, (dim + cols) // n_z, dim)] if 2 * cols == dim else [(dim, 2 * cols), (cols, dim)]
    return call(
        functools.partial(feed_grads_kernel, n, n_z, half),
        "feed_grads",
        [shape_of(*shape) for shape in shapes],
        [any_spec()] * (6 * n + 4),
        [whole_spec(shape) for shape in shapes],
        grid=(2 * n,),
        scratch=[
            pltpu.VMEM((2, 2 * half, dim), BF16),
            pltpu.VMEM((2, 2 * half, dim), BF16),
            pltpu.VMEM((2, 2 * half, cols), BF16),
            pltpu.VMEM((2, 2 * half, 2 * cols), BF16),
            pltpu.VMEM((dim, 2 * cols), F32),
            pltpu.VMEM((cols, dim), F32),
            pltpu.SemaphoreType.DMA((2, 6)),
        ],
        estimate=cost(20),
    )(info, *two[0], *two[1], *cots, *inners, *d_gus)


def turn_kernel(n, width, info, *refs):
    parts, (cot, hidden, w), (d_hidden, e_out), outs = (
        refs[:n],
        refs[n : n + 3],
        refs[n + 3 : n + 5],
        refs[n + 5 :],
    )
    d_norm = parts[0][...].astype(F32)
    for r in range(1, n):
        d_norm += parts[r][...].astype(F32)
    total = cot[0].astype(F32) + back_normed(hidden[...], d_norm)
    d_hidden[...] = total
    e_rows = total.astype(BF16)
    e_out[...] = e_rows
    for r in range(n):
        pair = mm_nt(e_rows, w[chip_rows(info, r, width), :]).astype(BF16)
        outs[r][info[1]] = pair[:, :width]
        outs[r][1 - info[1]] = pair[:, width:]


def turn(info, parts, cot, which, hidden, w_out, width, n):
    half, dim = hidden.shape
    return call(
        functools.partial(turn_kernel, n, width),
        "turn",
        [shape_of(half, dim, dtype=F32), shape_of(half, dim)] + [shape_of(2, half, width)] * n,
        [whole_spec((half, dim))] * n
        + [pick_spec((half, dim), which), whole_spec((half, dim)), whole_spec((dim, dim))],
        [whole_spec((half, dim))] * 2 + [whole_spec((2, half, width))] * n,
        estimate=cost(6),
    )(info, *parts, cot, hidden, w_out)


def out_grads_kernel(n, width, info, att0, att1, e0, e1, out):
    for r in range(n):
        cols = slice(2 * r * width, 2 * (r + 1) * width)
        total = mm_tn(att0[:, cols], e0[...]) + mm_tn(att1[:, cols], e1[...])
        out[chip_rows(info, r, width), :] = total.astype(BF16)


def out_grads(info, atts, es, width, n):
    half, dim = es[0].shape
    return call(
        functools.partial(out_grads_kernel, n, width),
        "out_grads",
        shape_of(dim, dim),
        [whole_spec((half, dim))] * 4,
        whole_spec((dim, dim)),
        estimate=cost(5),
    )(info, *atts, *es)


def qkv_grads_kernel(n, half, info, *refs):
    blocks, (d0, d1, out) = refs[: 2 * n], refs[2 * n :]
    total = None
    for s, d_qkv in enumerate((d0, d1)):
        for k in range(2 * n):
            part = mm_tn(d_qkv[k * half : (k + 1) * half, :], blocks[k][s])
            total = part if total is None else total + part
    out[...] = total.T.astype(BF16)


def qkv_grads(info, blocks, d_qkvs, n):
    half, dim = blocks[0].shape[1:]
    rows, width3 = d_qkvs[0].shape
    return call(
        functools.partial(qkv_grads_kernel, n, half),
        "qkv_grads",
        shape_of(dim, width3),
        [whole_spec((2, half, dim))] * (2 * n) + [whole_spec((rows, width3))] * 2,
        whole_spec((dim, width3)),
        estimate=cost(0.2),
    )(info, *blocks, *d_qkvs)


def pack_qkv_kernel(width, info, gain, wq, wk, wv, mine, theirs):
    scale = gain[...]
    mine[...] = jnp.zeros_like(mine)
    theirs[...] = jnp.zeros_like(theirs)
    for out, flip in ((mine, 0), (theirs, 1)):
        at = (info[0] * 2 + (info[1] ^ flip)) * width
        for i, w in enumerate((wq, wk, wv)):
            rows = w[:, pl.ds(pl.multiple_of(at, width), width)].astype(F32)
            out[:, i * width : (i + 1) * width] = (rows * scale).astype(BF16)


def pack_hidden_kernel(n_z, cut, down_rows, info, gain, wg, wu, mine, theirs):
    scale = gain[...]
    for out, flip in ((mine, 0), (theirs, 1)):
        for i, w in enumerate((wg, wu)):
            for z in range(n_z):
                at = (2 * z + (info[1] ^ flip)) * down_rows + info[0] * cut
                rows = w[:, pl.ds(pl.multiple_of(at, cut), cut)].astype(F32)
                to = (i * n_z + z) * cut
                out[:, to : to + cut] = (rows * scale).astype(BF16)


def pack(kernel, name, info, gain, weights, cols):
    shard = gain.shape[0]
    return call(
        kernel,
        name,
        [shape_of(shard, cols)] * 2,
        [whole_spec(a.shape) for a in (gain, *weights)],
        [whole_spec((shard, cols))] * 2,
        estimate=cost(9),
    )(info, gain, *weights)


def finish_kernel(n, shard, cut, down_rows, info, *refs):
    parts, (gain, wg, wu), (gg, gu, gd, gain_out) = refs[:n], refs[n : n + 3], refs[n + 3 :]
    chip, core = info[0], info[1]
    scale = gain[...]
    half = wg.shape[1] // (2 * n)
    total = jnp.zeros((shard, 1), F32)
    for r in range(n):
        gd[pl.ds(pl.multiple_of((chip ^ r) * cut, cut), cut), :] = parts[r][2 * shard : 2 * shard + cut, :].astype(F32)
        for q in range(2):
            rows = slice(q * shard, (q + 1) * shard)
            for z in range(half // cut):
                at = (2 * z + (core ^ q)) * down_rows + (chip ^ r) * cut
                at = pl.ds(pl.multiple_of(at, cut), cut)
                raw = parts[r][rows, z * cut : (z + 1) * cut].astype(F32)
                total += jnp.sum(raw * wg[:, at].astype(F32), axis=1, keepdims=True)
                gg[:, at] = raw * scale
                raw = parts[r][rows, half + z * cut : half + (z + 1) * cut].astype(F32)
                total += jnp.sum(raw * wu[:, at].astype(F32), axis=1, keepdims=True)
                gu[:, at] = raw * scale
    gain_out[...] = jnp.broadcast_to(total, (shard, 128)).T[0:1, :]


def finish_qkv_kernel(n, width, info, *refs):
    parts, (gain, *ws), (*grads, go, gain_out) = refs[:n], refs[n : n + 4], refs[n + 4 :]
    out = parts[0][:, 6 * width :].astype(F32)
    for r in range(1, n):
        out += parts[r][:, 6 * width :].astype(F32)
    go[...] = out
    scale = gain[...]
    total = jnp.zeros(scale.shape, F32)
    for r in range(n):
        for q in range(2):
            at = head_rows(info, r * 2 + q, width)
            for i in range(3):
                raw = parts[r][:, (3 * q + i) * width : (3 * q + i + 1) * width].astype(F32)
                total += jnp.sum(raw * ws[i][:, at].astype(F32), axis=1, keepdims=True)
                grads[i][:, at] = raw * scale
    gain_out[...] = jnp.broadcast_to(total, (scale.shape[0], 128)).T[0:1, :]


def send(value, step):
    count = lax.axis_size("ctx")
    return lax.ppermute(value, "ctx", [(i, i ^ step) for i in range(count)])


def swap(value):
    return lax.ppermute(value, "core", [(0, 1), (1, 0)])


def after(value, *others):
    return lax.optimization_barrier((value,) + others)[0]


def gather_near(own):
    n = lax.axis_size("ctx")
    return [send(own, r) for r in range(1, 3 if n == 4 else n)]


def onward_of(near):
    return jnp.where(lax.axis_index("core") == 0, near[1], near[0])


def gather_far(near):
    n = lax.axis_size("ctx")
    if n != 4:
        return near
    onward = onward_of(near)
    pairs = [(c * 2 + p, (c ^ (1 + p)) * 2 + p) for c in range(n) for p in range(2)]
    return near + [lax.ppermute(onward, ("ctx", "core"), pairs)]


def gather_cores(own, others):
    mine = [own] + others
    return mine + [swap(block) for block in mine]


def together(*values):
    return lax.optimization_barrier(values)


def plane_join(mine, other):
    return sum_cores(mine, swap(other))


def sum_cores(mine, got):
    return [(mine[r].astype(F32) + got[r].astype(F32)).astype(BF16) for r in range(mine.shape[0])]


def sum_far(joined):
    n = lax.axis_size("ctx")
    pairs = [(c * 2 + p, (c ^ (1 + p)) * 2 + p) for c in range(n) for p in range(2)]
    return lax.ppermute(joined[3], ("ctx", "core"), pairs)


def sum_onward(joined, far):
    core = lax.axis_index("core")
    by1, by2 = (
        (joined[r].astype(F32) + jnp.where(core == 2 - r, far.astype(F32), 0.0)).astype(BF16) for r in (1, 2)
    )
    return [by1, by2]


def plane_send(joined):
    return [joined[0]] + [send(joined[r], r) for r in range(1, len(joined))]


def ordered(first, second, core):
    return jnp.where(core == 0, jnp.stack([first, second]), jnp.stack([second, first]))


def send_heads(parts):
    return [parts[0]] + [send(parts[r], r) for r in range(1, len(parts))]


def other_heads(got):
    return swap(jnp.stack([g[1] for g in got]))


def mask_info(codes, half, chip, core):
    tiles = codes.reshape(-1, half)
    first, last = tiles[:, :1], tiles[:, half - 1 :]
    every = codes.reshape(1, -1)

    def count(test):
        return jnp.sum(test.astype(jnp.int32), axis=1)

    low = count(every // DOC < first // DOC) // half
    ends = jnp.minimum(count(every // DOC <= last // DOC), count(every % DOC <= last % DOC))
    high = (ends + half - 1) // half
    info = jnp.concatenate([jnp.stack([chip, core]).astype(jnp.int32), low, high])
    return info, every


def body(
    block_in, cotangent, doc_ids, block_ids, gain_attn, w_query, w_key, w_value, w_out, gain_ffn, w_gate, w_up, w_down
):
    n, n_z = lax.axis_size("ctx"), lax.axis_size("z")
    chip, core = lax.axis_index("ctx"), lax.axis_index("core")
    piece, dim = block_in.shape[1], block_in.shape[2]
    half = piece // 2
    shard = w_query.shape[0]
    width = dim // (2 * n)
    down_rows = w_down.shape[0]
    cut = down_rows // n
    me = jnp.stack([chip, core]).astype(jnp.int32)

    def own_half(rows, which):
        return lax.dynamic_slice_in_dim(rows, which * half, half, axis=0)

    def both_rows(rows):
        return ordered(own_half(rows, core), swap(own_half(rows, 1 - core)), core)

    x_rows = both_rows(block_in[0])
    n_one, inv1 = normed(x_rows.astype(F32))
    one_own = n_one.astype(BF16)
    one_near = gather_near(one_own)
    first = after(me, one_own)

    def head_cols(which):
        at = (chip * 2 + which) * width
        return jnp.concatenate(
            [lax.dynamic_slice_in_dim(w, at, width, axis=1) for w in (w_query, w_key, w_value)], axis=1
        )

    def hidden_slices(which):
        return jnp.concatenate(
            [
                lax.dynamic_slice_in_dim(w, (2 * z + which) * down_rows + chip * cut, cut, axis=1)
                for w in (w_gate, w_up)
                for z in range(n_z)
            ],
            axis=1,
        )

    def scaled(w, gain):
        return (w.astype(F32) * gain.astype(F32)[:, None]).astype(BF16)

    def core_rows(mine, theirs):
        return ordered(mine, swap(theirs), core).reshape(2 * shard, -1)

    def over_z(mine, theirs):
        return lax.all_gather(core_rows(mine, theirs), "z", axis=0, tiled=True)

    g1, g2 = gain_attn.astype(F32)[:, None], gain_ffn.astype(F32)[:, None]
    if cut % 128 == 0:
        packed = after(me, one_own)
        w_qkv = core_rows(
            *pack(functools.partial(pack_qkv_kernel, width), "pack_qkv", packed, g1, (w_query, w_key, w_value), 4 * width)
        )
        packed = after(packed, w_qkv)
        w_qkv = lax.all_gather(w_qkv, "z", axis=0, tiled=True)
        hidden_pair = pack(
            functools.partial(pack_hidden_kernel, n_z, cut, down_rows),
            "pack_hidden",
            packed,
            g2,
            (w_gate, w_up),
            2 * n_z * cut,
        )
    else:
        w_qkv = over_z(scaled(head_cols(core), gain_attn), scaled(head_cols(1 - core), gain_attn))
        hidden_pair = scaled(hidden_slices(core), gain_ffn), scaled(hidden_slices(1 - core), gain_ffn)
    w_out_full = lax.all_gather(after(w_out, w_qkv), ("z", "core"), axis=0, tiled=True)
    cols = n_z * cut
    down_cut = lax.dynamic_slice_in_dim(w_down, chip * cut, cut, axis=0)
    if 2 * cols == dim:
        gu_cut = ordered(hidden_pair[0], swap(hidden_pair[1]), core).reshape(2 * shard, dim)
        w_ff = jnp.concatenate([gu_cut, down_cut], axis=0)
        w_ffs = [lax.all_gather(w_ff, "z", axis=0)]
    else:
        w_ffs = [over_z(*hidden_pair), lax.all_gather(down_cut, "z", axis=0, tiled=True)]

    code = doc_ids[0] * DOC + block_ids[0]
    code, cot_rows = after((code, cotangent[0]), hidden_pair)
    codes = jnp.stack([code] + [send(code, r) for r in range(1, n)])
    codes = ordered(codes, swap(codes), core)
    ids = [mask_info(codes[s], half, chip, core) for s in range(2)]
    infos, code_rows = [i[0] for i in ids], [i[1] for i in ids]
    cot_rows = both_rows(cot_rows)
    one_near, infos, cot_rows = together(one_near, infos, cot_rows)
    one = gather_cores(one_own, gather_far(one_near))
    one, cot_own = together(one, cot_rows)

    def to_owner(part):
        mine = lax.dynamic_slice_in_dim(part, core * shard, shard, axis=0)
        theirs = lax.dynamic_slice_in_dim(part, (1 - core) * shard, shard, axis=0)
        return mine, swap(theirs)

    cot_near = gather_near(cot_own)
    qkv0, *mixed0, lse0 = attend(one, 0, w_qkv, (infos[0], code_rows[0]), n)
    mixed0, cot_near, go = together(mixed0, cot_near, me)
    got0 = send_heads(mixed0)
    other0 = other_heads(got0)
    att0, hidden0, norm0 = mix(go, got0, other0, x_rows, 0, w_out_full, n)
    norm0, cot_near, info1 = together(norm0, cot_near, infos[1])
    near0 = gather_near(norm0)
    cot_all = gather_far(cot_near)
    qkv1, *mixed1, lse1 = attend(one, 1, w_qkv, (info1, code_rows[1]), n)
    mixed1, near0, cot_all, go = together(mixed1, near0, cot_all, me)
    far0 = gather_far(near0)
    got1 = send_heads(mixed1)
    cots = gather_cores(cot_own, cot_all)
    other1 = other_heads(got1)
    two0 = gather_cores(norm0, far0)
    att1, hidden1, norm1 = mix(go, got1, other1, x_rows, 1, w_out_full, n)
    two0, norm1, cots, go = together(two0, norm1, cots, me)

    two_got = [send(norm1, r) for r in range(1, n)]
    inner0, d_gu0, d_mine0, d_other0, o_mine0, o_other0 = feed(two0, cots, 0, w_ffs, cols, go, n)
    two_got, d_mine0, d_other0, o_other0 = together(two_got, d_mine0, d_other0, o_other0)
    two1 = gather_cores(norm1, two_got)
    joined0 = plane_join(d_mine0, d_other0)
    o_got0 = swap(o_other0)
    joined0, two1, go = together(joined0, two1, me)
    parts0 = plane_send(joined0)
    inner1, d_gu1, d_mine1, d_other1, o_mine1, o_other1 = feed(two1, cots, 1, w_ffs, cols, go, n)
    parts0, d_mine1, d_other1, o_got0, go = together(parts0, d_mine1, d_other1, o_got0, me)
    d_got, o_got1 = swap(d_other1), swap(o_other1)
    d_hidden0, e0, *d_mix0 = turn(go, parts0, cot_rows, 0, hidden0, w_out_full, width, n)
    d_got, d_mix0, d_mine1, o_mine0, o_mine1, o_got1 = together(d_got, d_mix0, d_mine1, o_mine0, o_mine1, o_got1)
    joined1 = sum_cores(d_mine1, d_got)

    def out_sum(r, *more):
        pairs = ((o_mine0, o_got0), (o_mine1, o_got1))
        sums = [mine[r].astype(F32) + got[r].astype(F32) for mine, got in pairs]
        for far in more:
            sums = [a + b for a, b in zip(sums, far)]
        return jnp.stack([a.astype(BF16) for a in sums])

    out_far = out_sum(n - 1)
    joined1, d_mix0, out_far, go = together(joined1, d_mix0, out_far, me)
    d_got0 = send_heads(d_mix0)
    if n == 4:
        pairs = [(c * 2 + p, (c ^ (1 + p)) * 2 + p) for c in range(n) for p in range(2)]
        out_far = lax.ppermute(out_far, ("ctx", "core"), pairs)
    parts1, d_last = plane_send(joined1[: n - 1]), joined1[n - 1]
    raw_ff = feed_grads((two0, two1), cots, (inner0, inner1), (d_gu0, d_gu1), go, n, n_z)
    grads_ff = [lax.psum_scatter(g, "z", scatter_dimension=0, tiled=True) for g in raw_ff]
    parts1, d_got0, raw_ff, out_far, d_last = together(parts1, d_got0, raw_ff, out_far, d_last)
    d_other_heads0 = other_heads(d_got0)
    if n == 4:
        outs = [out_sum(0)]
        for r in range(1, 3):
            far = jnp.where(core == 2 - r, out_far.astype(F32), 0.0)
            outs.append(out_sum(r, [far[0], far[1]]))
    else:
        outs = [out_sum(r) for r in range(n - 1)] + [out_far]
    outs, d_other_heads0, info0, d_last = together(outs, d_other_heads0, infos[0], d_last)

    parts1 = parts1 + [send(d_last, n - 1)]
    out_parts = plane_send(outs)
    d_qkv0, a_mine0, a_other0 = attend_back(
        qkv0, w_qkv, lse0, mixed0, d_got0, d_other_heads0, (info0, code_rows[0]), n
    )
    out_parts, parts1, a_mine0, a_other0, go = together(out_parts, parts1, a_mine0, a_other0, me)
    a_got0 = swap(a_other0)
    d_hidden1, e1, *d_mix1 = turn(go, parts1, cot_rows, 1, hidden1, w_out_full, width, n)
    d_mix1, a_mine0, a_got0 = together(d_mix1, a_mine0, a_got0)
    d_got1 = send_heads(d_mix1)
    joined0 = sum_cores(a_mine0, a_got0)
    joined0, go = together(joined0, after(me, d_mix1))
    parts0 = plane_send(joined0)
    grads_wo = out_grads(go, (att0, att1), (e0, e1), width, n)
    grads_wo, d_got1 = together(grads_wo, d_got1)
    wo_shard = lax.psum_scatter(grads_wo, ("z", "core"), scatter_dimension=0, tiled=True)
    d_other_heads1 = other_heads(d_got1)
    info1, grads_ff, d_other_heads1 = together(infos[1], grads_ff, d_other_heads1)
    lanes = cut % 128 == 0
    if lanes:
        gu_part, dn_part = grads_ff[0][0, : 2 * shard], grads_ff[0][0, 2 * shard :]
        ff_own = jnp.concatenate([*to_owner(gu_part), dn_part], axis=0)
        ff_own, info1 = together(ff_own, info1)
        ff_packs = gather_near(ff_own)
    else:
        ff_own, ff_packs = None, []
    d_qkv1, a_mine1, a_other1 = attend_back(
        qkv1, w_qkv, lse1, mixed1, d_got1, d_other_heads1, (info1, code_rows[1]), n
    )
    raw_qkv = qkv_grads(me, one, (d_qkv0, d_qkv1), n)
    parts0, a_mine1, a_other1, ff_packs, wo_shard, _ = together(
        parts0, a_mine1, a_other1, ff_packs, wo_shard, raw_qkv
    )
    grad_qkv = lax.psum_scatter(raw_qkv, "z", scatter_dimension=0, tiled=True)
    a_got1 = swap(a_other1)
    if lanes:
        ff_packs = [ff_own] + gather_far(ff_packs)
    joined1 = sum_cores(a_mine1, a_got1)
    if lanes:
        joined1, ff_packs = together(joined1, ff_packs)
    parts1 = plane_send(joined1)
    out_rows = jnp.stack([hidden0, hidden1])
    for part in out_parts:
        out_rows = out_rows + part.astype(F32)
    out_rows = out_rows.astype(BF16)
    if lanes:
        both = jnp.concatenate([*to_owner(grad_qkv), wo_shard], axis=1)
        parts1 = after(parts1, both)
        boths = [both] + [send(both, r) for r in range(1, n)]
    in_rows = [
        d_hidden + back_normed(x_rows[s].astype(F32), sum(p.astype(F32) for p in parts))
        for s, (d_hidden, parts) in enumerate(((d_hidden0, parts0), (d_hidden1, parts1)))
    ]

    def own_rows(pair):
        mine = lax.dynamic_index_in_dim(pair, core, 0, keepdims=False)
        theirs = swap(lax.dynamic_index_in_dim(pair, 1 - core, 0, keepdims=False))
        return ordered(mine, theirs, core).reshape(1, piece, dim)

    block_out = own_rows(out_rows)
    input_grad = own_rows(jnp.stack(in_rows))

    if lanes:
        ff = w_gate.shape[1]
        raw = call(
            functools.partial(finish_kernel, n, shard, cut, down_rows),
            "finish",
            [shape_of(shard, ff, dtype=F32)] * 2
            + [shape_of(down_rows, dim, dtype=F32), shape_of(1, shard, dtype=F32)],
            [whole_spec(ff_own.shape)] * n + [whole_spec((shard, 1)), whole_spec((shard, ff)), whole_spec((shard, ff))],
            [whole_spec((shard, ff))] * 2 + [whole_spec((down_rows, dim)), whole_spec((1, shard))],
            estimate=cost(7),
        )(me, *ff_packs, g2, w_gate, w_up)
        grad_gate, grad_up, grad_down, grad_gain_ffn = raw
        raw = call(
            functools.partial(finish_qkv_kernel, n, width),
            "finish_qkv",
            [shape_of(shard, dim, dtype=F32)] * 4 + [shape_of(1, shard, dtype=F32)],
            [whole_spec(both.shape)] * n + [whole_spec((shard, 1))] + [whole_spec((shard, dim))] * 3,
            [whole_spec((shard, dim))] * 4 + [whole_spec((1, shard))],
            estimate=cost(4),
        )(after(me, grad_gain_ffn, input_grad, block_out), *boths, g1, w_query, w_key, w_value)
        grad_q, grad_k, grad_v, grad_wo, grad_gain_attn = raw
        grad_gain_attn, grad_gain_ffn = grad_gain_attn.reshape(shard), grad_gain_ffn.reshape(shard)
    else:

        def over_ctx(part):
            both = ordered(*to_owner(part), core)
            return lax.all_gather(both, "ctx", axis=0).transpose(2, 0, 1, 3)

        qkv_shard = over_ctx(grad_qkv).reshape(shard, 2 * n, 3, width).astype(F32)
        raw_q, raw_k, raw_v = (qkv_shard[:, :, i].reshape(shard, dim) for i in range(3))
        gu_part, dn_part = grads_ff
        gu_shard = over_ctx(gu_part).reshape(shard, n, 2, 2, n_z, cut).astype(F32)
        raw_g, raw_u = (
            gu_shard[:, :, :, i].transpose(0, 3, 2, 1, 4).reshape(shard, -1) for i in range(2)
        )
        grad_down = lax.all_gather(dn_part, "ctx", axis=0, tiled=True).astype(F32)
        grad_wo = lax.psum(wo_shard, "ctx").astype(F32)

        def row_sum(pairs):
            return sum(jnp.sum(w.astype(F32) * g, axis=1) for w, g in pairs)

        grad_gain_attn = row_sum([(w_query, raw_q), (w_key, raw_k), (w_value, raw_v)])
        grad_gain_ffn = row_sum([(w_gate, raw_g), (w_up, raw_u)])
        grad_q, grad_k, grad_v, grad_gate, grad_up = raw_q * g1, raw_k * g1, raw_v * g1, raw_g * g2, raw_u * g2
    return (
        block_out,
        input_grad,
        grad_gain_attn,
        grad_q,
        grad_k,
        grad_v,
        grad_wo,
        grad_gain_ffn,
        grad_gate,
        grad_up,
        grad_down,
    )


def solution(mesh):
    n_ctx, n_fsdp = mesh.devices.shape
    inner = Mesh(mesh.devices.reshape(n_ctx, n_fsdp // 2, 2), ("ctx", "z", "core"))
    fsdp = ("z", "core")
    act, ids, vec, mat = P(fsdp, "ctx", None), P(fsdp, "ctx"), P(fsdp), P(fsdp, None)
    return jax.shard_map(
        body,
        mesh=inner,
        in_specs=(act, act, ids, ids, vec, mat, mat, mat, mat, vec, mat, mat, mat),
        out_specs=(act, act, vec, mat, mat, mat, mat, vec, mat, mat, mat),
        check_vma=False,
    )
```
